32 devices in a mesh: dp: 16 (over z, y, core), node: 2 (over x).
Axes of the slice: x: 2, y: 2, z: 4, core: 2. Of those that a mesh axis runs over, the one named last changes fastest.
Arguments:
- node_feats: bfloat16 [768, 25, 128], P(('dp', 'node')), may hold values from -2 to 2
- cotangent: bfloat16 [768, 25, 128], P(('dp', 'node')), may hold values from -3 to 3
- wigner: bfloat16 [13, 25, 8192], P(None, None, ('dp', 'node')), may hold values from -1.25 to 1.25
- radial: bfloat16 [2, 8192, 128], P(None, ('dp', 'node')), may hold values from 0.29882812 to 3
- edge_src: int32 [8192], P(('dp', 'node')), may hold values from 0 to 23
- edge_dst: int32 [8192], P(('dp', 'node')), may hold values from 0 to 23
- edge_count: int32 [32], P(('dp', 'node')), may hold values from 128 to 256
- params: float32 [2, 933888], P(None, ('dp', 'node')), may hold values from -0.5 to 0.5
- moment1: float32 [2, 933888], P(None, ('dp', 'node')), may hold values from -3 to 3
- moment2: float32 [2, 933888], P(None, ('dp', 'node')), may hold values from 1 to 100
Outputs:
- new_params: float32 [2, 933888], P(None, ('dp', 'node'))
- new_moment1: float32 [2, 933888], P(None, ('dp', 'node'))
- new_moment2: float32 [2, 933888], P(None, ('dp', 'node'))
The draws below stay inside these ranges and needn't reach their ends.
Inputs may be any that keep to these rules, and one draw needn't show every extreme that they name: `edge_src`: atom numbers within the edge's own structure. `edge_dst`: atom numbers within the edge's own structure. `edge_count`: slots from this number on within a structure are padding.
All inputs are finite; a program needn't handle non-finite values.
Results may differ from the reference program's by a relative error of at most 0.017.
Values may be sent and summed in bfloat16 or wider, within the bound.
A program may use at most 64 MiB of HBM per device.

```python
import math
import jax
import jax.numpy as jnp
from jax import lax

C = 128
LMAX = 4
LAYERS = 2
NAT = 24
E_DEV = 256
COEF = 25
ROWS = 13
AVG = 10
PARAMS_LAYER = 933888
ATOMS = 768
EDGES = 8192
DEVICES = 32


def plant(result, key, low, top_value):
    longest = result.shape.index(max(result.shape))
    spots = []
    for shift in (0, 1):
        where = [jax.random.randint(jax.random.fold_in(key, axis), (), 0, length) for axis, length in enumerate(result.shape)]
        where[longest] = (where[longest] + shift) % result.shape[longest]
        spots.append(tuple(where))
    return result.at[spots[0]].set(low).at[spots[1]].set(top_value)


def block_scale(own_key, dims, shards, smallest, high):
    def one(position, blocks):
        steps = jax.random.uniform(jax.random.fold_in(jax.random.fold_in(own_key, 6), position), (blocks,), jnp.float32, smallest / len(shards), high / len(shards))
        return jnp.repeat(jnp.exp(steps), dims[position] // blocks).reshape((-1,) + (1,) * (len(dims) - position - 1))

    gain = one(*shards[0])
    for cut in shards[1:]:
        gain = gain * one(*cut)
    return gain


def scatter_about(own_key, dims, width, limit, cuts=(), kind=jnp.bfloat16):
    result = width * jax.random.normal(own_key, dims, jnp.float32)
    if cuts:
        result = result * block_scale(own_key, dims, cuts, -0.22, 0.18)
    return jnp.clip(result, -limit, limit).astype(kind)


def setup_inputs(seed: int = 0) -> dict:
    keys = jax.random.split(jax.random.key(seed), 11)
    node_feats = scatter_about(keys[0], (ATOMS, COEF, C), 0.25, 2.0, ((0, 32),))
    cotangent = scatter_about(keys[1], (ATOMS, COEF, C), 0.5, 3.0, ((0, 32),))
    wigner = scatter_about(keys[2], (ROWS, COEF, EDGES), COEF ** -0.5, 1.25, ((2, 32),))
    radial = jnp.clip(jnp.exp(math.log(3.0) - 2.306499 * jax.random.uniform(keys[3], (LAYERS, EDGES, C), jnp.float32) ** block_scale(keys[3], (LAYERS, EDGES, C), ((1, 32),), -0.2, 0.2)), 0.29882812, 3.0).astype(jnp.bfloat16)
    edge_src = plant(jax.random.randint(keys[4], (EDGES,), 0, NAT), jax.random.fold_in(keys[4], 1), 0, NAT - 1).astype(jnp.int32)
    edge_dst = plant(jax.random.randint(keys[5], (EDGES,), 0, NAT), jax.random.fold_in(keys[5], 1), 0, NAT - 1).astype(jnp.int32)
    edge_count = plant(jax.random.randint(keys[6], (DEVICES,), E_DEV // 2, E_DEV + 1), jax.random.fold_in(keys[6], 1), E_DEV // 2, E_DEV).astype(jnp.int32)
    params = scatter_about(keys[7], (LAYERS, PARAMS_LAYER), ((LMAX + 1) * C // 4) ** -0.5, 0.5, ((1, 32),), jnp.float32)
    moment1 = scatter_about(keys[8], (LAYERS, PARAMS_LAYER), 0.5, 3.0, ((1, 32),), jnp.float32)
    moment2 = jnp.clip(jnp.exp(math.log(100.0) - 4.6051702 * jax.random.uniform(keys[9], (LAYERS, PARAMS_LAYER), jnp.float32) ** block_scale(keys[9], (LAYERS, PARAMS_LAYER), ((1, 32),), -0.2, 0.2)), 1.0, 100.0)
    return dict(node_feats=node_feats, cotangent=cotangent, wigner=wigner, radial=radial, edge_src=edge_src, edge_dst=edge_dst, edge_count=edge_count, params=params, moment1=moment1, moment2=moment2)


def layer(x, flat, wig, rad, src, dst, valid):
    nat, coef, chan = x.shape
    rows = wig.shape[0]
    lone = (rows + 2) // 3
    lmore = lone - 1
    edges = src.shape[0]
    kzero = lone * chan
    kone = lmore * chan
    xs = jnp.take(x, src, axis=0)
    rot = jnp.einsum('kje,ejc->ekc', wig.astype(jnp.float32), xs.astype(jnp.float32))
    rot = (rot * rad.astype(jnp.float32)[:, None, :]).astype(jnp.bfloat16)
    azero = rot[:, :lone].reshape(edges, kzero)
    aplus = rot[:, lone:lone + lmore].reshape(edges, kone)
    aminus = rot[:, lone + lmore:].reshape(edges, kone)
    wzero = flat[:kzero * kzero].reshape(kzero, kzero)
    wreal = flat[kzero * kzero:kzero * kzero + kone * kone].reshape(kone, kone)
    wimag = flat[kzero * kzero + kone * kone:].reshape(kone, kone)
    yzero = jnp.dot(azero, wzero, preferred_element_type=jnp.float32)
    yplus = jnp.dot(aplus, wreal, preferred_element_type=jnp.float32) - jnp.dot(aminus, wimag, preferred_element_type=jnp.float32)
    yminus = jnp.dot(aplus, wimag, preferred_element_type=jnp.float32) + jnp.dot(aminus, wreal, preferred_element_type=jnp.float32)
    mixed = jnp.concatenate([yzero.reshape(edges, lone, chan), yplus.reshape(edges, lmore, chan), yminus.reshape(edges, lmore, chan)], axis=1).astype(jnp.bfloat16)
    message = jnp.einsum('kje,ekc->ejc', wig.astype(jnp.float32), mixed.astype(jnp.float32)) * valid[:, None, None]
    aggregated = jax.ops.segment_sum(message, dst, num_segments=nat) / AVG
    out = x.astype(jnp.float32) + aggregated
    scalar = out[:, 0, :]
    gated = jnp.concatenate([jax.nn.silu(scalar)[:, None, :], out[:, 1:, :] * jax.nn.sigmoid(scalar)[:, None, :]], axis=1)
    return gated.astype(jnp.bfloat16)

def reference(node_feats, cotangent, wigner, radial, edge_src, edge_dst, edge_count, params, moment1, moment2):
    weights = params.astype(jnp.bfloat16)
    feats = node_feats.reshape(DEVICES, NAT, COEF, C)
    cots = cotangent.reshape(DEVICES, NAT, COEF, C)
    wigs = jnp.moveaxis(wigner.reshape(ROWS, COEF, DEVICES, E_DEV), 2, 0)
    rads = jnp.moveaxis(radial.reshape(LAYERS, DEVICES, E_DEV, C), 1, 0)
    sources = edge_src.reshape(DEVICES, E_DEV)
    targets = edge_dst.reshape(DEVICES, E_DEV)

    def structure(carry, item):
        feat, cot, wig, rad, src, dst, count = item
        valid = (jnp.arange(E_DEV, dtype=jnp.int32) < count).astype(jnp.float32)

        def forward(wts):
            hidden = layer(feat, wts[0], wig, rad[0], src, dst, valid)
            return layer(hidden, wts[1], wig, rad[1], src, dst, valid)
        _, pull = jax.vjp(forward, weights)
        grad_dev, = pull(cot)
        return (carry + grad_dev.astype(jnp.float32), None)
    start = jnp.zeros((LAYERS, PARAMS_LAYER), jnp.float32)
    grad, _ = lax.scan(structure, start, (feats, cots, wigs, rads, sources, targets, edge_count))
    new_moment1 = 0.9 * moment1 + 0.1 * grad
    new_moment2 = 0.95 * moment2 + 0.05 * grad * grad
    m_hat = new_moment1 / (1.0 - 0.9 ** 60)
    v_hat = new_moment2 / (1.0 - 0.95 ** 60)
    new_params = params - 0.01 * (m_hat / (jnp.sqrt(v_hat) + 1e-08) + 0.1 * params)
    return (new_params, new_moment1, new_moment2)
```

```python
import functools

import jax
import jax.numpy as jnp
from jax import lax
from jax.experimental import pallas as pl
from jax.experimental.pallas import tpu as pltpu
from jax.sharding import PartitionSpec as P

AVG = 10
LANES = 128
PIECES = 3
LINK = jnp.bfloat16
WORK = 16


def split_axes(mesh):
    rest = mesh.shape["dp"] // 2
    y = 1
    while y * y * 4 <= rest and rest % (y * 2) == 0:
        y *= 2
    return rest // y, y, mesh.shape["node"]


def place(dims):
    zs, ys, xs = dims
    dp = lax.axis_index("dp")
    x = lax.axis_index("node")
    core = lax.rem(dp, 2)
    y = lax.rem(dp // 2, ys)
    z = dp // (2 * ys)
    return {"z": z, "y": y, "c": core, "x": x}


def device(dims, at):
    return {"dp": (at["z"] * dims[1] + at["y"]) * 2 + at["c"], "node": at["x"]}


def peer_of(dims, me, axis, step):
    size = {"z": dims[0], "y": dims[1], "c": 2, "x": dims[2]}[axis]
    other = dict(me)
    other[axis] = lax.rem(me[axis] + step, size)
    return other


def size_of(dims, axis):
    return {"z": dims[0], "y": dims[1], "c": 2, "x": dims[2]}[axis]


def greet(dims, me):
    barrier = pltpu.get_barrier_semaphore()
    count = 0
    for axis in "zyxc":
        for step in range(1, size_of(dims, axis)):
            pl.semaphore_signal(
                barrier,
                inc=1,
                device_id=device(dims, peer_of(dims, me, axis, step)),
                device_id_type=pl.DeviceIdType.MESH,
            )
            count += 1
    pl.semaphore_wait(barrier, count)


def gather_steps(dims, me, own_ref, out_ref, local_sem, send_sem, recv_sem):
    layers, rows = own_ref.shape[0], own_ref.shape[1]
    part = rows // PIECES
    mine = pltpu.make_async_copy(
        own_ref, out_ref.at[:, me["z"], me["y"], me["c"], me["x"]], local_sem
    )
    mine.start()
    most = max(size_of(dims, a) for a in "zyxc") - 1
    started = {}
    state = {"mine": True}

    def view(ref, layer, piece, spans, at):
        index = [layer]
        for axis in "zycx":
            index.append(slice(None) if axis in spans else at[axis])
        index.append(pl.ds(piece * part, part))
        return ref.at[tuple(index)]

    def advance(layer, phase):
        for piece in range(PIECES):
            number = layer * PIECES + piece
            order = "zyxc" if number % 2 == 0 else "zxyc"
            if phase:
                for copy in started[number, phase - 1]:
                    copy.wait_recv()
                if state["mine"]:
                    mine.wait()
                    state["mine"] = False
            if phase == 4:
                continue
            axis, spans = order[phase], order[:phase]
            copies = []
            for step in range(1, size_of(dims, axis)):
                if phase == 0:
                    src = own_ref.at[layer, pl.ds(piece * part, part)]
                else:
                    src = view(out_ref, layer, piece, spans, me)
                slot = (number * 4 + phase) * most + step - 1
                copy = pltpu.make_async_remote_copy(
                    src_ref=src,
                    dst_ref=view(out_ref, layer, piece, spans, me),
                    send_sem=send_sem.at[slot],
                    recv_sem=recv_sem.at[slot],
                    device_id=device(dims, peer_of(dims, me, axis, step)),
                    device_id_type=pl.DeviceIdType.MESH,
                )
                copy.start()
                copies.append(copy)
            started[number, phase] = copies

    def finish():
        for copies in started.values():
            for copy in copies:
                copy.wait_send()

    return advance, finish


def gather_kernel(dims, own_ref, out_ref, local_sem, send_sem, recv_sem):
    me = place(dims)
    greet(dims, me)
    advance, finish = gather_steps(dims, me, own_ref, out_ref, local_sem, send_sem, recv_sem)
    for phase in range(5):
        for layer in range(own_ref.shape[0]):
            advance(layer, phase)
    finish()


def gather_shards(dims, own, collective_id):
    layers, rows, lanes = own.shape
    zs, ys, xs = dims
    most = max(zs, ys, xs, 2) - 1
    slots = layers * PIECES * 4 * most
    return pl.pallas_call(
        functools.partial(gather_kernel, dims),
        out_shape=jax.ShapeDtypeStruct((layers, zs, ys, 2, xs, rows, lanes), own.dtype),
        in_specs=[pl.BlockSpec(memory_space=pltpu.VMEM)],
        out_specs=pl.BlockSpec(memory_space=pltpu.VMEM),
        scratch_shapes=[
            pltpu.SemaphoreType.DMA,
            pltpu.SemaphoreType.DMA((slots,)),
            pltpu.SemaphoreType.DMA((slots,)),
        ],
        compiler_params=pltpu.CompilerParams(
            collective_id=collective_id, has_side_effects=True, vmem_limit_bytes=48 << 20
        ),
        name="gather_shards",
    )(own)


def reduce_buffers(dims, pairs, part):
    zs = dims[0]
    buffers = []
    for first, second, count in pairs:
        n1, n2 = size_of(dims, first), size_of(dims, second)
        buffers += [
            pltpu.VMEM((count, zs, n2, part, LANES), jnp.float32),
            pltpu.VMEM((count, n1 - 1, zs, n2, part, LANES), LINK),
            pltpu.VMEM((count, n1 - 1, zs, n2, part, LANES), LINK),
            pltpu.VMEM((count, zs, part, LANES), jnp.float32),
            pltpu.VMEM((count, n2 - 1, zs, part, LANES), LINK),
            pltpu.VMEM((count, n2 - 1, zs, part, LANES), LINK),
            pltpu.VMEM((count, part, LANES), jnp.float32),
            pltpu.VMEM((count, zs - 1, part, LANES), LINK),
            pltpu.VMEM((count, zs - 1, part, LANES), LINK),
        ]
    return buffers


def reduce_items(layers):
    items = []
    for layer in reversed(range(layers)):
        for piece in range(PIECES):
            number = len(items)
            items.append((layer, piece, number % 2, number // 2))
    return items


def reduce_steps(dims, me, grad_ref, out_ref, pair_buf, scratch):
    zs = dims[0]
    buffers = (scratch[:9], scratch[9:18])
    send_sem, recv_sem = scratch[18:20]
    layers, rows = out_ref.shape[0], out_ref.shape[1]
    part = rows // PIECES
    items = reduce_items(layers)
    most = max(size_of(dims, a) for a in "zyxc") - 1
    pending = []

    def send(number, phase, step, axis, src, dst):
        slot = (number * 4 + phase) * most + step - 1
        copy = pltpu.make_async_remote_copy(
            src_ref=src,
            dst_ref=dst,
            send_sem=send_sem.at[slot],
            recv_sem=recv_sem.at[slot],
            device_id=device(dims, peer_of(dims, me, axis, step)),
            device_id_type=pl.DeviceIdType.MESH,
        )
        copy.start()
        pending.append(copy)
        return copy

    def f32(value):
        return value.astype(jnp.float32)

    waits = {}

    def advance(wanted, now):
        phase = now - 1
        for number, (layer, piece, kind, place_in) in enumerate(items):
            if layer != wanted:
                continue
            if now == 0:
                waits[number] = [
                    send(
                        number, 0, 1, "c",
                        grad_ref.at[layer, :, :, 1 - me["c"], :, pl.ds(piece * part, part)],
                        pair_buf.at[number],
                    )
                ]
                continue
            span = pl.ds(piece * part, part)
            acc1, send1, recv1, acc2, send2, recv2, acc3, send3, recv3 = (
                buf.at[place_in] for buf in buffers[kind]
            )
            first, second = ("x", "y") if kind == 0 else ("y", "x")
            n1, n2 = size_of(dims, first), size_of(dims, second)
            for copy in waits[number]:
                copy.wait_recv()
            copies = []
            if phase == 0:
                for step in list(range(1, n1)) + [0]:
                    k1 = lax.rem(me[first] + step, n1)

                    def one(i, carry, step=step, k1=k1):
                        z, k2 = i // n2, lax.rem(i, n2)
                        y, x = (k2, k1) if kind == 0 else (k1, k2)
                        total = f32(grad_ref[layer, z, y, me["c"], x, span]) + f32(
                            pair_buf[number, z, y, x]
                        )
                        if step:
                            send1[step - 1, z, k2] = total.astype(LINK)
                        else:
                            acc1[z, k2] = total
                        return carry

                    lax.fori_loop(0, zs * n2, one, 0)
                    if step:
                        copies.append(
                            send(number, 1, step, first, send1.at[step - 1], recv1.at[step - 1])
                        )
            elif phase == 1:
                for step in list(range(1, n2)) + [0]:
                    k2 = lax.rem(me[second] + step, n2)

                    def one(z, carry, step=step, k2=k2):
                        total = acc1[z, k2]
                        for e in range(n1 - 1):
                            total = total + f32(recv1[e, z, k2])
                        if step:
                            send2[step - 1, z] = total.astype(LINK)
                        else:
                            acc2[z] = total
                        return carry

                    lax.fori_loop(0, zs, one, 0)
                    if step:
                        copies.append(
                            send(number, 2, step, second, send2.at[step - 1], recv2.at[step - 1])
                        )
            elif phase == 2:
                for step in list(range(1, zs)) + [0]:
                    z = lax.rem(me["z"] + step, zs)
                    total = acc2[z]
                    for e in range(n2 - 1):
                        total = total + f32(recv2[e, z])
                    if step:
                        send3[step - 1] = total.astype(LINK)
                        copies.append(
                            send(number, 3, step, "z", send3.at[step - 1], recv3.at[step - 1])
                        )
                    else:
                        acc3[...] = total
            else:
                total = acc3[...]
                for e in range(zs - 1):
                    total = total + f32(recv3[e])
                out_ref[layer, span] = total
            waits[number] = copies

    def finish():
        for copy in pending:
            copy.wait_send()

    return advance, finish


def reduce_kernel(dims, grad_ref, out_ref, pair_buf, *scratch):
    me = place(dims)
    greet(dims, me)
    advance, finish = reduce_steps(dims, me, grad_ref, out_ref, pair_buf, scratch)
    for phase in range(5):
        for layer in reversed(range(out_ref.shape[0])):
            advance(layer, phase)
    finish()


def reduce_shards(dims, grad, collective_id):
    layers, _, _, _, _, rows, lanes = grad.shape
    return pl.pallas_call(
        functools.partial(reduce_kernel, dims),
        out_shape=jax.ShapeDtypeStruct((layers, rows, lanes), jnp.float32),
        in_specs=[pl.BlockSpec(memory_space=pltpu.VMEM)],
        out_specs=pl.BlockSpec(memory_space=pltpu.VMEM),
        scratch_shapes=reduce_scratch(dims, layers, rows),
        compiler_params=pltpu.CompilerParams(
            collective_id=collective_id, has_side_effects=True, vmem_limit_bytes=48 << 20
        ),
        name="reduce_shards",
    )(grad)


def dot(a, b, over=(1, 0)):
    return lax.dot_general(
        a, b, (((over[0],), (over[1],)), ((), ())), preferred_element_type=jnp.float32
    )


def compute_kernel(
    shape, count_ref, x_ref, cot_ref, wig_ref, rad_ref, src_ref, dst_ref, flat_ref, grad_ref,
    *scratch,
):
    rows_f = scratch[0]

    def unpack(layer):
        rows_f[...] = flat_ref[layer].astype(jnp.float32)

    def pack(layer):
        grad_ref[layer] = rows_f[...].astype(jnp.bfloat16)

    refs = (count_ref, x_ref, cot_ref, wig_ref, rad_ref, src_ref, dst_ref)
    compute(shape, refs, scratch, unpack, pack, lambda *step: None, lambda *step: None)


def node_rows(nat, coef):
    return -(-nat * coef // 32) * 32


def compute(shape, refs, scratch, unpack, pack, gather, reduce):
    count_ref, x_ref, cot_ref, wig_ref, rad_ref, src_ref, dst_ref = refs
    (
        rows_f, wzero, wreal, wimag, pick, put, scale, rotated, flat_a, mixed, node_t,
        outs, nodes, back, dnode, dmix,
    ) = scratch
    nat, coef, chan, rows, edges = shape
    lone = (rows + 2) // 3
    kzero, kone = lone * chan, (lone - 1) * chan
    used, tall = nat * coef, node_rows(nat, coef)
    bf16, f32 = jnp.bfloat16, jnp.float32
    eye = (
        lax.broadcasted_iota(jnp.int32, (chan, chan), 0)
        == lax.broadcasted_iota(jnp.int32, (chan, chan), 1)
    ).astype(f32).astype(bf16)

    def span(k, size):
        return slice(k * size, (k + 1) * size)

    def filled(value):
        value = value.reshape(used, chan)
        return jnp.concatenate([value, jnp.zeros((tall - used, chan), f32)], axis=0)

    def spread_wigner(hooks):
        atoms = lax.broadcasted_iota(jnp.int32, (nat, edges), 0)
        slots = lax.broadcasted_iota(jnp.int32, (nat, edges), 1)
        taken = (src_ref[...] == atoms).astype(f32)
        live = ((dst_ref[...] == atoms) & (slots < count_ref[0])).astype(f32)

        def write(first, coefs, at, size):
            values = [wig_ref[first + n].astype(f32) for n in range(coefs)]
            for k in range(rows):
                for ref, mask in ((pick, taken), (put, live)):
                    parts = [value[k : k + 1] * mask for value in values]
                    if size > coefs * nat:
                        parts.append(jnp.zeros((size - coefs * nat, edges), f32))
                    ref[pl.ds(at, size), span(k, edges)] = jnp.concatenate(
                        parts, axis=0
                    ).astype(bf16)

        pairs = coef // 2

        def one(p, carry):
            write(2 * p, 2, pl.multiple_of(p * 2 * nat, 2 * nat), 2 * nat)
            return carry

        parts = len(hooks) + 1
        for n in range(parts):
            lax.fori_loop(n * pairs // parts, (n + 1) * pairs // parts, one, 0)
            if n < len(hooks):
                hooks[n]()
        at = pairs * 2 * nat
        write(2 * pairs, coef - 2 * pairs, at, tall - at)

    def blocks():
        cut = kzero * kzero // LANES
        step = kone * kone // LANES
        return ((wzero, 0, kzero), (wreal, cut, kone), (wimag, cut + step, kone))

    def load_weights(layer):
        unpack(layer)
        for ref, start, size in blocks():
            per = size // LANES
            for c in range(per):
                ref[:, c * LANES : (c + 1) * LANES] = rows_f[
                    pl.ds(start + c, size, stride=per), :
                ].astype(bf16)

    def store_grads(layer, grads):
        for (_, start, size), grad in zip(blocks(), grads):
            per = size // LANES
            wide = 2 * LANES
            for n in range(0, size, wide):
                value = grad(n, min(n + wide, size))
                for c in range(value.shape[1] // LANES):
                    rows_f[pl.ds(start + n // LANES + c, size, stride=per), :] = value[
                        :, span(c, LANES)
                    ]
        pack(layer)

    def to_nodes(matrix, source):
        half = tall // 2
        return jnp.concatenate(
            [dot(matrix[span(n, half), :], source[...]) for n in range(2)], axis=0
        )[:used]

    def rotate(layer):
        node_t[:chan] = dot(eye, nodes[...], (1, 1)).astype(bf16)
        for k in range(rows):
            value = dot(node_t[:chan], pick[:, span(k, edges)]) * scale[layer]
            value = value.astype(bf16)
            rotated[layer, span(k, chan)] = value
            flat_a[:, span(k, chan)] = value.T

    def forward(layer, last, hooks):
        gather(layer, 4)
        load_weights(layer)
        azero = flat_a[:, :kzero]
        aplus = flat_a[:, kzero : kzero + kone]
        aminus = flat_a[:, kzero + kone :]

        def keep(first, value):
            for c in range(value.shape[1] // chan):
                mixed[span(first + c, edges)] = value[:, span(c, chan)].astype(bf16)

        wide = 2 * LANES
        for n in range(0, kzero, wide):
            keep(n // chan, dot(azero, wzero[:, n : min(n + wide, kzero)]))
        for n in range(0, kone, wide):
            real, imag = (w[:, n : min(n + wide, kone)] for w in (wreal, wimag))
            keep(lone + n // chan, dot(aplus, real) - dot(aminus, imag))
            keep(2 * lone - 1 + n // chan, dot(aplus, imag) + dot(aminus, real))
        for hook in hooks:
            hook()
        total = to_nodes(put, mixed)
        before = nodes[...].astype(f32)[:used]
        outs[layer] = before + total / AVG
        if last:
            return
        value = outs[layer].reshape(coef, nat, chan)
        gate = jax.nn.sigmoid(value[0])
        nodes[...] = filled(value * gate[None]).astype(bf16)

    def backward(layer, cot, last, hooks):
        value = outs[layer].reshape(coef, nat, chan)
        scalar = value[0]
        gate = jax.nn.sigmoid(scalar)
        slope = gate * (1.0 - gate)
        total = jnp.sum(cot[1:] * value[1:], axis=0)
        lead = cot[0] * (gate + scalar * slope) + total * slope
        dout = jnp.concatenate([lead[None], cot[1:] * gate[None]], axis=0)
        dnode[...] = dout.reshape(used, chan)
        share = filled(dout / AVG)
        high = share.astype(bf16)
        low = (share - high.astype(f32)).astype(bf16)
        node_t[:chan] = dot(eye, high, (1, 1)).astype(bf16)
        node_t[chan:] = dot(eye, low, (1, 1)).astype(bf16)
        for k in range(rows):
            both = dot(node_t[...], put[:, span(k, edges)])
            dmix[span(k, chan)] = (both[:chan] + both[chan:]).astype(bf16)
        dzero = dmix.at[:kzero]
        dplus = dmix.at[kzero : kzero + kone]
        dminus = dmix.at[kzero + kone :]
        azero = rotated[layer, :kzero]
        aplus = rotated[layer, kzero : kzero + kone]
        aminus = rotated[layer, kzero + kone :]
        for hook in hooks[:1]:
            hook()
        nt = (1, 1)
        store_grads(
            layer,
            (
                lambda a, b: dot(azero, dzero[a:b], nt),
                lambda a, b: dot(aplus, dplus[a:b], nt) + dot(aminus, dminus[a:b], nt),
                lambda a, b: dot(aplus, dminus[a:b], nt) - dot(aminus, dplus[a:b], nt),
            ),
        )
        reduce(layer, 0)
        if last:
            return

        def keep(first, value):
            for c in range(value.shape[0] // chan):
                part = value[span(c, chan)].astype(bf16).astype(f32) * scale[layer]
                mixed[span(first + c, edges)] = part.astype(bf16).T

        keep(0, dot(wzero[...], dzero[...]))
        keep(lone, dot(wreal[...], dplus[...]) + dot(wimag[...], dminus[...]))
        for hook in hooks[1:2]:
            hook()
        keep(2 * lone - 1, dot(wreal[...], dminus[...]) - dot(wimag[...], dplus[...]))
        total = to_nodes(pick, mixed)
        for hook in hooks[2:]:
            hook()
        back[...] = filled(dnode[...] + total).astype(bf16)

    def step(move, layer, phase):
        return lambda: move(layer, phase)

    def none():
        return None

    nodes[...] = filled(x_ref[...].astype(f32)).astype(bf16)
    for layer in range(rad_ref.shape[0]):
        scale[layer] = rad_ref[layer].astype(f32).T
    spread_wigner((step(gather, 0, 1),))
    rotate(0)
    gather(0, 2)
    gather(0, 3)
    forward(0, False, (step(gather, 1, 1),))
    gather(1, 2)
    rotate(1)
    gather(1, 3)
    forward(1, True, ())
    backward(1, cot_ref[...].astype(f32), False, (none, step(reduce, 1, 1), step(reduce, 1, 2)))
    reduce(1, 3)
    backward(
        0, back[...].astype(f32)[:used].reshape(coef, nat, chan), True, (step(reduce, 1, 4),)
    )


def fused_kernel(
    dims, shape, length, own_ref, count_ref, x_ref, cot_ref, wig_ref, rad_ref, src_ref, dst_ref,
    out_ref, full_ref, grad_ref, local_sem, gather_send, gather_recv, *scratch,
):
    zs, ys, xs = dims
    me = place(dims)
    greet(dims, me)
    work, rest = scratch[:WORK], scratch[WORK:]
    rows_f = work[0]
    used, rows = length // LANES, own_ref.shape[1]
    gather, gathered = gather_steps(
        dims, me, own_ref, full_ref, local_sem, gather_send, gather_recv
    )
    reduce, reduced = reduce_steps(dims, me, grad_ref, out_ref, rest[0], rest[1:])

    def shards():
        number = 0
        for z in range(zs):
            for y in range(ys):
                for c in range(2):
                    for x in range(xs):
                        yield number, (z, y, c, x)
                        number += 1

    def unpack(layer):
        for number, at in shards():
            rows_f[number * used : number * used + rows, :] = full_ref[(layer,) + at].astype(
                jnp.float32
            )

    def pack(layer):
        for number, at in shards():
            grad_ref[(layer,) + at] = rows_f[number * used : number * used + rows, :].astype(
                jnp.bfloat16
            )

    def moved(layer, phase):
        gather(layer, phase)
        if (layer, phase) == (0, 2):
            gather(1, 0)

    gather(0, 0)
    refs = (count_ref, x_ref, cot_ref, wig_ref, rad_ref, src_ref, dst_ref)
    compute(shape, refs, work, unpack, pack, moved, reduce)
    for phase in range(1, 5):
        reduce(0, phase)
    gathered()
    reduced()


def work_buffers(shape, flat_rows):
    nat, coef, chan, rows, edges = shape
    lone = (rows + 2) // 3
    kzero, kone = lone * chan, (lone - 1) * chan
    used, tall = nat * coef, node_rows(nat, coef)
    return [
        pltpu.VMEM((flat_rows, LANES), jnp.float32),
        pltpu.VMEM((kzero, kzero), jnp.bfloat16),
        pltpu.VMEM((kone, kone), jnp.bfloat16),
        pltpu.VMEM((kone, kone), jnp.bfloat16),
        pltpu.VMEM((tall, rows * edges), jnp.bfloat16),
        pltpu.VMEM((tall, rows * edges), jnp.bfloat16),
        pltpu.VMEM((2, chan, edges), jnp.float32),
        pltpu.VMEM((2, rows * chan, edges), jnp.bfloat16),
        pltpu.VMEM((edges, rows * chan), jnp.bfloat16),
        pltpu.VMEM((rows * edges, chan), jnp.bfloat16),
        pltpu.VMEM((2 * chan, tall), jnp.bfloat16),
        pltpu.VMEM((2, used, chan), jnp.float32),
        pltpu.VMEM((tall, chan), jnp.bfloat16),
        pltpu.VMEM((tall, chan), jnp.bfloat16),
        pltpu.VMEM((used, chan), jnp.float32),
        pltpu.VMEM((rows * chan, edges), jnp.bfloat16),
    ]


def reduce_scratch(dims, layers, rows):
    zs, ys, xs = dims
    part = rows // PIECES
    most = max(zs, ys, xs, 2) - 1
    count = layers * PIECES
    slots = count * 4 * most
    even, odd = (count + 1) // 2, count // 2
    return (
        [pltpu.VMEM((count, zs, ys, xs, part, LANES), jnp.bfloat16)]
        + reduce_buffers(dims, (("x", "y", even), ("y", "x", odd)), part)
        + [pltpu.SemaphoreType.DMA((slots,)), pltpu.SemaphoreType.DMA((slots,))]
    )


def owned_grads(dims, own, length, inputs, shape, collective_id):
    zs, ys, xs = dims
    layers, rows, _ = own.shape
    most = max(zs, ys, xs, 2) - 1
    slots = layers * PIECES * 4 * most
    spread = (layers, zs, ys, 2, xs, rows, LANES)
    flat_rows = zs * ys * 2 * xs * (length // LANES)
    flat_rows = -(-(flat_rows + rows) // 8) * 8
    vmem = pl.BlockSpec(memory_space=pltpu.VMEM)
    return pl.pallas_call(
        functools.partial(fused_kernel, dims, shape, length),
        out_shape=jax.ShapeDtypeStruct(own.shape, jnp.float32),
        in_specs=[vmem, pl.BlockSpec(memory_space=pltpu.SMEM)] + [vmem] * 6,
        out_specs=vmem,
        scratch_shapes=[
            pltpu.VMEM(spread, jnp.bfloat16),
            pltpu.VMEM(spread, jnp.bfloat16),
            pltpu.SemaphoreType.DMA,
            pltpu.SemaphoreType.DMA((slots,)),
            pltpu.SemaphoreType.DMA((slots,)),
        ]
        + work_buffers(shape, flat_rows)
        + reduce_scratch(dims, layers, rows),
        compiler_params=pltpu.CompilerParams(
            collective_id=collective_id, has_side_effects=True, vmem_limit_bytes=60 << 20
        ),
        name="owned_grads",
    )(own, *inputs)


def device_grads(inputs, flat, shape):
    vmem = pl.BlockSpec(memory_space=pltpu.VMEM)
    return pl.pallas_call(
        functools.partial(compute_kernel, shape),
        out_shape=jax.ShapeDtypeStruct(flat.shape, jnp.bfloat16),
        in_specs=[pl.BlockSpec(memory_space=pltpu.SMEM)] + [vmem] * 7,
        out_specs=vmem,
        scratch_shapes=work_buffers(shape, flat.shape[1]),
        compiler_params=pltpu.CompilerParams(vmem_limit_bytes=56 << 20),
        name="device_grads",
    )(*inputs, flat)


def local(
    dims, node_feats, cotangent, wigner, radial, edge_src, edge_dst, edge_count, params, moment1,
    moment2,
):
    nat, coef, chan = node_feats.shape
    layers, length = params.shape
    zs, ys, xs = dims
    shards = zs * ys * 2 * xs
    block = LANES * 16 * PIECES
    padded = -(-length // block) * block
    rows = padded // LANES
    own = jnp.pad(params.astype(jnp.bfloat16), ((0, 0), (0, padded - length)))
    own = own.reshape(layers, rows, LANES)
    edges = edge_src.shape[0]
    shape = (nat, coef, chan, wigner.shape[0], edges)

    inputs = (
        edge_count,
        jnp.transpose(node_feats, (1, 0, 2)),
        jnp.transpose(cotangent, (1, 0, 2)),
        jnp.transpose(wigner, (1, 0, 2)),
        radial,
        edge_src[None, :],
        edge_dst[None, :],
    )
    if length % LANES == 0:
        owned = owned_grads(dims, own, length, inputs, shape, 0)
    else:
        full = gather_shards(dims, own, 0).reshape(layers, shards, padded)[:, :, :length]
        full = full.reshape(layers, shards * length // LANES, LANES)
        grad = device_grads(inputs, full, shape).reshape(layers, shards, length)
        grad = jnp.pad(grad, ((0, 0), (0, 0), (0, padded - length)))
        owned = reduce_shards(dims, grad.reshape(layers, zs, ys, 2, xs, rows, LANES), 1)
    grad = owned.reshape(layers, padded)[:, :length]
    new_moment1 = 0.9 * moment1 + 0.1 * grad
    new_moment2 = 0.95 * moment2 + 0.05 * grad * grad
    m_hat = new_moment1 / (1.0 - 0.9**60)
    v_hat = new_moment2 / (1.0 - 0.95**60)
    new_params = params - 0.01 * (m_hat / (jnp.sqrt(v_hat) + 1e-08) + 0.1 * params)
    return (new_params, new_moment1, new_moment2)


def solution(mesh):
    both = ("dp", "node")
    return jax.shard_map(
        functools.partial(local, split_axes(mesh)),
        mesh=mesh,
        in_specs=(
            P(both, None, None),
            P(both, None, None),
            P(None, None, both),
            P(None, both, None),
            P(both),
            P(both),
            P(both),
            P(None, both),
            P(None, both),
            P(None, both),
        ),
        out_specs=(P(None, both), P(None, both), P(None, both)),
        check_vma=False,
    )
```

```python
import functools

import jax
import jax.numpy as jnp
from jax import lax
from jax.experimental import pallas as pl
from jax.experimental.layout import Layout, with_layout_constraint
from jax.experimental.pallas import tpu as pltpu
from jax.sharding import PartitionSpec as P

AVG = 10
LANES = 128
PIECES = 3
LINK = jnp.bfloat16
WORK = 16


def split_axes(mesh):
    rest = mesh.shape["dp"] // 2
    y = 1
    while y * y * 4 <= rest and rest % (y * 2) == 0:
        y *= 2
    return rest // y, y, mesh.shape["node"]


def place(dims):
    zs, ys, xs = dims
    dp = lax.axis_index("dp")
    x = lax.axis_index("node")
    core = lax.rem(dp, 2)
    y = lax.rem(dp // 2, ys)
    z = dp // (2 * ys)
    return {"z": z, "y": y, "c": core, "x": x}


def device(dims, at):
    return {"dp": (at["z"] * dims[1] + at["y"]) * 2 + at["c"], "node": at["x"]}


def peer_of(dims, me, axis, step):
    size = {"z": dims[0], "y": dims[1], "c": 2, "x": dims[2]}[axis]
    other = dict(me)
    other[axis] = lax.rem(me[axis] + step, size)
    return other


def size_of(dims, axis):
    return {"z": dims[0], "y": dims[1], "c": 2, "x": dims[2]}[axis]


def greet(dims, me):
    barrier = pltpu.get_barrier_semaphore()
    count = 0
    for axis in "zyxc":
        for step in range(1, size_of(dims, axis)):
            pl.semaphore_signal(
                barrier,
                inc=1,
                device_id=device(dims, peer_of(dims, me, axis, step)),
                device_id_type=pl.DeviceIdType.MESH,
            )
            count += 1
    pl.semaphore_wait(barrier, count)


def gather_steps(dims, me, own_ref, out_ref, local_sem, send_sem, recv_sem):
    layers, rows = own_ref.shape[0], own_ref.shape[1]
    part = rows // PIECES
    mine = pltpu.make_async_copy(
        own_ref, out_ref.at[:, me["z"], me["y"], me["c"], me["x"]], local_sem
    )
    mine.start()
    most = max(size_of(dims, a) for a in "zyxc") - 1
    started = {}
    state = {"mine": True}

    def view(ref, layer, piece, spans, at):
        index = [layer]
        for axis in "zycx":
            index.append(slice(None) if axis in spans else at[axis])
        index.append(pl.ds(piece * part, part))
        return ref.at[tuple(index)]

    def advance(layer, phase):
        for piece in range(PIECES):
            number = layer * PIECES + piece
            order = "zyxc" if number % 2 == 0 else "zxyc"
            if phase:
                for copy in started[number, phase - 1]:
                    copy.wait_recv()
                if state["mine"]:
                    mine.wait()
                    state["mine"] = False
            if phase == 4:
                continue
            axis, spans = order[phase], order[:phase]
            copies = []
            for step in range(1, size_of(dims, axis)):
                if phase == 0:
                    src = own_ref.at[layer, pl.ds(piece * part, part)]
                else:
                    src = view(out_ref, layer, piece, spans, me)
                slot = (number * 4 + phase) * most + step - 1
                copy = pltpu.make_async_remote_copy(
                    src_ref=src,
                    dst_ref=view(out_ref, layer, piece, spans, me),
                    send_sem=send_sem.at[slot],
                    recv_sem=recv_sem.at[slot],
                    device_id=device(dims, peer_of(dims, me, axis, step)),
                    device_id_type=pl.DeviceIdType.MESH,
                )
                copy.start()
                copies.append(copy)
            started[number, phase] = copies

    def finish():
        for copies in started.values():
            for copy in copies:
                copy.wait_send()

    return advance, finish


def gather_kernel(dims, own_ref, out_ref, local_sem, send_sem, recv_sem):
    me = place(dims)
    greet(dims, me)
    advance, finish = gather_steps(dims, me, own_ref, out_ref, local_sem, send_sem, recv_sem)
    for phase in range(5):
        for layer in range(own_ref.shape[0]):
            advance(layer, phase)
    finish()


def gather_shards(dims, own, collective_id):
    layers, rows, lanes = own.shape
    zs, ys, xs = dims
    most = max(zs, ys, xs, 2) - 1
    slots = layers * PIECES * 4 * most
    return pl.pallas_call(
        functools.partial(gather_kernel, dims),
        out_shape=jax.ShapeDtypeStruct((layers, zs, ys, 2, xs, rows, lanes), own.dtype),
        in_specs=[pl.BlockSpec(memory_space=pltpu.VMEM)],
        out_specs=pl.BlockSpec(memory_space=pltpu.VMEM),
        scratch_shapes=[
            pltpu.SemaphoreType.DMA,
            pltpu.SemaphoreType.DMA((slots,)),
            pltpu.SemaphoreType.DMA((slots,)),
        ],
        compiler_params=pltpu.CompilerParams(
            collective_id=collective_id, has_side_effects=True, vmem_limit_bytes=48 << 20
        ),
        name="gather_shards",
    )(own)


def reduce_buffers(dims, pairs, part):
    zs = dims[0]
    buffers = []
    for first, second, count in pairs:
        n1, n2 = size_of(dims, first), size_of(dims, second)
        buffers += [
            pltpu.VMEM((count, zs, n2, part, LANES), jnp.float32),
            pltpu.VMEM((count, n1 - 1, zs, n2, part, LANES), LINK),
            pltpu.VMEM((count, n1 - 1, zs, n2, part, LANES), LINK),
            pltpu.VMEM((count, zs, part, LANES), jnp.float32),
            pltpu.VMEM((count, n2 - 1, zs, part, LANES), LINK),
            pltpu.VMEM((count, n2 - 1, zs, part, LANES), LINK),
            pltpu.VMEM((count, part, LANES), jnp.float32),
            pltpu.VMEM((count, zs - 1, part, LANES), LINK),
            pltpu.VMEM((count, zs - 1, part, LANES), LINK),
        ]
    return buffers


def reduce_items(layers):
    items = []
    for layer in reversed(range(layers)):
        for piece in range(PIECES):
            number = len(items)
            items.append((layer, piece, number % 2, number // 2))
    return items


def reduce_steps(dims, me, grad_ref, out_ref, pair_buf, scratch):
    zs = dims[0]
    buffers = (scratch[:9], scratch[9:18])
    send_sem, recv_sem = scratch[18:20]
    layers, rows = out_ref.shape[0], out_ref.shape[1]
    part = rows // PIECES
    items = reduce_items(layers)
    most = max(size_of(dims, a) for a in "zyxc") - 1
    pending = []

    def send(number, phase, step, axis, src, dst):
        slot = (number * 4 + phase) * most + step - 1
        copy = pltpu.make_async_remote_copy(
            src_ref=src,
            dst_ref=dst,
            send_sem=send_sem.at[slot],
            recv_sem=recv_sem.at[slot],
            device_id=device(dims, peer_of(dims, me, axis, step)),
            device_id_type=pl.DeviceIdType.MESH,
        )
        copy.start()
        pending.append(copy)
        return copy

    def f32(value):
        return value.astype(jnp.float32)

    waits = {}

    def advance(wanted, now):
        phase = now - 1
        for number, (layer, piece, kind, place_in) in enumerate(items):
            if layer != wanted:
                continue
            if now == 0:
                waits[number] = [
                    send(
                        number, 0, 1, "c",
                        grad_ref.at[layer, :, :, 1 - me["c"], :, pl.ds(piece * part, part)],
                        pair_buf.at[number],
                    )
                ]
                continue
            span = pl.ds(piece * part, part)
            acc1, send1, recv1, acc2, send2, recv2, acc3, send3, recv3 = (
                buf.at[place_in] for buf in buffers[kind]
            )
            first, second = ("x", "y") if kind == 0 else ("y", "x")
            n1, n2 = size_of(dims, first), size_of(dims, second)
            for copy in waits[number]:
                copy.wait_recv()
            copies = []
            if phase == 0:
                for step in list(range(1, n1)) + [0]:
                    k1 = lax.rem(me[first] + step, n1)

                    def one(i, carry, step=step, k1=k1):
                        z, k2 = i // n2, lax.rem(i, n2)
                        y, x = (k2, k1) if kind == 0 else (k1, k2)
                        total = f32(grad_ref[layer, z, y, me["c"], x, span]) + f32(
                            pair_buf[number, z, y, x]
                        )
                        if step:
                            send1[step - 1, z, k2] = total.astype(LINK)
                        else:
                            acc1[z, k2] = total
                        return carry

                    lax.fori_loop(0, zs * n2, one, 0)
                    if step:
                        copies.append(
                            send(number, 1, step, first, send1.at[step - 1], recv1.at[step - 1])
                        )
            elif phase == 1:
                for step in list(range(1, n2)) + [0]:
                    k2 = lax.rem(me[second] + step, n2)

                    def one(z, carry, step=step, k2=k2):
                        total = acc1[z, k2]
                        for e in range(n1 - 1):
                            total = total + f32(recv1[e, z, k2])
                        if step:
                            send2[step - 1, z] = total.astype(LINK)
                        else:
                            acc2[z] = total
                        return carry

                    lax.fori_loop(0, zs, one, 0)
                    if step:
                        copies.append(
                            send(number, 2, step, second, send2.at[step - 1], recv2.at[step - 1])
                        )
            elif phase == 2:
                for step in list(range(1, zs)) + [0]:
                    z = lax.rem(me["z"] + step, zs)
                    total = acc2[z]
                    for e in range(n2 - 1):
                        total = total + f32(recv2[e, z])
                    if step:
                        send3[step - 1] = total.astype(LINK)
                        copies.append(
                            send(number, 3, step, "z", send3.at[step - 1], recv3.at[step - 1])
                        )
                    else:
                        acc3[...] = total
            else:
                total = acc3[...]
                for e in range(zs - 1):
                    total = total + f32(recv3[e])
                out_ref[layer, span] = total
            waits[number] = copies

    def finish():
        for copy in pending:
            copy.wait_send()

    return advance, finish


def reduce_kernel(dims, grad_ref, out_ref, pair_buf, *scratch):
    me = place(dims)
    greet(dims, me)
    advance, finish = reduce_steps(dims, me, grad_ref, out_ref, pair_buf, scratch)
    for phase in range(5):
        for layer in reversed(range(out_ref.shape[0])):
            advance(layer, phase)
    finish()


def reduce_shards(dims, grad, collective_id):
    layers, _, _, _, _, rows, lanes = grad.shape
    return pl.pallas_call(
        functools.partial(reduce_kernel, dims),
        out_shape=jax.ShapeDtypeStruct((layers, rows, lanes), jnp.float32),
        in_specs=[pl.BlockSpec(memory_space=pltpu.VMEM)],
        out_specs=pl.BlockSpec(memory_space=pltpu.VMEM),
        scratch_shapes=reduce_scratch(dims, layers, rows),
        compiler_params=pltpu.CompilerParams(
            collective_id=collective_id, has_side_effects=True, vmem_limit_bytes=48 << 20
        ),
        name="reduce_shards",
    )(grad)


def dot(a, b, over=(1, 0)):
    return lax.dot_general(
        a, b, (((over[0],), (over[1],)), ((), ())), preferred_element_type=jnp.float32
    )


def compute_kernel(
    shape, count_ref, x_ref, cot_ref, wig_ref, rad_ref, src_ref, dst_ref, flat_ref, grad_ref,
    *scratch,
):
    rows_f = scratch[0]

    def unpack(layer):
        rows_f[...] = flat_ref[layer].astype(jnp.float32)

    def packed(layer, block):
        if block == 2:
            grad_ref[layer] = rows_f[...].astype(jnp.bfloat16)

    refs = (count_ref, x_ref, cot_ref, wig_ref, rad_ref, src_ref, dst_ref)
    compute(shape, refs, scratch, unpack, packed, lambda *step: None, lambda *step: None)


def node_rows(nat, coef):
    return -(-nat * coef // 32) * 32


def compute(shape, refs, scratch, unpack, packed, gather, reduce):
    count_ref, x_ref, cot_ref, wig_ref, rad_ref, src_ref, dst_ref = refs
    (
        rows_f, wzero, wreal, wimag, pick, put, scale, rotated, flat_a, mixed, node_t,
        outs, nodes, back, dnode, dmix,
    ) = scratch
    nat, coef, chan, rows, edges = shape
    lone = (rows + 2) // 3
    kzero, kone = lone * chan, (lone - 1) * chan
    used, tall = nat * coef, node_rows(nat, coef)
    bf16, f32 = jnp.bfloat16, jnp.float32
    eye = (
        lax.broadcasted_iota(jnp.int32, (chan, chan), 0)
        == lax.broadcasted_iota(jnp.int32, (chan, chan), 1)
    ).astype(f32).astype(bf16)

    def span(k, size):
        return slice(k * size, (k + 1) * size)

    def filled(value):
        value = value.reshape(used, chan)
        return jnp.concatenate([value, jnp.zeros((tall - used, chan), f32)], axis=0)

    def spread_wigner(hooks):
        atoms = lax.broadcasted_iota(jnp.int32, (nat, edges), 0)
        slots = lax.broadcasted_iota(jnp.int32, (nat, edges), 1)
        taken = (src_ref[...] == atoms).astype(f32)
        live = ((dst_ref[...] == atoms) & (slots < count_ref[0])).astype(f32)

        def write(first, coefs, at, size):
            values = [wig_ref[first + n].astype(f32) for n in range(coefs)]
            for k in range(rows):
                for ref, mask in ((pick, taken), (put, live)):
                    parts = [value[k : k + 1] * mask for value in values]
                    if size > coefs * nat:
                        parts.append(jnp.zeros((size - coefs * nat, edges), f32))
                    ref[pl.ds(at, size), span(k, edges)] = jnp.concatenate(
                        parts, axis=0
                    ).astype(bf16)

        pairs = coef // 2

        def one(p, carry):
            write(2 * p, 2, pl.multiple_of(p * 2 * nat, 2 * nat), 2 * nat)
            return carry

        parts = len(hooks) + 1
        for n in range(parts):
            lax.fori_loop(n * pairs // parts, (n + 1) * pairs // parts, one, 0)
            if n < len(hooks):
                hooks[n]()
        at = pairs * 2 * nat
        write(2 * pairs, coef - 2 * pairs, at, tall - at)

    def blocks():
        cut = kzero * kzero // LANES
        step = kone * kone // LANES
        return ((wzero, 0, kzero), (wreal, cut, kone), (wimag, cut + step, kone))

    def load_weights(layer):
        unpack(layer)
        for ref, start, size in blocks():
            per = size // LANES
            for c in range(per):
                ref[:, c * LANES : (c + 1) * LANES] = rows_f[
                    pl.ds(start + c, size, stride=per), :
                ].astype(bf16)

    def store_grads(layer, grads):
        for block, ((_, start, size), grad) in enumerate(zip(blocks(), grads)):
            per = size // LANES
            wide = 2 * LANES
            for n in range(0, size, wide):
                value = grad(n, min(n + wide, size))
                for c in range(value.shape[1] // LANES):
                    rows_f[pl.ds(start + n // LANES + c, size, stride=per), :] = value[
                        :, span(c, LANES)
                    ]
            packed(layer, block)

    def to_nodes(matrix, source):
        half = tall // 2
        return jnp.concatenate(
            [dot(matrix[span(n, half), :], source[...]) for n in range(2)], axis=0
        )[:used]

    def rotate(layer, hooks):
        node_t[:chan] = dot(eye, nodes[...], (1, 1)).astype(bf16)
        for k in range(rows):
            for n, hook in enumerate(hooks):
                if k == (n + 1) * rows // (len(hooks) + 1):
                    hook()
            value = dot(node_t[:chan], pick[:, span(k, edges)]) * scale[layer]
            value = value.astype(bf16)
            rotated[layer, span(k, chan)] = value
            flat_a[:, span(k, chan)] = value.T

    def forward(layer, last, hooks):
        gather(layer, 5)
        load_weights(layer)
        for hook in hooks[:1]:
            hook()
        azero = flat_a[:, :kzero]
        aplus = flat_a[:, kzero : kzero + kone]
        aminus = flat_a[:, kzero + kone :]

        def keep(first, value):
            for c in range(value.shape[1] // chan):
                mixed[span(first + c, edges)] = value[:, span(c, chan)].astype(bf16)

        wide = 2 * LANES
        for n in range(0, kzero, wide):
            keep(n // chan, dot(azero, wzero[:, n : min(n + wide, kzero)]))
        for n in range(0, kone, wide):
            real, imag = (w[:, n : min(n + wide, kone)] for w in (wreal, wimag))
            keep(lone + n // chan, dot(aplus, real) - dot(aminus, imag))
            keep(2 * lone - 1 + n // chan, dot(aplus, imag) + dot(aminus, real))
        for hook in hooks[1:]:
            hook()
        total = to_nodes(put, mixed)
        before = nodes[...].astype(f32)[:used]
        outs[layer] = before + total / AVG
        if last:
            return
        value = outs[layer].reshape(coef, nat, chan)
        gate = jax.nn.sigmoid(value[0])
        nodes[...] = filled(value * gate[None]).astype(bf16)

    def backward(layer, cot, last, hooks):
        value = outs[layer].reshape(coef, nat, chan)
        scalar = value[0]
        gate = jax.nn.sigmoid(scalar)
        slope = gate * (1.0 - gate)
        total = jnp.sum(cot[1:] * value[1:], axis=0)
        lead = cot[0] * (gate + scalar * slope) + total * slope
        dout = jnp.concatenate([lead[None], cot[1:] * gate[None]], axis=0)
        dnode[...] = dout.reshape(used, chan)
        share = filled(dout / AVG)
        high = share.astype(bf16)
        low = (share - high.astype(f32)).astype(bf16)
        node_t[:chan] = dot(eye, high, (1, 1)).astype(bf16)
        node_t[chan:] = dot(eye, low, (1, 1)).astype(bf16)
        for k in range(rows):
            both = dot(node_t[...], put[:, span(k, edges)])
            dmix[span(k, chan)] = (both[:chan] + both[chan:]).astype(bf16)
        dzero = dmix.at[:kzero]
        dplus = dmix.at[kzero : kzero + kone]
        dminus = dmix.at[kzero + kone :]
        azero = rotated[layer, :kzero]
        aplus = rotated[layer, kzero : kzero + kone]
        aminus = rotated[layer, kzero + kone :]
        for hook in hooks[:1]:
            hook()
        nt = (1, 1)
        store_grads(
            layer,
            (
                lambda a, b: dot(azero, dzero[a:b], nt),
                lambda a, b: dot(aplus, dplus[a:b], nt) + dot(aminus, dminus[a:b], nt),
                lambda a, b: dot(aplus, dminus[a:b], nt) - dot(aminus, dplus[a:b], nt),
            ),
        )
        if last:
            return

        def keep(first, value):
            for c in range(value.shape[0] // chan):
                part = value[span(c, chan)].astype(bf16).astype(f32) * scale[layer]
                mixed[span(first + c, edges)] = part.astype(bf16).T

        keep(0, dot(wzero[...], dzero[...]))
        keep(lone, dot(wreal[...], dplus[...]) + dot(wimag[...], dminus[...]))
        for hook in hooks[1:2]:
            hook()
        keep(2 * lone - 1, dot(wreal[...], dminus[...]) - dot(wimag[...], dplus[...]))
        total = to_nodes(pick, mixed)
        for hook in hooks[2:]:
            hook()
        back[...] = filled(dnode[...] + total).astype(bf16)

    def step(move, layer, phase):
        return lambda: move(layer, phase)

    def none():
        return None

    def both(*moves):
        def run():
            for move in moves:
                move()

        return run

    nodes[...] = filled(x_ref[...].astype(f32)).astype(bf16)
    for layer in range(rad_ref.shape[0]):
        scale[layer] = rad_ref[layer].astype(f32).T
    gather(0, 0)
    spread_wigner((none, step(gather, 0, 1)))
    gather(0, 2)
    gather(1, 0)
    rotate(0, (step(gather, 0, 3), step(gather, 0, 4)))
    gather(1, 1)
    forward(0, False, (step(gather, 1, 2), step(gather, 1, 3)))
    rotate(1, (step(gather, 1, 4),))
    forward(1, True, ())
    backward(1, cot_ref[...].astype(f32), False, (none, step(reduce, 1, 1), step(reduce, 1, 2)))
    backward(
        0, back[...].astype(f32)[:used].reshape(coef, nat, chan), True, (step(reduce, 1, 3),)
    )
    reduce(0, 1)
    reduce(1, 4)
    for phase in range(2, 5):
        reduce(0, phase)


def side(me):
    core = me["c"]
    return me["y"] * (1 - core) + me["x"] * core, me["x"] * (1 - core) + me["y"] * core


def spot(me, z, a, b):
    core = me["c"]
    return {"z": z, "y": a * (1 - core) + b * core, "c": core, "x": b * (1 - core) + a * core}


def order_of(zs):
    return sorted(range(1, zs), key=lambda step: (min(step, zs - step), step))


def remote(src, dst, send_sem, recv_sem, target):
    return pltpu.make_async_remote_copy(
        src_ref=src,
        dst_ref=dst,
        send_sem=send_sem,
        recv_sem=recv_sem,
        device_id=target,
        device_id_type=pl.DeviceIdType.MESH,
    )


def gather_slots(dims):
    return 4 * dims[0] + 3


def stream_gather(dims, me, full_ref, send_sem, recv_sem):
    zs = dims[0]
    a, b = side(me)
    near = order_of(zs)
    copies = {}

    def send(layer, slot, at, target):
        where = full_ref.at[(layer, at["z"], at["y"], at["c"], at["x"])]
        sems = (send_sem.at[layer, slot], recv_sem.at[layer, slot])
        copies[layer, slot] = remote(where, where, *sems, device(dims, target))
        copies[layer, slot].start()

    def by_z(layer, step):
        target = dict(me, z=lax.rem(me["z"] + step, zs))
        send(layer, step - 1, me, target)

    def by_a(layer, step):
        z = lax.rem(me["z"] + zs - step, zs)
        send(layer, zs - 1 + step, spot(me, z, a, b), spot(me, me["z"], 1 - a, b))

    def by_b(layer, step, far):
        z = lax.rem(me["z"] + zs - step, zs)
        at = spot(me, z, 1 - a if far else a, b)
        send(layer, (3 if far else 2) * zs - 1 + step, at, spot(me, me["z"], a, 1 - b))

    def by_c(layer, number):
        at = spot(me, slice(None), 1 - a if number % 2 else a, 1 - b if number // 2 else b)
        send(layer, 4 * zs - 1 + number, at, dict(me, c=1 - me["c"]))

    def wait(layer, slot):
        copies[layer, slot].wait_recv()

    def advance(layer, phase):
        if phase == 0:
            for step in reversed(near):
                by_z(layer, step)
            by_a(layer, 0)
            by_b(layer, 0, False)
        elif phase == 1:
            for step in near:
                wait(layer, step - 1)
                by_a(layer, step)
                by_b(layer, step, False)
            wait(layer, zs - 1)
            by_b(layer, 0, True)
            by_c(layer, 0)
        elif phase == 2:
            for step in near:
                wait(layer, zs - 1 + step)
                by_b(layer, step, True)
            by_c(layer, 1)
        elif phase == 3:
            for step in [0] + near:
                wait(layer, 2 * zs - 1 + step)
            by_c(layer, 2)
        elif phase == 4:
            for step in [0] + near:
                wait(layer, 3 * zs - 1 + step)
            by_c(layer, 3)
        else:
            for number in range(4):
                wait(layer, 4 * zs - 1 + number)

    def finish():
        for copy in copies.values():
            copy.wait_send()

    return advance, finish


def reduce_slots(dims):
    return 5 * dims[0] - 1


def stream_reduce(dims, me, grad_ref, store, buffers, send_sem, recv_sem):
    zs = dims[0]
    a, b = side(me)
    pair, send_b, recv_b, send_a, recv_a, send_z, recv_z, total = buffers
    steps = list(reversed(order_of(zs))) + [0]
    copies = {}

    def send(key, layer, slot, src, dst, target):
        sems = (send_sem.at[layer, slot], recv_sem.at[layer, slot])
        copies[key] = remote(src, dst, *sems, device(dims, target))
        copies[key].start()

    def f32(value):
        return value.astype(jnp.float32)

    def depth(step):
        return lax.rem(me["z"] + step, zs)

    def own(layer, z, a, b):
        at = spot(me, z, a, b)
        return f32(grad_ref[layer, z, at["y"], at["c"], at["x"]]) + f32(
            pair[layer, z, at["y"], at["x"]]
        )

    def exchange(layer, z):
        send(
            ("c", layer, z), layer, z, grad_ref.at[layer, z, :, 1 - me["c"]], pair.at[layer, z],
            dict(me, c=1 - me["c"]),
        )

    def advance(layer, phase):
        if phase == 1:
            for z in range(zs):
                copies["c", layer, z].wait_recv()
            for near in range(2):
                for step in steps:
                    value = own(layer, depth(step), a if near else 1 - a, 1 - b)
                    send_b[layer, step, near] = value.astype(LINK)
                    send(
                        ("b", layer, step, near), layer, zs + 2 * step + near,
                        send_b.at[layer, step, near], recv_b.at[layer, step, near],
                        spot(me, me["z"], a, 1 - b),
                    )
        elif phase == 2:
            for step in steps:
                copies["b", layer, step, 0].wait_recv()
                value = own(layer, depth(step), 1 - a, b) + f32(recv_b[layer, step, 0])
                send_a[layer, step] = value.astype(LINK)
                send(
                    ("a", layer, step), layer, 3 * zs + step, send_a.at[layer, step],
                    recv_a.at[layer, step], spot(me, me["z"], 1 - a, b),
                )
        elif phase == 3:
            for step in steps:
                copies["b", layer, step, 1].wait_recv()
                copies["a", layer, step].wait_recv()
                value = (
                    own(layer, depth(step), a, b)
                    + f32(recv_b[layer, step, 1])
                    + f32(recv_a[layer, step])
                )
                if step == 0:
                    total[layer] = value
                    continue
                send_z[layer, step - 1] = value.astype(LINK)
                send(
                    ("z", layer, step), layer, 4 * zs + step - 1, send_z.at[layer, step - 1],
                    recv_z.at[layer, step - 1], dict(me, z=depth(step)),
                )
        else:
            value = total[layer]
            for step in order_of(zs):
                copies["z", layer, step].wait_recv()
                value = value + f32(recv_z[layer, step - 1])
            store(layer, value)

    def finish():
        for copy in copies.values():
            copy.wait_send()

    return exchange, advance, finish


def fused_kernel(
    dims, shape, length, own_ref, count_ref, x_ref, cot_ref, wig_ref, rad_ref, src_ref, dst_ref,
    out_ref, full_ref, grad_ref, gather_send, gather_recv, reduce_send, reduce_recv, *scratch,
):
    zs, ys, xs = dims
    me = place(dims)
    work, rest = scratch[:WORK], scratch[WORK:]
    rows_f = work[0]
    used, rows = length // LANES, full_ref.shape[-2]
    layers, tail = full_ref.shape[0], used % 8
    odd = me["x"] == 1
    wide = used + tail

    def store(layer, value):
        value = jnp.where(odd, value[tail:wide], value[:used])
        out_ref[pl.ds(layer, used, stride=layers), :] = value

    for layer in range(layers):
        value = own_ref[pl.ds(layer, used, stride=layers), :]
        low = jnp.zeros((tail, LANES), jnp.float32)
        high = jnp.zeros((rows - wide, LANES), jnp.float32)
        value = jnp.where(
            odd,
            jnp.concatenate([low, value, high], axis=0),
            jnp.concatenate([value, low, high], axis=0),
        )
        full_ref[layer, me["z"], me["y"], me["c"], me["x"]] = value.astype(jnp.bfloat16)
    greet(dims, me)
    gather, gathered = stream_gather(dims, me, full_ref, gather_send, gather_recv)
    exchange, reduce, reduced = stream_reduce(
        dims, me, grad_ref, store, rest, reduce_send, reduce_recv
    )

    def pairs():
        for number in range(zs * ys * 2):
            yield number, (number // (2 * ys), number // 2 % ys, number % 2)

    def unpack(layer):
        for number, at in pairs():
            even, uneven = (full_ref[(layer,) + at + (x,)].astype(jnp.float32) for x in range(2))
            first, cut = number * 2 * used, used - tail
            if tail:
                rows_f[first : first + cut, :] = even[:cut]
                rows_f[first + cut : first + cut + 8, :] = even[cut : cut + 8] + uneven[:8]
                rows_f[first + cut + 8 : first + 2 * used, :] = uneven[8:wide]
            else:
                rows_f[first : first + used, :] = even[:used]
                rows_f[first + used : first + 2 * used, :] = uneven[:used]

    ends = [0]
    for size, count in (((shape[3] + 2) // 3, 1), ((shape[3] + 2) // 3 - 1, 2)):
        for _ in range(count):
            ends.append(ends[-1] + (size * shape[2]) ** 2 // LANES)

    def packed(layer, block):
        for number, at in pairs():
            last = (number // (2 * ys) + 1) * (2 * ys) * 2 * used
            if not ends[block] < last <= ends[block + 1]:
                continue
            first = number * 2 * used
            for x, start in enumerate((first, first + used - tail)):
                grad_ref[(layer,) + at + (x,)] = rows_f[start : start + rows, :].astype(
                    jnp.bfloat16
                )
            if number % (2 * ys) == 2 * ys - 1:
                exchange(layer, at[0])

    refs = (count_ref, x_ref, cot_ref, wig_ref, rad_ref, src_ref, dst_ref)
    compute(shape, refs, work, unpack, packed, gather, reduce)
    gathered()
    reduced()


def work_buffers(shape, flat_rows):
    nat, coef, chan, rows, edges = shape
    lone = (rows + 2) // 3
    kzero, kone = lone * chan, (lone - 1) * chan
    used, tall = nat * coef, node_rows(nat, coef)
    return [
        pltpu.VMEM((flat_rows, LANES), jnp.float32),
        pltpu.VMEM((kzero, kzero), jnp.bfloat16),
        pltpu.VMEM((kone, kone), jnp.bfloat16),
        pltpu.VMEM((kone, kone), jnp.bfloat16),
        pltpu.VMEM((tall, rows * edges), jnp.bfloat16),
        pltpu.VMEM((tall, rows * edges), jnp.bfloat16),
        pltpu.VMEM((2, chan, edges), jnp.float32),
        pltpu.VMEM((2, rows * chan, edges), jnp.bfloat16),
        pltpu.VMEM((edges, rows * chan), jnp.bfloat16),
        pltpu.VMEM((rows * edges, chan), jnp.bfloat16),
        pltpu.VMEM((2 * chan, tall), jnp.bfloat16),
        pltpu.VMEM((2, used, chan), jnp.float32),
        pltpu.VMEM((tall, chan), jnp.bfloat16),
        pltpu.VMEM((tall, chan), jnp.bfloat16),
        pltpu.VMEM((used, chan), jnp.float32),
        pltpu.VMEM((rows * chan, edges), jnp.bfloat16),
    ]


def reduce_scratch(dims, layers, rows):
    zs, ys, xs = dims
    part = rows // PIECES
    most = max(zs, ys, xs, 2) - 1
    count = layers * PIECES
    slots = count * 4 * most
    even, odd = (count + 1) // 2, count // 2
    return (
        [pltpu.VMEM((count, zs, ys, xs, part, LANES), jnp.bfloat16)]
        + reduce_buffers(dims, (("x", "y", even), ("y", "x", odd)), part)
        + [pltpu.SemaphoreType.DMA((slots,)), pltpu.SemaphoreType.DMA((slots,))]
    )


def owned_grads(dims, own, length, inputs, shape, collective_id):
    zs, ys, xs = dims
    used = length // LANES
    layers = own.shape[0] // used
    rows = -(-(used + used % 8) // 16) * 16
    spread = (layers, zs, ys, 2, xs, rows, LANES)
    flat_rows = zs * ys * 2 * xs * used
    flat_rows = -(-(flat_rows + rows) // 8) * 8
    vmem = pl.BlockSpec(memory_space=pltpu.VMEM)
    item, link = (rows, LANES), jnp.bfloat16
    return pl.pallas_call(
        functools.partial(fused_kernel, dims, shape, length),
        out_shape=jax.ShapeDtypeStruct(own.shape, jnp.float32),
        in_specs=[vmem, pl.BlockSpec(memory_space=pltpu.SMEM)] + [vmem] * 6,
        out_specs=vmem,
        scratch_shapes=[
            pltpu.VMEM(spread, jnp.bfloat16),
            pltpu.VMEM(spread, jnp.bfloat16),
            pltpu.SemaphoreType.DMA((layers, gather_slots(dims))),
            pltpu.SemaphoreType.DMA((layers, gather_slots(dims))),
            pltpu.SemaphoreType.DMA((layers, reduce_slots(dims))),
            pltpu.SemaphoreType.DMA((layers, reduce_slots(dims))),
        ]
        + work_buffers(shape, flat_rows)
        + [
            pltpu.VMEM((layers, zs, ys, xs) + item, link),
            pltpu.VMEM((layers, zs, 2) + item, link),
            pltpu.VMEM((layers, zs, 2) + item, link),
            pltpu.VMEM((layers, zs) + item, link),
            pltpu.VMEM((layers, zs) + item, link),
            pltpu.VMEM((layers, zs - 1) + item, link),
            pltpu.VMEM((layers, zs - 1) + item, link),
            pltpu.VMEM((layers,) + item, jnp.float32),
        ],
        compiler_params=pltpu.CompilerParams(
            collective_id=collective_id, has_side_effects=True, vmem_limit_bytes=60 << 20
        ),
        name="owned_grads",
    )(own, *inputs)


def device_grads(inputs, flat, shape):
    vmem = pl.BlockSpec(memory_space=pltpu.VMEM)
    return pl.pallas_call(
        functools.partial(compute_kernel, shape),
        out_shape=jax.ShapeDtypeStruct(flat.shape, jnp.bfloat16),
        in_specs=[pl.BlockSpec(memory_space=pltpu.SMEM)] + [vmem] * 7,
        out_specs=vmem,
        scratch_shapes=work_buffers(shape, flat.shape[1]),
        compiler_params=pltpu.CompilerParams(vmem_limit_bytes=56 << 20),
        name="device_grads",
    )(*inputs, flat)


def woven(rows):
    return with_layout_constraint(rows, Layout(major_to_minor=(1, 0, 2)))


def local(
    dims, node_feats, cotangent, wigner, radial, edge_src, edge_dst, edge_count, params, moment1,
    moment2,
):
    nat, coef, chan = node_feats.shape
    layers, length = params.shape
    zs, ys, xs = dims
    shards = zs * ys * 2 * xs
    edges = edge_src.shape[0]
    shape = (nat, coef, chan, wigner.shape[0], edges)

    inputs = (
        edge_count,
        jnp.transpose(node_feats, (1, 0, 2)),
        jnp.transpose(cotangent, (1, 0, 2)),
        jnp.transpose(wigner, (1, 0, 2)),
        radial,
        edge_src[None, :],
        edge_dst[None, :],
    )
    if length % (4 * LANES) == 0 and ys == 2 and xs == 2 and zs > 1:
        used = length // LANES
        own = woven(params.reshape(layers, used, LANES))
        own = jnp.transpose(own, (1, 0, 2)).reshape(used * layers, LANES)
        owned = owned_grads(dims, own, length, inputs, shape, 0)
        grad = woven(jnp.transpose(owned.reshape(used, layers, LANES), (1, 0, 2)))
        grad = grad.reshape(layers, length)
    else:
        block = LANES * 16 * PIECES
        padded = -(-length // block) * block
        rows = padded // LANES
        own = jnp.pad(params.astype(jnp.bfloat16), ((0, 0), (0, padded - length)))
        full = gather_shards(dims, own.reshape(layers, rows, LANES), 0)
        full = full.reshape(layers, shards, padded)[:, :, :length]
        full = full.reshape(layers, shards * length // LANES, LANES)
        grad = device_grads(inputs, full, shape).reshape(layers, shards, length)
        grad = jnp.pad(grad, ((0, 0), (0, 0), (0, padded - length)))
        owned = reduce_shards(dims, grad.reshape(layers, zs, ys, 2, xs, rows, LANES), 1)
        grad = owned.reshape(layers, padded)[:, :length]
    new_moment1 = 0.9 * moment1 + 0.1 * grad
    new_moment2 = 0.95 * moment2 + 0.05 * grad * grad
    m_hat = new_moment1 / (1.0 - 0.9**60)
    v_hat = new_moment2 / (1.0 - 0.95**60)
    new_params = params - 0.01 * (m_hat / (jnp.sqrt(v_hat) + 1e-08) + 0.1 * params)
    return (new_params, new_moment1, new_moment2)


def solution(mesh):
    both = ("dp", "node")
    return jax.shard_map(
        functools.partial(local, split_axes(mesh)),
        mesh=mesh,
        in_specs=(
            P(both, None, None),
            P(both, None, None),
            P(None, None, both),
            P(None, both, None),
            P(both),
            P(both),
            P(both),
            P(None, both),
            P(None, both),
            P(None, both),
        ),
        out_specs=(P(None, both), P(None, both), P(None, both)),
        check_vma=False,
    )
```

```python
import functools

import jax
import jax.numpy as jnp
from jax import lax
from jax.experimental import pallas as pl
from jax.experimental.layout import Layout, with_layout_constraint
from jax.experimental.pallas import tpu as pltpu
from jax.sharding import PartitionSpec as P

AVG = 10
LANES = 128
PIECES = 3
LINK = jnp.bfloat16
WORK = 16


def split_axes(mesh):
    rest = mesh.shape["dp"] // 2
    y = 1
    while y * y * 4 <= rest and rest % (y * 2) == 0:
        y *= 2
    return rest // y, y, mesh.shape["node"]


def place(dims):
    zs, ys, xs = dims
    dp = lax.axis_index("dp")
    x = lax.axis_index("node")
    core = lax.rem(dp, 2)
    y = lax.rem(dp // 2, ys)
    z = dp // (2 * ys)
    return {"z": z, "y": y, "c": core, "x": x}


def device(dims, at):
    return {"dp": (at["z"] * dims[1] + at["y"]) * 2 + at["c"], "node": at["x"]}


def peer_of(dims, me, axis, step):
    size = {"z": dims[0], "y": dims[1], "c": 2, "x": dims[2]}[axis]
    other = dict(me)
    other[axis] = lax.rem(me[axis] + step, size)
    return other


def size_of(dims, axis):
    return {"z": dims[0], "y": dims[1], "c": 2, "x": dims[2]}[axis]


def greet(dims, me, meanwhile=lambda: None):
    barrier = pltpu.get_barrier_semaphore()
    count = 0
    for axis in "zyxc":
        for step in range(1, size_of(dims, axis)):
            pl.semaphore_signal(
                barrier,
                inc=1,
                device_id=device(dims, peer_of(dims, me, axis, step)),
                device_id_type=pl.DeviceIdType.MESH,
            )
            count += 1
    meanwhile()
    pl.semaphore_wait(barrier, count)


def gather_steps(dims, me, own_ref, out_ref, local_sem, send_sem, recv_sem):
    layers, rows = own_ref.shape[0], own_ref.shape[1]
    part = rows // PIECES
    mine = pltpu.make_async_copy(
        own_ref, out_ref.at[:, me["z"], me["y"], me["c"], me["x"]], local_sem
    )
    mine.start()
    most = max(size_of(dims, a) for a in "zyxc") - 1
    started = {}
    state = {"mine": True}

    def view(ref, layer, piece, spans, at):
        index = [layer]
        for axis in "zycx":
            index.append(slice(None) if axis in spans else at[axis])
        index.append(pl.ds(piece * part, part))
        return ref.at[tuple(index)]

    def advance(layer, phase):
        for piece in range(PIECES):
            number = layer * PIECES + piece
            order = "zyxc" if number % 2 == 0 else "zxyc"
            if phase:
                for copy in started[number, phase - 1]:
                    copy.wait_recv()
                if state["mine"]:
                    mine.wait()
                    state["mine"] = False
            if phase == 4:
                continue
            axis, spans = order[phase], order[:phase]
            copies = []
            for step in range(1, size_of(dims, axis)):
                if phase == 0:
                    src = own_ref.at[layer, pl.ds(piece * part, part)]
                else:
                    src = view(out_ref, layer, piece, spans, me)
                slot = (number * 4 + phase) * most + step - 1
                copy = pltpu.make_async_remote_copy(
                    src_ref=src,
                    dst_ref=view(out_ref, layer, piece, spans, me),
                    send_sem=send_sem.at[slot],
                    recv_sem=recv_sem.at[slot],
                    device_id=device(dims, peer_of(dims, me, axis, step)),
                    device_id_type=pl.DeviceIdType.MESH,
                )
                copy.start()
                copies.append(copy)
            started[number, phase] = copies

    def finish():
        for copies in started.values():
            for copy in copies:
                copy.wait_send()

    return advance, finish


def gather_kernel(dims, own_ref, out_ref, local_sem, send_sem, recv_sem):
    me = place(dims)
    greet(dims, me)
    advance, finish = gather_steps(dims, me, own_ref, out_ref, local_sem, send_sem, recv_sem)
    for phase in range(5):
        for layer in range(own_ref.shape[0]):
            advance(layer, phase)
    finish()


def gather_shards(dims, own, collective_id):
    layers, rows, lanes = own.shape
    zs, ys, xs = dims
    most = max(zs, ys, xs, 2) - 1
    slots = layers * PIECES * 4 * most
    return pl.pallas_call(
        functools.partial(gather_kernel, dims),
        out_shape=jax.ShapeDtypeStruct((layers, zs, ys, 2, xs, rows, lanes), own.dtype),
        in_specs=[pl.BlockSpec(memory_space=pltpu.VMEM)],
        out_specs=pl.BlockSpec(memory_space=pltpu.VMEM),
        scratch_shapes=[
            pltpu.SemaphoreType.DMA,
            pltpu.SemaphoreType.DMA((slots,)),
            pltpu.SemaphoreType.DMA((slots,)),
        ],
        compiler_params=pltpu.CompilerParams(
            collective_id=collective_id, has_side_effects=True, vmem_limit_bytes=48 << 20
        ),
        name="gather_shards",
    )(own)


def reduce_buffers(dims, pairs, part):
    zs = dims[0]
    buffers = []
    for first, second, count in pairs:
        n1, n2 = size_of(dims, first), size_of(dims, second)
        buffers += [
            pltpu.VMEM((count, zs, n2, part, LANES), jnp.float32),
            pltpu.VMEM((count, n1 - 1, zs, n2, part, LANES), LINK),
            pltpu.VMEM((count, n1 - 1, zs, n2, part, LANES), LINK),
            pltpu.VMEM((count, zs, part, LANES), jnp.float32),
            pltpu.VMEM((count, n2 - 1, zs, part, LANES), LINK),
            pltpu.VMEM((count, n2 - 1, zs, part, LANES), LINK),
            pltpu.VMEM((count, part, LANES), jnp.float32),
            pltpu.VMEM((count, zs - 1, part, LANES), LINK),
            pltpu.VMEM((count, zs - 1, part, LANES), LINK),
        ]
    return buffers


def reduce_items(layers):
    items = []
    for layer in reversed(range(layers)):
        for piece in range(PIECES):
            number = len(items)
            items.append((layer, piece, number % 2, number // 2))
    return items


def reduce_steps(dims, me, grad_ref, out_ref, pair_buf, scratch):
    zs = dims[0]
    buffers = (scratch[:9], scratch[9:18])
    send_sem, recv_sem = scratch[18:20]
    layers, rows = out_ref.shape[0], out_ref.shape[1]
    part = rows // PIECES
    items = reduce_items(layers)
    most = max(size_of(dims, a) for a in "zyxc") - 1
    pending = []

    def send(number, phase, step, axis, src, dst):
        slot = (number * 4 + phase) * most + step - 1
        copy = pltpu.make_async_remote_copy(
            src_ref=src,
            dst_ref=dst,
            send_sem=send_sem.at[slot],
            recv_sem=recv_sem.at[slot],
            device_id=device(dims, peer_of(dims, me, axis, step)),
            device_id_type=pl.DeviceIdType.MESH,
        )
        copy.start()
        pending.append(copy)
        return copy

    def f32(value):
        return value.astype(jnp.float32)

    waits = {}

    def advance(wanted, now):
        phase = now - 1
        for number, (layer, piece, kind, place_in) in enumerate(items):
            if layer != wanted:
                continue
            if now == 0:
                waits[number] = [
                    send(
                        number, 0, 1, "c",
                        grad_ref.at[layer, :, :, 1 - me["c"], :, pl.ds(piece * part, part)],
                        pair_buf.at[number],
                    )
                ]
                continue
            span = pl.ds(piece * part, part)
            acc1, send1, recv1, acc2, send2, recv2, acc3, send3, recv3 = (
                buf.at[place_in] for buf in buffers[kind]
            )
            first, second = ("x", "y") if kind == 0 else ("y", "x")
            n1, n2 = size_of(dims, first), size_of(dims, second)
            for copy in waits[number]:
                copy.wait_recv()
            copies = []
            if phase == 0:
                for step in list(range(1, n1)) + [0]:
                    k1 = lax.rem(me[first] + step, n1)

                    def one(i, carry, step=step, k1=k1):
                        z, k2 = i // n2, lax.rem(i, n2)
                        y, x = (k2, k1) if kind == 0 else (k1, k2)
                        total = f32(grad_ref[layer, z, y, me["c"], x, span]) + f32(
                            pair_buf[number, z, y, x]
                        )
                        if step:
                            send1[step - 1, z, k2] = total.astype(LINK)
                        else:
                            acc1[z, k2] = total
                        return carry

                    lax.fori_loop(0, zs * n2, one, 0)
                    if step:
                        copies.append(
                            send(number, 1, step, first, send1.at[step - 1], recv1.at[step - 1])
                        )
            elif phase == 1:
                for step in list(range(1, n2)) + [0]:
                    k2 = lax.rem(me[second] + step, n2)

                    def one(z, carry, step=step, k2=k2):
                        total = acc1[z, k2]
                        for e in range(n1 - 1):
                            total = total + f32(recv1[e, z, k2])
                        if step:
                            send2[step - 1, z] = total.astype(LINK)
                        else:
                            acc2[z] = total
                        return carry

                    lax.fori_loop(0, zs, one, 0)
                    if step:
                        copies.append(
                            send(number, 2, step, second, send2.at[step - 1], recv2.at[step - 1])
                        )
            elif phase == 2:
                for step in list(range(1, zs)) + [0]:
                    z = lax.rem(me["z"] + step, zs)
                    total = acc2[z]
                    for e in range(n2 - 1):
                        total = total + f32(recv2[e, z])
                    if step:
                        send3[step - 1] = total.astype(LINK)
                        copies.append(
                            send(number, 3, step, "z", send3.at[step - 1], recv3.at[step - 1])
                        )
                    else:
                        acc3[...] = total
            else:
                total = acc3[...]
                for e in range(zs - 1):
                    total = total + f32(recv3[e])
                out_ref[layer, span] = total
            waits[number] = copies

    def finish():
        for copy in pending:
            copy.wait_send()

    return advance, finish


def reduce_kernel(dims, grad_ref, out_ref, pair_buf, *scratch):
    me = place(dims)
    greet(dims, me)
    advance, finish = reduce_steps(dims, me, grad_ref, out_ref, pair_buf, scratch)
    for phase in range(5):
        for layer in reversed(range(out_ref.shape[0])):
            advance(layer, phase)
    finish()


def reduce_shards(dims, grad, collective_id):
    layers, _, _, _, _, rows, lanes = grad.shape
    return pl.pallas_call(
        functools.partial(reduce_kernel, dims),
        out_shape=jax.ShapeDtypeStruct((layers, rows, lanes), jnp.float32),
        in_specs=[pl.BlockSpec(memory_space=pltpu.VMEM)],
        out_specs=pl.BlockSpec(memory_space=pltpu.VMEM),
        scratch_shapes=reduce_scratch(dims, layers, rows),
        compiler_params=pltpu.CompilerParams(
            collective_id=collective_id, has_side_effects=True, vmem_limit_bytes=48 << 20
        ),
        name="reduce_shards",
    )(grad)


def dot(a, b, over=(1, 0)):
    return lax.dot_general(
        a, b, (((over[0],), (over[1],)), ((), ())), preferred_element_type=jnp.float32
    )


def compute_kernel(
    shape, count_ref, x_ref, cot_ref, wig_ref, rad_ref, src_ref, dst_ref, flat_ref, grad_ref,
    *scratch,
):
    rows_f = scratch[0]

    def unpack(layer):
        rows_f[...] = flat_ref[layer].astype(jnp.float32)

    def packed(layer, block):
        if block == 2:
            grad_ref[layer] = rows_f[...].astype(jnp.bfloat16)

    refs = (count_ref, x_ref, cot_ref, wig_ref, rad_ref, src_ref, dst_ref)
    skip = lambda *step: None
    compute(shape, refs, scratch, unpack, packed, skip, skip, skip)


def node_rows(nat, coef):
    return -(-nat * coef // 32) * 32


def compute(shape, refs, scratch, unpack, packed, gather, reduce, ready):
    count_ref, x_ref, cot_ref, wig_ref, rad_ref, src_ref, dst_ref = refs
    (
        rows_f, wzero, wreal, wimag, pick, put, scale, rotated, flat_a, mixed, node_t,
        outs, nodes, back, dnode, dmix,
    ) = scratch
    nat, coef, chan, rows, edges = shape
    lone = (rows + 2) // 3
    kzero, kone = lone * chan, (lone - 1) * chan
    used, tall = nat * coef, node_rows(nat, coef)
    bf16, f32 = jnp.bfloat16, jnp.float32
    eye = (
        lax.broadcasted_iota(jnp.int32, (chan, chan), 0)
        == lax.broadcasted_iota(jnp.int32, (chan, chan), 1)
    ).astype(f32).astype(bf16)

    def span(k, size):
        return slice(k * size, (k + 1) * size)

    def filled(value):
        value = value.reshape(used, chan)
        return jnp.concatenate([value, jnp.zeros((tall - used, chan), f32)], axis=0)

    def spread_wigner(hooks):
        atoms = lax.broadcasted_iota(jnp.int32, (nat, edges), 0)
        slots = lax.broadcasted_iota(jnp.int32, (nat, edges), 1)
        taken = (src_ref[...] == atoms).astype(f32)
        live = ((dst_ref[...] == atoms) & (slots < count_ref[0])).astype(f32)

        def write(first, coefs, at, size):
            values = [wig_ref[first + n].astype(f32) for n in range(coefs)]
            for k in range(rows):
                for ref, mask in ((pick, taken), (put, live)):
                    parts = [value[k : k + 1] * mask for value in values]
                    if size > coefs * nat:
                        parts.append(jnp.zeros((size - coefs * nat, edges), f32))
                    ref[pl.ds(at, size), span(k, edges)] = jnp.concatenate(
                        parts, axis=0
                    ).astype(bf16)

        pairs = coef // 2

        def one(p, carry):
            write(2 * p, 2, pl.multiple_of(p * 2 * nat, 2 * nat), 2 * nat)
            return carry

        parts = len(hooks) + 1
        for n in range(parts):
            lax.fori_loop(n * pairs // parts, (n + 1) * pairs // parts, one, 0)
            if n < len(hooks):
                hooks[n]()
        at = pairs * 2 * nat
        write(2 * pairs, coef - 2 * pairs, at, tall - at)

    def blocks():
        cut = kzero * kzero // LANES
        step = kone * kone // LANES
        return ((wzero, 0, kzero), (wreal, cut, kone), (wimag, cut + step, kone))

    def load_weights(layer):
        unpack(layer)
        for ref, start, size in blocks():
            per = size // LANES
            for c in range(per):
                ref[:, c * LANES : (c + 1) * LANES] = rows_f[
                    pl.ds(start + c, size, stride=per), :
                ].astype(bf16)

    def store_grads(layer, grads):
        for block, ((_, start, size), grad) in enumerate(zip(blocks(), grads)):
            per = size // LANES
            wide = 2 * LANES
            for n in range(0, size, wide):
                value = grad(n, min(n + wide, size))
                for c in range(value.shape[1] // LANES):
                    rows_f[pl.ds(start + n // LANES + c, size, stride=per), :] = value[
                        :, span(c, LANES)
                    ]
            packed(layer, block)

    def to_nodes(matrix, source):
        half = tall // 2
        return jnp.concatenate(
            [dot(matrix[span(n, half), :], source[...]) for n in range(2)], axis=0
        )[:used]

    def rotate(layer, hooks):
        node_t[:chan] = dot(eye, nodes[...], (1, 1)).astype(bf16)
        for k in range(rows):
            for n, hook in enumerate(hooks):
                if k == (n + 1) * rows // (len(hooks) + 1):
                    hook()
            value = dot(node_t[:chan], pick[:, span(k, edges)]) * scale[layer]
            value = value.astype(bf16)
            rotated[layer, span(k, chan)] = value
            flat_a[:, span(k, chan)] = value.T

    def forward(layer, last, hooks):
        gather(layer, 5)
        load_weights(layer)
        for hook in hooks[:1]:
            hook()
        azero = flat_a[:, :kzero]
        aplus = flat_a[:, kzero : kzero + kone]
        aminus = flat_a[:, kzero + kone :]

        def keep(first, value):
            for c in range(value.shape[1] // chan):
                mixed[span(first + c, edges)] = value[:, span(c, chan)].astype(bf16)

        wide = 2 * LANES
        for n in range(0, kzero, wide):
            keep(n // chan, dot(azero, wzero[:, n : min(n + wide, kzero)]))
        for n in range(0, kone, wide):
            real, imag = (w[:, n : min(n + wide, kone)] for w in (wreal, wimag))
            keep(lone + n // chan, dot(aplus, real) - dot(aminus, imag))
            keep(2 * lone - 1 + n // chan, dot(aplus, imag) + dot(aminus, real))
        for hook in hooks[1:]:
            hook()
        total = to_nodes(put, mixed)
        before = nodes[...].astype(f32)[:used]
        outs[layer] = before + total / AVG
        if last:
            return
        value = outs[layer].reshape(coef, nat, chan)
        gate = jax.nn.sigmoid(value[0])
        nodes[...] = filled(value * gate[None]).astype(bf16)

    def backward(layer, cot, last, hooks):
        value = outs[layer].reshape(coef, nat, chan)
        scalar = value[0]
        gate = jax.nn.sigmoid(scalar)
        slope = gate * (1.0 - gate)
        total = jnp.sum(cot[1:] * value[1:], axis=0)
        lead = cot[0] * (gate + scalar * slope) + total * slope
        dout = jnp.concatenate([lead[None], cot[1:] * gate[None]], axis=0)
        dnode[...] = dout.reshape(used, chan)
        share = filled(dout / AVG)
        high = share.astype(bf16)
        low = (share - high.astype(f32)).astype(bf16)
        node_t[:chan] = dot(eye, high, (1, 1)).astype(bf16)
        node_t[chan:] = dot(eye, low, (1, 1)).astype(bf16)
        for k in range(rows):
            both = dot(node_t[...], put[:, span(k, edges)])
            dmix[span(k, chan)] = (both[:chan] + both[chan:]).astype(bf16)
        dzero = dmix.at[:kzero]
        dplus = dmix.at[kzero : kzero + kone]
        dminus = dmix.at[kzero + kone :]
        azero = rotated[layer, :kzero]
        aplus = rotated[layer, kzero : kzero + kone]
        aminus = rotated[layer, kzero + kone :]
        for hook in hooks[:1]:
            hook()
        nt = (1, 1)
        store_grads(
            layer,
            (
                lambda a, b: dot(azero, dzero[a:b], nt),
                lambda a, b: dot(aplus, dplus[a:b], nt) + dot(aminus, dminus[a:b], nt),
                lambda a, b: dot(aplus, dminus[a:b], nt) - dot(aminus, dplus[a:b], nt),
            ),
        )
        if last:
            return

        def keep(first, value):
            for c in range(value.shape[0] // chan):
                part = value[span(c, chan)].astype(bf16).astype(f32) * scale[layer]
                mixed[span(first + c, edges)] = part.astype(bf16).T

        keep(0, dot(wzero[...], dzero[...]))
        keep(lone, dot(wreal[...], dplus[...]) + dot(wimag[...], dminus[...]))
        for hook in hooks[1:2]:
            hook()
        keep(2 * lone - 1, dot(wreal[...], dminus[...]) - dot(wimag[...], dplus[...]))
        total = to_nodes(pick, mixed)
        for hook in hooks[2:]:
            hook()
        back[...] = filled(dnode[...] + total).astype(bf16)

    def step(move, layer, phase):
        return lambda: move(layer, phase)

    def none():
        return None

    gather(0, 0)
    gather(0, 6)
    ready("x")
    nodes[...] = filled(x_ref[...].astype(f32)).astype(bf16)
    ready("rad")
    for layer in range(rad_ref.shape[0]):
        scale[layer] = rad_ref[layer].astype(f32).T
    ready("wig")
    spread_wigner((none, step(gather, 0, 1)))
    gather(1, 0)
    rotate(0, (step(gather, 0, 2),))
    gather(0, 3)
    gather(1, 6)
    gather(0, 4)
    gather(1, 1)
    forward(0, False, (step(gather, 1, 2),))
    rotate(1, (step(gather, 1, 3), step(gather, 1, 4)))
    forward(1, True, ())
    ready("cot")
    backward(1, cot_ref[...].astype(f32), False, (none, step(reduce, 1, 1)))
    last = back[...].astype(f32)[:used].reshape(coef, nat, chan)
    backward(0, last, True, ())
    for layer, phase in ((1, 2), (0, 1), (1, 3), (0, 2), (0, 3), (1, 4), (0, 4)):
        reduce(layer, phase)


def side(me):
    core = me["c"]
    return me["y"] * (1 - core) + me["x"] * core, me["x"] * (1 - core) + me["y"] * core


def spot(me, z, a, b):
    core = me["c"]
    return {"z": z, "y": a * (1 - core) + b * core, "c": core, "x": b * (1 - core) + a * core}


def order_of(zs):
    return sorted(range(1, zs), key=lambda step: (min(step, zs - step), step))


def remote(src, dst, send_sem, recv_sem, target):
    return pltpu.make_async_remote_copy(
        src_ref=src,
        dst_ref=dst,
        send_sem=send_sem,
        recv_sem=recv_sem,
        device_id=target,
        device_id_type=pl.DeviceIdType.MESH,
    )


def gather_slots(dims):
    return 4 * dims[0] + 3


def stream_gather(dims, me, full_ref, send_sem, recv_sem):
    zs = dims[0]
    a, b = side(me)
    near = order_of(zs)
    copies = {}

    def send(layer, slot, at, target):
        where = full_ref.at[(layer, at["z"], at["y"], at["c"], at["x"])]
        sems = (send_sem.at[layer, slot], recv_sem.at[layer, slot])
        copies[layer, slot] = remote(where, where, *sems, device(dims, target))
        copies[layer, slot].start()

    def by_z(layer, step):
        target = dict(me, z=lax.rem(me["z"] + step, zs))
        send(layer, step - 1, me, target)

    def by_a(layer, step):
        z = lax.rem(me["z"] + zs - step, zs)
        send(layer, zs - 1 + step, spot(me, z, a, b), spot(me, me["z"], 1 - a, b))

    def by_b(layer, step, far):
        z = lax.rem(me["z"] + zs - step, zs)
        at = spot(me, z, 1 - a if far else a, b)
        send(layer, (3 if far else 2) * zs - 1 + step, at, spot(me, me["z"], a, 1 - b))

    def by_c(layer, number):
        at = spot(me, slice(None), 1 - a if number % 2 else a, 1 - b if number // 2 else b)
        send(layer, 4 * zs - 1 + number, at, dict(me, c=1 - me["c"]))

    def wait(layer, slot):
        copies[layer, slot].wait_recv()

    def advance(layer, phase):
        if phase == 0:
            for step in near:
                by_z(layer, step)
        elif phase == 6:
            by_a(layer, 0)
            by_b(layer, 0, False)
        elif phase == 1:
            for step in near:
                wait(layer, step - 1)
                by_a(layer, step)
                by_b(layer, step, False)
            wait(layer, zs - 1)
            by_b(layer, 0, True)
            by_c(layer, 0)
        elif phase == 2:
            for step in near:
                wait(layer, zs - 1 + step)
                by_b(layer, step, True)
            by_c(layer, 1)
        elif phase == 3:
            for step in [0] + near:
                wait(layer, 2 * zs - 1 + step)
            by_c(layer, 2)
        elif phase == 4:
            for step in [0] + near:
                wait(layer, 3 * zs - 1 + step)
            by_c(layer, 3)
        else:
            for number in range(4):
                wait(layer, 4 * zs - 1 + number)

    def finish():
        for copy in copies.values():
            copy.wait_send()

    return advance, finish


def reduce_slots(dims):
    return 5 * dims[0] - 1


def stream_reduce(dims, me, grad_ref, store, buffers, send_sem, recv_sem):
    zs = dims[0]
    a, b = side(me)
    pair, send_b, recv_b, send_a, recv_a, send_z, recv_z, total = buffers
    steps = list(reversed(order_of(zs))) + [0]
    copies = {}

    def send(key, layer, slot, src, dst, target):
        sems = (send_sem.at[layer, slot], recv_sem.at[layer, slot])
        copies[key] = remote(src, dst, *sems, device(dims, target))
        copies[key].start()

    def f32(value):
        return value.astype(jnp.float32)

    def depth(step):
        return lax.rem(me["z"] + step, zs)

    def own(layer, z, a, b):
        at = spot(me, z, a, b)
        return f32(grad_ref[layer, z, at["y"], at["c"], at["x"]]) + f32(
            pair[layer, z, at["y"], at["x"]]
        )

    def exchange(layer, z):
        send(
            ("c", layer, z), layer, z, grad_ref.at[layer, z, :, 1 - me["c"]], pair.at[layer, z],
            dict(me, c=1 - me["c"]),
        )

    def advance(layer, phase):
        if phase == 1:
            for z in range(zs):
                copies["c", layer, z].wait_recv()
            for near in range(2):
                for step in steps:
                    value = own(layer, depth(step), a if near else 1 - a, 1 - b)
                    send_b[layer, step, near] = value.astype(LINK)
                    send(
                        ("b", layer, step, near), layer, zs + 2 * step + near,
                        send_b.at[layer, step, near], recv_b.at[layer, step, near],
                        spot(me, me["z"], a, 1 - b),
                    )
        elif phase == 2:
            for step in steps:
                copies["b", layer, step, 0].wait_recv()
                value = own(layer, depth(step), 1 - a, b) + f32(recv_b[layer, step, 0])
                send_a[layer, step] = value.astype(LINK)
                send(
                    ("a", layer, step), layer, 3 * zs + step, send_a.at[layer, step],
                    recv_a.at[layer, step], spot(me, me["z"], 1 - a, b),
                )
        elif phase == 3:
            for step in steps:
                copies["b", layer, step, 1].wait_recv()
                copies["a", layer, step].wait_recv()
                value = (
                    own(layer, depth(step), a, b)
                    + f32(recv_b[layer, step, 1])
                    + f32(recv_a[layer, step])
                )
                if step == 0:
                    total[layer] = value
                    continue
                send_z[layer, step - 1] = value.astype(LINK)
                send(
                    ("z", layer, step), layer, 4 * zs + step - 1, send_z.at[layer, step - 1],
                    recv_z.at[layer, step - 1], dict(me, z=depth(step)),
                )
        else:
            value = total[layer]
            for step in order_of(zs):
                copies["z", layer, step].wait_recv()
                value = value + f32(recv_z[layer, step - 1])
            store(layer, value)

    def finish():
        for copy in copies.values():
            copy.wait_send()

    return exchange, advance, finish


def fused_kernel(
    dims, shape, length, own_ref, count_ref, x_ref, cot_ref, wig_ref, rad_ref, src_ref, dst_ref,
    out_ref, par, x, cot, wig, rad, load_sem, full_ref, grad_ref, gather_send, gather_recv,
    reduce_send, reduce_recv, *scratch,
):
    zs, ys, xs = dims
    me = place(dims)
    loads = {}
    for number, (name, source, ref) in enumerate(
        (
            ("own", own_ref, par), ("x", x_ref, x), ("rad", rad_ref, rad), ("wig", wig_ref, wig),
            ("cot", cot_ref, cot),
        )
    ):
        loads[name] = pltpu.make_async_copy(source, ref, load_sem.at[number])

    def ready(name):
        loads[name].wait()

    work, rest = scratch[:WORK], scratch[WORK:]
    rows_f = work[0]
    used, rows = length // LANES, full_ref.shape[-2]
    layers, tail = full_ref.shape[0], used % 8
    odd = me["x"] == 1
    wide = used + tail

    def store(layer, value):
        value = jnp.where(odd, value[tail:wide], value[:used])
        out_ref[pl.ds(layer, used, stride=layers), :] = value

    def meanwhile():
        for load in loads.values():
            load.start()
        ready("own")
        for layer in range(layers):
            value = par[pl.ds(layer, used, stride=layers), :]
            low = jnp.zeros((tail, LANES), jnp.float32)
            high = jnp.zeros((rows - wide, LANES), jnp.float32)
            value = jnp.where(
                odd,
                jnp.concatenate([low, value, high], axis=0),
                jnp.concatenate([value, low, high], axis=0),
            )
            full_ref[layer, me["z"], me["y"], me["c"], me["x"]] = value.astype(jnp.bfloat16)

    greet(dims, me, meanwhile)
    gather, gathered = stream_gather(dims, me, full_ref, gather_send, gather_recv)
    exchange, reduce, reduced = stream_reduce(
        dims, me, grad_ref, store, rest, reduce_send, reduce_recv
    )

    def pairs():
        for number in range(zs * ys * 2):
            yield number, (number // (2 * ys), number // 2 % ys, number % 2)

    def unpack(layer):
        for number, at in pairs():
            even, uneven = (full_ref[(layer,) + at + (x,)].astype(jnp.float32) for x in range(2))
            first, cut = number * 2 * used, used - tail
            if tail:
                rows_f[first : first + cut, :] = even[:cut]
                rows_f[first + cut : first + cut + 8, :] = even[cut : cut + 8] + uneven[:8]
                rows_f[first + cut + 8 : first + 2 * used, :] = uneven[8:wide]
            else:
                rows_f[first : first + used, :] = even[:used]
                rows_f[first + used : first + 2 * used, :] = uneven[:used]

    ends = [0]
    for size, count in (((shape[3] + 2) // 3, 1), ((shape[3] + 2) // 3 - 1, 2)):
        for _ in range(count):
            ends.append(ends[-1] + (size * shape[2]) ** 2 // LANES)

    def packed(layer, block):
        for number, at in pairs():
            last = (number // (2 * ys) + 1) * (2 * ys) * 2 * used
            if not ends[block] < last <= ends[block + 1]:
                continue
            first = number * 2 * used
            for x, start in enumerate((first, first + used - tail)):
                grad_ref[(layer,) + at + (x,)] = rows_f[start : start + rows, :].astype(
                    jnp.bfloat16
                )
            if number % (2 * ys) == 2 * ys - 1:
                exchange(layer, at[0])

    refs = (count_ref, x, cot, wig, rad, src_ref, dst_ref)
    compute(shape, refs, work, unpack, packed, gather, reduce, ready)
    gathered()
    reduced()


def work_buffers(shape, flat_rows):
    nat, coef, chan, rows, edges = shape
    lone = (rows + 2) // 3
    kzero, kone = lone * chan, (lone - 1) * chan
    used, tall = nat * coef, node_rows(nat, coef)
    return [
        pltpu.VMEM((flat_rows, LANES), jnp.float32),
        pltpu.VMEM((kzero, kzero), jnp.bfloat16),
        pltpu.VMEM((kone, kone), jnp.bfloat16),
        pltpu.VMEM((kone, kone), jnp.bfloat16),
        pltpu.VMEM((tall, rows * edges), jnp.bfloat16),
        pltpu.VMEM((tall, rows * edges), jnp.bfloat16),
        pltpu.VMEM((2, chan, edges), jnp.float32),
        pltpu.VMEM((2, rows * chan, edges), jnp.bfloat16),
        pltpu.VMEM((edges, rows * chan), jnp.bfloat16),
        pltpu.VMEM((rows * edges, chan), jnp.bfloat16),
        pltpu.VMEM((2 * chan, tall), jnp.bfloat16),
        pltpu.VMEM((2, used, chan), jnp.float32),
        pltpu.VMEM((tall, chan), jnp.bfloat16),
        pltpu.VMEM((tall, chan), jnp.bfloat16),
        pltpu.VMEM((used, chan), jnp.float32),
        pltpu.VMEM((rows * chan, edges), jnp.bfloat16),
    ]


def reduce_scratch(dims, layers, rows):
    zs, ys, xs = dims
    part = rows // PIECES
    most = max(zs, ys, xs, 2) - 1
    count = layers * PIECES
    slots = count * 4 * most
    even, odd = (count + 1) // 2, count // 2
    return (
        [pltpu.VMEM((count, zs, ys, xs, part, LANES), jnp.bfloat16)]
        + reduce_buffers(dims, (("x", "y", even), ("y", "x", odd)), part)
        + [pltpu.SemaphoreType.DMA((slots,)), pltpu.SemaphoreType.DMA((slots,))]
    )


def owned_grads(dims, own, length, inputs, shape, collective_id):
    zs, ys, xs = dims
    used = length // LANES
    layers = own.shape[0] // used
    rows = -(-(used + used % 8) // 16) * 16
    spread = (layers, zs, ys, 2, xs, rows, LANES)
    flat_rows = zs * ys * 2 * xs * used
    flat_rows = -(-(flat_rows + rows) // 8) * 8
    vmem = pl.BlockSpec(memory_space=pltpu.VMEM)
    hbm = pl.BlockSpec(memory_space=pl.ANY)
    item, link = (rows, LANES), jnp.bfloat16
    return pl.pallas_call(
        functools.partial(fused_kernel, dims, shape, length),
        out_shape=jax.ShapeDtypeStruct(own.shape, jnp.float32),
        in_specs=[hbm, pl.BlockSpec(memory_space=pltpu.SMEM)] + [hbm] * 4 + [vmem] * 2,
        out_specs=vmem,
        scratch_shapes=[
            pltpu.VMEM(own.shape, own.dtype),
            pltpu.VMEM(inputs[1].shape, inputs[1].dtype),
            pltpu.VMEM(inputs[2].shape, inputs[2].dtype),
            pltpu.VMEM(inputs[3].shape, inputs[3].dtype),
            pltpu.VMEM(inputs[4].shape, inputs[4].dtype),
            pltpu.SemaphoreType.DMA((5,)),
            pltpu.VMEM(spread, jnp.bfloat16),
            pltpu.VMEM(spread, jnp.bfloat16),
            pltpu.SemaphoreType.DMA((layers, gather_slots(dims))),
            pltpu.SemaphoreType.DMA((layers, gather_slots(dims))),
            pltpu.SemaphoreType.DMA((layers, reduce_slots(dims))),
            pltpu.SemaphoreType.DMA((layers, reduce_slots(dims))),
        ]
        + work_buffers(shape, flat_rows)
        + [
            pltpu.VMEM((layers, zs, ys, xs) + item, link),
            pltpu.VMEM((layers, zs, 2) + item, link),
            pltpu.VMEM((layers, zs, 2) + item, link),
            pltpu.VMEM((layers, zs) + item, link),
            pltpu.VMEM((layers, zs) + item, link),
            pltpu.VMEM((layers, zs - 1) + item, link),
            pltpu.VMEM((layers, zs - 1) + item, link),
            pltpu.VMEM((layers,) + item, jnp.float32),
        ],
        compiler_params=pltpu.CompilerParams(
            collective_id=collective_id, has_side_effects=True, vmem_limit_bytes=60 << 20
        ),
        name="owned_grads",
    )(own, *inputs)


def device_grads(inputs, flat, shape):
    vmem = pl.BlockSpec(memory_space=pltpu.VMEM)
    return pl.pallas_call(
        functools.partial(compute_kernel, shape),
        out_shape=jax.ShapeDtypeStruct(flat.shape, jnp.bfloat16),
        in_specs=[pl.BlockSpec(memory_space=pltpu.SMEM)] + [vmem] * 7,
        out_specs=vmem,
        scratch_shapes=work_buffers(shape, flat.shape[1]),
        compiler_params=pltpu.CompilerParams(vmem_limit_bytes=56 << 20),
        name="device_grads",
    )(*inputs, flat)


def woven(rows):
    return with_layout_constraint(rows, Layout(major_to_minor=(1, 0, 2)))


def local(
    dims, node_feats, cotangent, wigner, radial, edge_src, edge_dst, edge_count, params, moment1,
    moment2,
):
    nat, coef, chan = node_feats.shape
    layers, length = params.shape
    zs, ys, xs = dims
    shards = zs * ys * 2 * xs
    edges = edge_src.shape[0]
    shape = (nat, coef, chan, wigner.shape[0], edges)

    inputs = (
        edge_count,
        jnp.transpose(node_feats, (1, 0, 2)),
        jnp.transpose(cotangent, (1, 0, 2)),
        jnp.transpose(wigner, (1, 0, 2)),
        radial,
        edge_src[None, :],
        edge_dst[None, :],
    )
    if length % (4 * LANES) == 0 and ys == 2 and xs == 2 and zs > 1:
        used = length // LANES
        own = woven(params.reshape(layers, used, LANES))
        own = jnp.transpose(own, (1, 0, 2)).reshape(used * layers, LANES)
        owned = owned_grads(dims, own, length, inputs, shape, 0)
        grad = woven(jnp.transpose(owned.reshape(used, layers, LANES), (1, 0, 2)))
        grad = grad.reshape(layers, length)
    else:
        block = LANES * 16 * PIECES
        padded = -(-length // block) * block
        rows = padded // LANES
        own = jnp.pad(params.astype(jnp.bfloat16), ((0, 0), (0, padded - length)))
        full = gather_shards(dims, own.reshape(layers, rows, LANES), 0)
        full = full.reshape(layers, shards, padded)[:, :, :length]
        full = full.reshape(layers, shards * length // LANES, LANES)
        grad = device_grads(inputs, full, shape).reshape(layers, shards, length)
        grad = jnp.pad(grad, ((0, 0), (0, 0), (0, padded - length)))
        owned = reduce_shards(dims, grad.reshape(layers, zs, ys, 2, xs, rows, LANES), 1)
        grad = owned.reshape(layers, padded)[:, :length]
    new_moment1 = 0.9 * moment1 + 0.1 * grad
    new_moment2 = 0.95 * moment2 + 0.05 * grad * grad
    m_hat = new_moment1 / (1.0 - 0.9**60)
    v_hat = new_moment2 / (1.0 - 0.95**60)
    new_params = params - 0.01 * (m_hat / (jnp.sqrt(v_hat) + 1e-08) + 0.1 * params)
    return (new_params, new_moment1, new_moment2)


def solution(mesh):
    both = ("dp", "node")
    return jax.shard_map(
        functools.partial(local, split_axes(mesh)),
        mesh=mesh,
        in_specs=(
            P(both, None, None),
            P(both, None, None),
            P(None, None, both),
            P(None, both, None),
            P(both),
            P(both),
            P(both),
            P(None, both),
            P(None, both),
            P(None, both),
        ),
        out_specs=(P(None, both), P(None, both), P(None, both)),
        check_vma=False,
    )
```

```python
import functools

import jax
import jax.numpy as jnp
from jax import lax
from jax.experimental import pallas as pl
from jax.experimental.layout import Layout, with_layout_constraint
from jax.experimental.pallas import tpu as pltpu
from jax.sharding import PartitionSpec as P

AVG = 10
LANES = 128
PIECES = 3
LINK = jnp.bfloat16
WORK = 16
ACROSS = (1, 1)


def split_axes(mesh):
    rest = mesh.shape["dp"] // 2
    y = 1
    while y * y * 4 <= rest and rest % (y * 2) == 0:
        y *= 2
    return rest // y, y, mesh.shape["node"]


def place(dims):
    zs, ys, xs = dims
    dp = lax.axis_index("dp")
    x = lax.axis_index("node")
    core = lax.rem(dp, 2)
    y = lax.rem(dp // 2, ys)
    z = dp // (2 * ys)
    return {"z": z, "y": y, "c": core, "x": x}


def device(dims, at):
    return {"dp": (at["z"] * dims[1] + at["y"]) * 2 + at["c"], "node": at["x"]}


def peer_of(dims, me, axis, step):
    size = {"z": dims[0], "y": dims[1], "c": 2, "x": dims[2]}[axis]
    other = dict(me)
    other[axis] = lax.rem(me[axis] + step, size)
    return other


def size_of(dims, axis):
    return {"z": dims[0], "y": dims[1], "c": 2, "x": dims[2]}[axis]


def greet(dims, me, meanwhile=lambda: None, corner=False):
    barrier = pltpu.get_barrier_semaphore()
    count = 0
    if corner:
        pl.semaphore_signal(
            barrier,
            inc=1,
            device_id=device(dims, dict(me, x=1 - me["x"], y=1 - me["y"])),
            device_id_type=pl.DeviceIdType.MESH,
        )
        count += 1
    for axis in "zyxc":
        for step in range(1, size_of(dims, axis)):
            pl.semaphore_signal(
                barrier,
                inc=1,
                device_id=device(dims, peer_of(dims, me, axis, step)),
                device_id_type=pl.DeviceIdType.MESH,
            )
            count += 1
    meanwhile()
    pl.semaphore_wait(barrier, count)


def gather_steps(dims, me, own_ref, out_ref, local_sem, send_sem, recv_sem):
    layers, rows = own_ref.shape[0], own_ref.shape[1]
    part = rows // PIECES
    mine = pltpu.make_async_copy(
        own_ref, out_ref.at[:, me["z"], me["y"], me["c"], me["x"]], local_sem
    )
    mine.start()
    most = max(size_of(dims, a) for a in "zyxc") - 1
    started = {}
    state = {"mine": True}

    def view(ref, layer, piece, spans, at):
        index = [layer]
        for axis in "zycx":
            index.append(slice(None) if axis in spans else at[axis])
        index.append(pl.ds(piece * part, part))
        return ref.at[tuple(index)]

    def advance(layer, phase):
        for piece in range(PIECES):
            number = layer * PIECES + piece
            order = "zyxc" if number % 2 == 0 else "zxyc"
            if phase:
                for copy in started[number, phase - 1]:
                    copy.wait_recv()
                if state["mine"]:
                    mine.wait()
                    state["mine"] = False
            if phase == 4:
                continue
            axis, spans = order[phase], order[:phase]
            copies = []
            for step in range(1, size_of(dims, axis)):
                if phase == 0:
                    src = own_ref.at[layer, pl.ds(piece * part, part)]
                else:
                    src = view(out_ref, layer, piece, spans, me)
                slot = (number * 4 + phase) * most + step - 1
                copy = pltpu.make_async_remote_copy(
                    src_ref=src,
                    dst_ref=view(out_ref, layer, piece, spans, me),
                    send_sem=send_sem.at[slot],
                    recv_sem=recv_sem.at[slot],
                    device_id=device(dims, peer_of(dims, me, axis, step)),
                    device_id_type=pl.DeviceIdType.MESH,
                )
                copy.start()
                copies.append(copy)
            started[number, phase] = copies

    def finish():
        for copies in started.values():
            for copy in copies:
                copy.wait_send()

    return advance, finish


def gather_kernel(dims, own_ref, out_ref, local_sem, send_sem, recv_sem):
    me = place(dims)
    greet(dims, me)
    advance, finish = gather_steps(dims, me, own_ref, out_ref, local_sem, send_sem, recv_sem)
    for phase in range(5):
        for layer in range(own_ref.shape[0]):
            advance(layer, phase)
    finish()


def gather_shards(dims, own, collective_id):
    layers, rows, lanes = own.shape
    zs, ys, xs = dims
    most = max(zs, ys, xs, 2) - 1
    slots = layers * PIECES * 4 * most
    return pl.pallas_call(
        functools.partial(gather_kernel, dims),
        out_shape=jax.ShapeDtypeStruct((layers, zs, ys, 2, xs, rows, lanes), own.dtype),
        in_specs=[pl.BlockSpec(memory_space=pltpu.VMEM)],
        out_specs=pl.BlockSpec(memory_space=pltpu.VMEM),
        scratch_shapes=[
            pltpu.SemaphoreType.DMA,
            pltpu.SemaphoreType.DMA((slots,)),
            pltpu.SemaphoreType.DMA((slots,)),
        ],
        compiler_params=pltpu.CompilerParams(
            collective_id=collective_id, has_side_effects=True, vmem_limit_bytes=48 << 20
        ),
        name="gather_shards",
    )(own)


def reduce_buffers(dims, pairs, part):
    zs = dims[0]
    buffers = []
    for first, second, count in pairs:
        n1, n2 = size_of(dims, first), size_of(dims, second)
        buffers += [
            pltpu.VMEM((count, zs, n2, part, LANES), jnp.float32),
            pltpu.VMEM((count, n1 - 1, zs, n2, part, LANES), LINK),
            pltpu.VMEM((count, n1 - 1, zs, n2, part, LANES), LINK),
            pltpu.VMEM((count, zs, part, LANES), jnp.float32),
            pltpu.VMEM((count, n2 - 1, zs, part, LANES), LINK),
            pltpu.VMEM((count, n2 - 1, zs, part, LANES), LINK),
            pltpu.VMEM((count, part, LANES), jnp.float32),
            pltpu.VMEM((count, zs - 1, part, LANES), LINK),
            pltpu.VMEM((count, zs - 1, part, LANES), LINK),
        ]
    return buffers


def reduce_items(layers):
    items = []
    for layer in reversed(range(layers)):
        for piece in range(PIECES):
            number = len(items)
            items.append((layer, piece, number % 2, number // 2))
    return items


def reduce_steps(dims, me, grad_ref, out_ref, pair_buf, scratch):
    zs = dims[0]
    buffers = (scratch[:9], scratch[9:18])
    send_sem, recv_sem = scratch[18:20]
    layers, rows = out_ref.shape[0], out_ref.shape[1]
    part = rows // PIECES
    items = reduce_items(layers)
    most = max(size_of(dims, a) for a in "zyxc") - 1
    pending = []

    def send(number, phase, step, axis, src, dst):
        slot = (number * 4 + phase) * most + step - 1
        copy = pltpu.make_async_remote_copy(
            src_ref=src,
            dst_ref=dst,
            send_sem=send_sem.at[slot],
            recv_sem=recv_sem.at[slot],
            device_id=device(dims, peer_of(dims, me, axis, step)),
            device_id_type=pl.DeviceIdType.MESH,
        )
        copy.start()
        pending.append(copy)
        return copy

    def f32(value):
        return value.astype(jnp.float32)

    waits = {}

    def advance(wanted, now):
        phase = now - 1
        for number, (layer, piece, kind, place_in) in enumerate(items):
            if layer != wanted:
                continue
            if now == 0:
                waits[number] = [
                    send(
                        number, 0, 1, "c",
                        grad_ref.at[layer, :, :, 1 - me["c"], :, pl.ds(piece * part, part)],
                        pair_buf.at[number],
                    )
                ]
                continue
            span = pl.ds(piece * part, part)
            acc1, send1, recv1, acc2, send2, recv2, acc3, send3, recv3 = (
                buf.at[place_in] for buf in buffers[kind]
            )
            first, second = ("x", "y") if kind == 0 else ("y", "x")
            n1, n2 = size_of(dims, first), size_of(dims, second)
            for copy in waits[number]:
                copy.wait_recv()
            copies = []
            if phase == 0:
                for step in list(range(1, n1)) + [0]:
                    k1 = lax.rem(me[first] + step, n1)

                    def one(i, carry, step=step, k1=k1):
                        z, k2 = i // n2, lax.rem(i, n2)
                        y, x = (k2, k1) if kind == 0 else (k1, k2)
                        total = f32(grad_ref[layer, z, y, me["c"], x, span]) + f32(
                            pair_buf[number, z, y, x]
                        )
                        if step:
                            send1[step - 1, z, k2] = total.astype(LINK)
                        else:
                            acc1[z, k2] = total
                        return carry

                    lax.fori_loop(0, zs * n2, one, 0)
                    if step:
                        copies.append(
                            send(number, 1, step, first, send1.at[step - 1], recv1.at[step - 1])
                        )
            elif phase == 1:
                for step in list(range(1, n2)) + [0]:
                    k2 = lax.rem(me[second] + step, n2)

                    def one(z, carry, step=step, k2=k2):
                        total = acc1[z, k2]
                        for e in range(n1 - 1):
                            total = total + f32(recv1[e, z, k2])
                        if step:
                            send2[step - 1, z] = total.astype(LINK)
                        else:
                            acc2[z] = total
                        return carry

                    lax.fori_loop(0, zs, one, 0)
                    if step:
                        copies.append(
                            send(number, 2, step, second, send2.at[step - 1], recv2.at[step - 1])
                        )
            elif phase == 2:
                for step in list(range(1, zs)) + [0]:
                    z = lax.rem(me["z"] + step, zs)
                    total = acc2[z]
                    for e in range(n2 - 1):
                        total = total + f32(recv2[e, z])
                    if step:
                        send3[step - 1] = total.astype(LINK)
                        copies.append(
                            send(number, 3, step, "z", send3.at[step - 1], recv3.at[step - 1])
                        )
                    else:
                        acc3[...] = total
            else:
                total = acc3[...]
                for e in range(zs - 1):
                    total = total + f32(recv3[e])
                out_ref[layer, span] = total
            waits[number] = copies

    def finish():
        for copy in pending:
            copy.wait_send()

    return advance, finish


def reduce_kernel(dims, grad_ref, out_ref, pair_buf, *scratch):
    me = place(dims)
    greet(dims, me)
    advance, finish = reduce_steps(dims, me, grad_ref, out_ref, pair_buf, scratch)
    for phase in range(5):
        for layer in reversed(range(out_ref.shape[0])):
            advance(layer, phase)
    finish()


def reduce_shards(dims, grad, collective_id):
    layers, _, _, _, _, rows, lanes = grad.shape
    return pl.pallas_call(
        functools.partial(reduce_kernel, dims),
        out_shape=jax.ShapeDtypeStruct((layers, rows, lanes), jnp.float32),
        in_specs=[pl.BlockSpec(memory_space=pltpu.VMEM)],
        out_specs=pl.BlockSpec(memory_space=pltpu.VMEM),
        scratch_shapes=reduce_scratch(dims, layers, rows),
        compiler_params=pltpu.CompilerParams(
            collective_id=collective_id, has_side_effects=True, vmem_limit_bytes=48 << 20
        ),
        name="reduce_shards",
    )(grad)


def dot(a, b, over=(1, 0)):
    return lax.dot_general(
        a, b, (((over[0],), (over[1],)), ((), ())), preferred_element_type=jnp.float32
    )


def compute_kernel(
    shape, count_ref, x_ref, cot_ref, wig_ref, rad_ref, src_ref, dst_ref, flat_ref, grad_ref,
    *scratch,
):
    rows_f = scratch[0]

    def unpack(layer):
        rows_f[...] = flat_ref[layer].astype(jnp.float32)

    def packed(layer, block):
        if block == 2:
            grad_ref[layer] = rows_f[...].astype(jnp.bfloat16)

    refs = (count_ref, x_ref, cot_ref, wig_ref, rad_ref, src_ref, dst_ref)
    skip = lambda *step: None
    compute(shape, refs, scratch, unpack, packed, skip, skip, skip)


def node_rows(nat, coef):
    return -(-nat * coef // 32) * 32


def compute(shape, refs, scratch, unpack, packed, gather, reduce, ready):
    count_ref, x_ref, cot_ref, wig_ref, rad_ref, src_ref, dst_ref = refs
    (
        rows_f, wzero, wreal, wimag, pick, put, scale, rotated, flat_a, mixed, node_t,
        outs, nodes, back, dnode, dmix,
    ) = scratch
    nat, coef, chan, rows, edges = shape
    lone = (rows + 2) // 3
    kzero, kone = lone * chan, (lone - 1) * chan
    used, tall = nat * coef, node_rows(nat, coef)
    bf16, f32 = jnp.bfloat16, jnp.float32
    eye = (
        lax.broadcasted_iota(jnp.int32, (chan, chan), 0)
        == lax.broadcasted_iota(jnp.int32, (chan, chan), 1)
    ).astype(f32).astype(bf16)

    def span(k, size):
        return slice(k * size, (k + 1) * size)

    def filled(value):
        value = value.reshape(used, chan)
        return jnp.concatenate([value, jnp.zeros((tall - used, chan), f32)], axis=0)

    def spread_wigner(hooks):
        atoms = lax.broadcasted_iota(jnp.int32, (nat, edges), 0)
        slots = lax.broadcasted_iota(jnp.int32, (nat, edges), 1)
        taken = (src_ref[...] == atoms).astype(f32)
        live = ((dst_ref[...] == atoms) & (slots < count_ref[0])).astype(f32)

        def write(first, coefs, at, size):
            values = [wig_ref[first + n].astype(f32) for n in range(coefs)]
            for k in range(rows):
                for ref, mask in ((pick, taken), (put, live)):
                    parts = [value[k : k + 1] * mask for value in values]
                    if size > coefs * nat:
                        parts.append(jnp.zeros((size - coefs * nat, edges), f32))
                    ref[pl.ds(at, size), span(k, edges)] = jnp.concatenate(
                        parts, axis=0
                    ).astype(bf16)

        pairs = coef // 2

        def one(p, carry):
            write(2 * p, 2, pl.multiple_of(p * 2 * nat, 2 * nat), 2 * nat)
            return carry

        parts = len(hooks) + 1
        for n in range(parts):
            lax.fori_loop(n * pairs // parts, (n + 1) * pairs // parts, one, 0)
            if n < len(hooks):
                hooks[n]()
        at = pairs * 2 * nat
        write(2 * pairs, coef - 2 * pairs, at, tall - at)

    def blocks():
        cut = kzero * kzero // LANES
        step = kone * kone // LANES
        return ((wzero, 0, kzero), (wreal, cut, kone), (wimag, cut + step, kone))

    def load_weights(layer):
        unpack(layer)
        for ref, start, size in blocks():
            per = size // LANES
            for c in range(per):
                ref[:, c * LANES : (c + 1) * LANES] = rows_f[
                    pl.ds(start + c, size, stride=per), :
                ].astype(bf16)

    def store_grads(layer, grads):
        for block, ((_, start, size), grad) in enumerate(zip(blocks(), grads)):
            per = size // LANES
            wide = 2 * LANES
            for n in range(0, size, wide):
                value = grad(n, min(n + wide, size))
                for c in range(value.shape[1] // LANES):
                    rows_f[pl.ds(start + n // LANES + c, size, stride=per), :] = value[
                        :, span(c, LANES)
                    ]
            packed(layer, block)

    def to_nodes(matrix, source):
        half = tall // 2
        return jnp.concatenate(
            [dot(matrix[span(n, half), :], source[...]) for n in range(2)], axis=0
        )[:used]

    def rotate(layer, hooks):
        node_t[...] = dot(eye, nodes[...], (1, 1)).astype(bf16)
        for k in range(rows):
            for n, hook in enumerate(hooks):
                if k == (n + 1) * rows // (len(hooks) + 1):
                    hook()
            value = dot(node_t[...], pick[:, span(k, edges)]) * scale[layer]
            value = value.astype(bf16)
            rotated[layer, span(k, chan)] = value
            flat_a[:, span(k, chan)] = value.T

    def forward(layer, last, hooks):
        gather(layer, 5)
        load_weights(layer)
        for hook in hooks[:1]:
            hook()
        azero = flat_a[:, :kzero]
        aplus = flat_a[:, kzero : kzero + kone]
        aminus = flat_a[:, kzero + kone :]

        def keep(first, value):
            for c in range(value.shape[1] // chan):
                mixed[span(first + c, edges)] = value[:, span(c, chan)].astype(bf16)

        wide = 2 * LANES
        for n in range(0, kzero, wide):
            keep(n // chan, dot(azero, wzero[:, n : min(n + wide, kzero)]))
        for n in range(0, kone, wide):
            real, imag = (w[:, n : min(n + wide, kone)] for w in (wreal, wimag))
            keep(lone + n // chan, dot(aplus, real) - dot(aminus, imag))
            keep(2 * lone - 1 + n // chan, dot(aplus, imag) + dot(aminus, real))
        for hook in hooks[1:]:
            hook()
        total = to_nodes(put, mixed)
        before = nodes[...].astype(f32)[:used]
        outs[layer] = before + total / AVG
        if last:
            return
        value = outs[layer].reshape(coef, nat, chan)
        gate = jax.nn.sigmoid(value[0])
        nodes[...] = filled(value * gate[None]).astype(bf16)

    def backward(layer, cot, last, hooks):
        value = outs[layer].reshape(coef, nat, chan)
        scalar = value[0]
        gate = jax.nn.sigmoid(scalar)
        slope = gate * (1.0 - gate)
        total = jnp.sum(cot[1:] * value[1:], axis=0)
        lead = cot[0] * (gate + scalar * slope) + total * slope
        dout = jnp.concatenate([lead[None], cot[1:] * gate[None]], axis=0)
        dnode[...] = dout.reshape(used, chan)
        share = filled(dout / AVG)
        high = share.astype(bf16)
        node_t[...] = dot(eye, high, (1, 1)).astype(bf16)
        for k in range(rows):
            dmix[span(k, chan)] = dot(node_t[...], put[:, span(k, edges)]).astype(bf16)
        dzero = dmix.at[:kzero]
        dplus = dmix.at[kzero : kzero + kone]
        dminus = dmix.at[kzero + kone :]
        azero = rotated[layer, :kzero]
        aplus = rotated[layer, kzero : kzero + kone]
        aminus = rotated[layer, kzero + kone :]
        for hook in hooks[:1]:
            hook()
        nt = (1, 1)
        store_grads(
            layer,
            (
                lambda a, b: dot(azero, dzero[a:b], nt),
                lambda a, b: dot(aplus, dplus[a:b], nt) + dot(aminus, dminus[a:b], nt),
                lambda a, b: dot(aplus, dminus[a:b], nt) - dot(aminus, dplus[a:b], nt),
            ),
        )
        if last:
            return

        def keep(first, value):
            for c in range(value.shape[0] // chan):
                part = value[span(c, chan)].astype(bf16).astype(f32) * scale[layer]
                mixed[span(first + c, edges)] = part.astype(bf16).T

        keep(0, dot(wzero[...], dzero[...]))
        keep(lone, dot(wreal[...], dplus[...]) + dot(wimag[...], dminus[...]))
        for hook in hooks[1:2]:
            hook()
        keep(2 * lone - 1, dot(wreal[...], dminus[...]) - dot(wimag[...], dplus[...]))
        total = to_nodes(pick, mixed)
        for hook in hooks[2:]:
            hook()
        back[...] = filled(dnode[...] + total).astype(bf16)

    def step(move, layer, phase):
        return lambda: move(layer, phase)

    def none():
        return None

    gather(0, 0)
    gather(0, 6)
    ready("next")
    ready("x")
    nodes[...] = filled(x_ref[...].astype(f32)).astype(bf16)
    ready("rad")
    for layer in range(rad_ref.shape[0]):
        scale[layer] = rad_ref[layer].astype(f32).T
    ready("wig")
    spread_wigner((none, step(gather, 0, 1)))
    gather(1, 0)
    gather(1, 6)
    rotate(0, (step(gather, 0, 2), ))
    gather(0, 3)
    gather(1, 1)
    gather(0, 4)
    forward(0, False, (step(gather, 1, 2), ))
    rotate(1, (step(gather, 1, 3), step(gather, 1, 4), ))
    forward(1, True, ())
    ready("cot")
    backward(1, cot_ref[...].astype(f32), False, (none, step(reduce, 1, 1)))
    last = back[...].astype(f32)[:used].reshape(coef, nat, chan)
    backward(0, last, True, ())
    for layer, phase in ((1, 2), (0, 1), (1, 3), (0, 2), (0, 3), (1, 4), (0, 4)):
        reduce(layer, phase)


def side(me):
    core = me["c"]
    return me["y"] * (1 - core) + me["x"] * core, me["x"] * (1 - core) + me["y"] * core


def spot(me, z, a, b):
    core = me["c"]
    return {"z": z, "y": a * (1 - core) + b * core, "c": core, "x": b * (1 - core) + a * core}


def order_of(zs):
    return sorted(range(1, zs), key=lambda step: (min(step, zs - step), step))


def remote(src, dst, send_sem, recv_sem, target):
    return pltpu.make_async_remote_copy(
        src_ref=src,
        dst_ref=dst,
        send_sem=send_sem,
        recv_sem=recv_sem,
        device_id=target,
        device_id_type=pl.DeviceIdType.MESH,
    )


def gather_slots(dims):
    return 4 * dims[0] + 3


def stream_gather(dims, me, full_ref, send_sem, recv_sem):
    zs = dims[0]
    a, b = side(me)
    near = order_of(zs)
    across = {layer: near[len(near) - count :] for layer, count in enumerate(ACROSS)}
    copies = {}

    def send(layer, slot, at, target):
        where = full_ref.at[(layer, at["z"], at["y"], at["c"], at["x"])]
        sems = (send_sem.at[layer, slot], recv_sem.at[layer, slot])
        copies[layer, slot] = remote(where, where, *sems, device(dims, target))
        copies[layer, slot].start()

    def by_z(layer, step):
        target = dict(me, z=lax.rem(me["z"] + step, zs))
        send(layer, step - 1, me, target)

    def by_a(layer, step):
        z = lax.rem(me["z"] + zs - step, zs)
        send(layer, zs - 1 + step, spot(me, z, a, b), spot(me, me["z"], 1 - a, b))

    def by_b(layer, step, far):
        z = lax.rem(me["z"] + zs - step, zs)
        at = spot(me, z, 1 - a if far else a, b)
        send(layer, (3 if far else 2) * zs - 1 + step, at, spot(me, me["z"], a, 1 - b))

    def by_corner(layer, step):
        z = lax.rem(me["z"] + zs - step, zs)
        send(layer, 3 * zs - 1 + step, spot(me, z, a, b), spot(me, me["z"], 1 - a, 1 - b))

    def by_c(layer, number):
        at = spot(me, slice(None), 1 - a if number % 2 else a, 1 - b if number // 2 else b)
        send(layer, 4 * zs - 1 + number, at, dict(me, c=1 - me["c"]))

    def wait(layer, slot):
        copies[layer, slot].wait_recv()

    def advance(layer, phase):
        if phase == 0:
            for step in near:
                by_z(layer, step)
        elif phase == 6:
            by_a(layer, 0)
            by_b(layer, 0, False)
        elif phase == 1:
            for step in near:
                wait(layer, step - 1)
                by_a(layer, step)
                by_b(layer, step, False)
                if step in across[layer]:
                    by_corner(layer, step)
            wait(layer, zs - 1)
            by_b(layer, 0, True)
            by_c(layer, 0)
        elif phase == 2:
            for step in near:
                wait(layer, zs - 1 + step)
                if step not in across[layer]:
                    by_b(layer, step, True)
            by_c(layer, 1)
        elif phase == 3:
            for step in [0] + near:
                wait(layer, 2 * zs - 1 + step)
            by_c(layer, 2)
        elif phase == 4:
            for step in [0] + near:
                wait(layer, 3 * zs - 1 + step)
            by_c(layer, 3)
        else:
            for number in range(4):
                wait(layer, 4 * zs - 1 + number)

    def finish():
        for copy in copies.values():
            copy.wait_send()

    return advance, finish


def reduce_slots(dims):
    return 5 * dims[0] - 1


def stream_reduce(dims, me, grad_ref, store, buffers, send_sem, recv_sem):
    zs = dims[0]
    a, b = side(me)
    pair, send_b, recv_b, send_a, recv_a, send_z, recv_z, total = buffers
    steps = list(reversed(order_of(zs))) + [0]
    copies = {}

    def send(key, layer, slot, src, dst, target):
        sems = (send_sem.at[layer, slot], recv_sem.at[layer, slot])
        copies[key] = remote(src, dst, *sems, device(dims, target))
        copies[key].start()

    def f32(value):
        return value.astype(jnp.float32)

    def depth(step):
        return lax.rem(me["z"] + step, zs)

    def own(layer, z, a, b):
        at = spot(me, z, a, b)
        return f32(grad_ref[layer, z, at["y"], at["c"], at["x"]]) + f32(
            pair[layer, z, at["y"], at["x"]]
        )

    def exchange(layer, z):
        send(
            ("c", layer, z), layer, z, grad_ref.at[layer, z, :, 1 - me["c"]], pair.at[layer, z],
            dict(me, c=1 - me["c"]),
        )

    def advance(layer, phase):
        if phase == 1:
            for z in range(zs):
                copies["c", layer, z].wait_recv()
            for near in range(2):
                for step in steps:
                    value = own(layer, depth(step), a if near else 1 - a, 1 - b)
                    send_b[layer, step, near] = value.astype(LINK)
                    send(
                        ("b", layer, step, near), layer, zs + 2 * step + near,
                        send_b.at[layer, step, near], recv_b.at[layer, step, near],
                        spot(me, me["z"], a, 1 - b),
                    )
        elif phase == 2:
            for step in steps:
                copies["b", layer, step, 0].wait_recv()
                value = own(layer, depth(step), 1 - a, b) + f32(recv_b[layer, step, 0])
                send_a[layer, step] = value.astype(LINK)
                send(
                    ("a", layer, step), layer, 3 * zs + step, send_a.at[layer, step],
                    recv_a.at[layer, step], spot(me, me["z"], 1 - a, b),
                )
        elif phase == 3:
            for step in steps:
                copies["b", layer, step, 1].wait_recv()
                copies["a", layer, step].wait_recv()
                value = (
                    own(layer, depth(step), a, b)
                    + f32(recv_b[layer, step, 1])
                    + f32(recv_a[layer, step])
                )
                if step == 0:
                    total[layer] = value
                    continue
                send_z[layer, step - 1] = value.astype(LINK)
                send(
                    ("z", layer, step), layer, 4 * zs + step - 1, send_z.at[layer, step - 1],
                    recv_z.at[layer, step - 1], dict(me, z=depth(step)),
                )
        else:
            value = total[layer]
            for step in order_of(zs):
                copies["z", layer, step].wait_recv()
                value = value + f32(recv_z[layer, step - 1])
            store(layer, value)

    def finish():
        for copy in copies.values():
            copy.wait_send()

    return exchange, advance, finish


def fused_kernel(
    dims, shape, length, own_ref, count_ref, x_ref, cot_ref, wig_ref, rad_ref, src_ref, dst_ref,
    out_ref, par, x, cot, wig, rad, load_sem, full_ref, grad_ref, gather_send, gather_recv,
    reduce_send, reduce_recv, *scratch,
):
    zs, ys, xs = dims
    me = place(dims)
    loads = {}
    for number, (name, source, ref) in enumerate(
        (
            ("own", own_ref, par), ("x", x_ref, x), ("rad", rad_ref, rad), ("wig", wig_ref, wig),
            ("cot", cot_ref, cot),
        )
    ):
        loads[name] = pltpu.make_async_copy(source, ref, load_sem.at[number])

    def ready(name):
        if name == "next":
            for layer in range(1, layers):
                place_own(layer)
            return
        loads[name].wait()

    work, rest = scratch[:WORK], scratch[WORK:]
    rows_f = work[0]
    used, rows = length // LANES, full_ref.shape[-2]
    layers, tail = full_ref.shape[0], used % 8
    odd = me["x"] == 1
    wide = used + tail

    def store(layer, value):
        value = jnp.where(odd, value[tail:wide], value[:used])
        out_ref[pl.ds(layer, used, stride=layers), :] = value

    loads["own"].start()

    def meanwhile():
        for name, load in loads.items():
            if name != "own":
                load.start()
        ready("own")
        place_own(0)

    def place_own(layer):
        value = par[pl.ds(layer, used, stride=layers), :]
        low = jnp.zeros((tail, LANES), jnp.float32)
        high = jnp.zeros((rows - wide, LANES), jnp.float32)
        value = jnp.where(
            odd,
            jnp.concatenate([low, value, high], axis=0),
            jnp.concatenate([value, low, high], axis=0),
        )
        full_ref[layer, me["z"], me["y"], me["c"], me["x"]] = value.astype(jnp.bfloat16)

    greet(dims, me, meanwhile, True)
    gather, gathered = stream_gather(dims, me, full_ref, gather_send, gather_recv)
    exchange, reduce, reduced = stream_reduce(
        dims, me, grad_ref, store, rest, reduce_send, reduce_recv
    )

    def pairs():
        for number in range(zs * ys * 2):
            yield number, (number // (2 * ys), number // 2 % ys, number % 2)

    def unpack(layer):
        for number, at in pairs():
            even, uneven = (full_ref[(layer,) + at + (x,)].astype(jnp.float32) for x in range(2))
            first, cut = number * 2 * used, used - tail
            if tail:
                rows_f[first : first + cut, :] = even[:cut]
                rows_f[first + cut : first + cut + 8, :] = even[cut : cut + 8] + uneven[:8]
                rows_f[first + cut + 8 : first + 2 * used, :] = uneven[8:wide]
            else:
                rows_f[first : first + used, :] = even[:used]
                rows_f[first + used : first + 2 * used, :] = uneven[:used]

    ends = [0]
    for size, count in (((shape[3] + 2) // 3, 1), ((shape[3] + 2) // 3 - 1, 2)):
        for _ in range(count):
            ends.append(ends[-1] + (size * shape[2]) ** 2 // LANES)

    def packed(layer, block):
        for number, at in pairs():
            last = (number // (2 * ys) + 1) * (2 * ys) * 2 * used
            if not ends[block] < last <= ends[block + 1]:
                continue
            first = number * 2 * used
            for x, start in enumerate((first, first + used - tail)):
                grad_ref[(layer,) + at + (x,)] = rows_f[start : start + rows, :].astype(
                    jnp.bfloat16
                )
            if number % (2 * ys) == 2 * ys - 1:
                exchange(layer, at[0])

    refs = (count_ref, x, cot, wig, rad, src_ref, dst_ref)
    compute(shape, refs, work, unpack, packed, gather, reduce, ready)
    gathered()
    reduced()


def work_buffers(shape, flat_rows):
    nat, coef, chan, rows, edges = shape
    lone = (rows + 2) // 3
    kzero, kone = lone * chan, (lone - 1) * chan
    used, tall = nat * coef, node_rows(nat, coef)
    return [
        pltpu.VMEM((flat_rows, LANES), jnp.float32),
        pltpu.VMEM((kzero, kzero), jnp.bfloat16),
        pltpu.VMEM((kone, kone), jnp.bfloat16),
        pltpu.VMEM((kone, kone), jnp.bfloat16),
        pltpu.VMEM((tall, rows * edges), jnp.bfloat16),
        pltpu.VMEM((tall, rows * edges), jnp.bfloat16),
        pltpu.VMEM((2, chan, edges), jnp.float32),
        pltpu.VMEM((2, rows * chan, edges), jnp.bfloat16),
        pltpu.VMEM((edges, rows * chan), jnp.bfloat16),
        pltpu.VMEM((rows * edges, chan), jnp.bfloat16),
        pltpu.VMEM((chan, tall), jnp.bfloat16),
        pltpu.VMEM((2, used, chan), jnp.float32),
        pltpu.VMEM((tall, chan), jnp.bfloat16),
        pltpu.VMEM((tall, chan), jnp.bfloat16),
        pltpu.VMEM((used, chan), jnp.float32),
        pltpu.VMEM((rows * chan, edges), jnp.bfloat16),
    ]


def reduce_scratch(dims, layers, rows):
    zs, ys, xs = dims
    part = rows // PIECES
    most = max(zs, ys, xs, 2) - 1
    count = layers * PIECES
    slots = count * 4 * most
    even, odd = (count + 1) // 2, count // 2
    return (
        [pltpu.VMEM((count, zs, ys, xs, part, LANES), jnp.bfloat16)]
        + reduce_buffers(dims, (("x", "y", even), ("y", "x", odd)), part)
        + [pltpu.SemaphoreType.DMA((slots,)), pltpu.SemaphoreType.DMA((slots,))]
    )


def owned_grads(dims, own, length, inputs, shape, collective_id):
    zs, ys, xs = dims
    used = length // LANES
    layers = own.shape[0] // used
    rows = -(-(used + used % 8) // 16) * 16
    spread = (layers, zs, ys, 2, xs, rows, LANES)
    flat_rows = zs * ys * 2 * xs * used
    flat_rows = -(-(flat_rows + rows) // 8) * 8
    vmem = pl.BlockSpec(memory_space=pltpu.VMEM)
    hbm = pl.BlockSpec(memory_space=pl.ANY)
    item, link = (rows, LANES), jnp.bfloat16
    return pl.pallas_call(
        functools.partial(fused_kernel, dims, shape, length),
        out_shape=jax.ShapeDtypeStruct(own.shape, jnp.float32),
        in_specs=[hbm, pl.BlockSpec(memory_space=pltpu.SMEM)] + [hbm] * 4 + [vmem] * 2,
        out_specs=vmem,
        scratch_shapes=[
            pltpu.VMEM(own.shape, own.dtype),
            pltpu.VMEM(inputs[1].shape, inputs[1].dtype),
            pltpu.VMEM(inputs[2].shape, inputs[2].dtype),
            pltpu.VMEM(inputs[3].shape, inputs[3].dtype),
            pltpu.VMEM(inputs[4].shape, inputs[4].dtype),
            pltpu.SemaphoreType.DMA((5,)),
            pltpu.VMEM(spread, jnp.bfloat16),
            pltpu.VMEM(spread, jnp.bfloat16),
            pltpu.SemaphoreType.DMA((layers, gather_slots(dims))),
            pltpu.SemaphoreType.DMA((layers, gather_slots(dims))),
            pltpu.SemaphoreType.DMA((layers, reduce_slots(dims))),
            pltpu.SemaphoreType.DMA((layers, reduce_slots(dims))),
        ]
        + work_buffers(shape, flat_rows)
        + [
            pltpu.VMEM((layers, zs, ys, xs) + item, link),
            pltpu.VMEM((layers, zs, 2) + item, link),
            pltpu.VMEM((layers, zs, 2) + item, link),
            pltpu.VMEM((layers, zs) + item, link),
            pltpu.VMEM((layers, zs) + item, link),
            pltpu.VMEM((layers, zs - 1) + item, link),
            pltpu.VMEM((layers, zs - 1) + item, link),
            pltpu.VMEM((layers,) + item, jnp.float32),
        ],
        compiler_params=pltpu.CompilerParams(
            collective_id=collective_id, has_side_effects=True, vmem_limit_bytes=60 << 20
        ),
        name="owned_grads",
    )(own, *inputs)


def device_grads(inputs, flat, shape):
    vmem = pl.BlockSpec(memory_space=pltpu.VMEM)
    return pl.pallas_call(
        functools.partial(compute_kernel, shape),
        out_shape=jax.ShapeDtypeStruct(flat.shape, jnp.bfloat16),
        in_specs=[pl.BlockSpec(memory_space=pltpu.SMEM)] + [vmem] * 7,
        out_specs=vmem,
        scratch_shapes=work_buffers(shape, flat.shape[1]),
        compiler_params=pltpu.CompilerParams(vmem_limit_bytes=56 << 20),
        name="device_grads",
    )(*inputs, flat)


def woven(rows):
    return with_layout_constraint(rows, Layout(major_to_minor=(1, 0, 2)))


def local(
    dims, node_feats, cotangent, wigner, radial, edge_src, edge_dst, edge_count, params, moment1,
    moment2,
):
    nat, coef, chan = node_feats.shape
    layers, length = params.shape
    zs, ys, xs = dims
    shards = zs * ys * 2 * xs
    edges = edge_src.shape[0]
    shape = (nat, coef, chan, wigner.shape[0], edges)

    inputs = (
        edge_count,
        jnp.transpose(node_feats, (1, 0, 2)),
        jnp.transpose(cotangent, (1, 0, 2)),
        jnp.transpose(wigner, (1, 0, 2)),
        radial,
        edge_src[None, :],
        edge_dst[None, :],
    )
    if length % (4 * LANES) == 0 and ys == 2 and xs == 2 and zs > 1:
        used = length // LANES
        own = woven(params.reshape(layers, used, LANES))
        own = jnp.transpose(own, (1, 0, 2)).reshape(used * layers, LANES)
        owned = owned_grads(dims, own, length, inputs, shape, 0)
        grad = woven(jnp.transpose(owned.reshape(used, layers, LANES), (1, 0, 2)))
        grad = grad.reshape(layers, length)
    else:
        block = LANES * 16 * PIECES
        padded = -(-length // block) * block
        rows = padded // LANES
        own = jnp.pad(params.astype(jnp.bfloat16), ((0, 0), (0, padded - length)))
        full = gather_shards(dims, own.reshape(layers, rows, LANES), 0)
        full = full.reshape(layers, shards, padded)[:, :, :length]
        full = full.reshape(layers, shards * length // LANES, LANES)
        grad = device_grads(inputs, full, shape).reshape(layers, shards, length)
        grad = jnp.pad(grad, ((0, 0), (0, 0), (0, padded - length)))
        owned = reduce_shards(dims, grad.reshape(layers, zs, ys, 2, xs, rows, LANES), 1)
        grad = owned.reshape(layers, padded)[:, :length]
    new_moment1 = 0.9 * moment1 + 0.1 * grad
    new_moment2 = 0.95 * moment2 + 0.05 * grad * grad
    m_hat = new_moment1 / (1.0 - 0.9**60)
    v_hat = new_moment2 / (1.0 - 0.95**60)
    new_params = params - 0.01 * (m_hat / (jnp.sqrt(v_hat) + 1e-08) + 0.1 * params)
    return (new_params, new_moment1, new_moment2)


def solution(mesh):
    both = ("dp", "node")
    return jax.shard_map(
        functools.partial(local, split_axes(mesh)),
        mesh=mesh,
        in_specs=(
            P(both, None, None),
            P(both, None, None),
            P(None, None, both),
            P(None, both, None),
            P(both),
            P(both),
            P(both),
            P(None, both),
            P(None, both),
            P(None, both),
        ),
        out_specs=(P(None, both), P(None, both), P(None, both)),
        check_vma=False,
    )
```

```python
import functools

import jax
import jax.numpy as jnp
from jax import lax
from jax.experimental import pallas as pl
from jax.experimental.layout import Layout, with_layout_constraint
from jax.experimental.pallas import tpu as pltpu
from jax.sharding import PartitionSpec as P

AVG = 10
LANES = 128
PIECES = 3
LINK = jnp.bfloat16
WORK = 16
ACROSS = (1, 1)


def split_axes(mesh):
    rest = mesh.shape["dp"] // 2
    y = 1
    while y * y * 4 <= rest and rest % (y * 2) == 0:
        y *= 2
    return rest // y, y, mesh.shape["node"]


def place(dims):
    zs, ys, xs = dims
    dp = lax.axis_index("dp")
    x = lax.axis_index("node")
    core = lax.rem(dp, 2)
    y = lax.rem(dp // 2, ys)
    z = dp // (2 * ys)
    return {"z": z, "y": y, "c": core, "x": x}


def device(dims, at):
    return {"dp": (at["z"] * dims[1] + at["y"]) * 2 + at["c"], "node": at["x"]}


def peer_of(dims, me, axis, step):
    size = {"z": dims[0], "y": dims[1], "c": 2, "x": dims[2]}[axis]
    other = dict(me)
    other[axis] = lax.rem(me[axis] + step, size)
    return other


def size_of(dims, axis):
    return {"z": dims[0], "y": dims[1], "c": 2, "x": dims[2]}[axis]


def greet(dims, me, meanwhile=lambda: None, corner=False):
    barrier = pltpu.get_barrier_semaphore()
    count = 0
    if corner:
        pl.semaphore_signal(
            barrier,
            inc=1,
            device_id=device(dims, dict(me, x=1 - me["x"], y=1 - me["y"])),
            device_id_type=pl.DeviceIdType.MESH,
        )
        count += 1
    for axis in "zyxc":
        for step in range(1, size_of(dims, axis)):
            pl.semaphore_signal(
                barrier,
                inc=1,
                device_id=device(dims, peer_of(dims, me, axis, step)),
                device_id_type=pl.DeviceIdType.MESH,
            )
            count += 1
    meanwhile()
    pl.semaphore_wait(barrier, count)


def gather_steps(dims, me, own_ref, out_ref, local_sem, send_sem, recv_sem):
    layers, rows = own_ref.shape[0], own_ref.shape[1]
    part = rows // PIECES
    mine = pltpu.make_async_copy(
        own_ref, out_ref.at[:, me["z"], me["y"], me["c"], me["x"]], local_sem
    )
    mine.start()
    most = max(size_of(dims, a) for a in "zyxc") - 1
    started = {}
    state = {"mine": True}

    def view(ref, layer, piece, spans, at):
        index = [layer]
        for axis in "zycx":
            index.append(slice(None) if axis in spans else at[axis])
        index.append(pl.ds(piece * part, part))
        return ref.at[tuple(index)]

    def advance(layer, phase):
        for piece in range(PIECES):
            number = layer * PIECES + piece
            order = "zyxc" if number % 2 == 0 else "zxyc"
            if phase:
                for copy in started[number, phase - 1]:
                    copy.wait_recv()
                if state["mine"]:
                    mine.wait()
                    state["mine"] = False
            if phase == 4:
                continue
            axis, spans = order[phase], order[:phase]
            copies = []
            for step in range(1, size_of(dims, axis)):
                if phase == 0:
                    src = own_ref.at[layer, pl.ds(piece * part, part)]
                else:
                    src = view(out_ref, layer, piece, spans, me)
                slot = (number * 4 + phase) * most + step - 1
                copy = pltpu.make_async_remote_copy(
                    src_ref=src,
                    dst_ref=view(out_ref, layer, piece, spans, me),
                    send_sem=send_sem.at[slot],
                    recv_sem=recv_sem.at[slot],
                    device_id=device(dims, peer_of(dims, me, axis, step)),
                    device_id_type=pl.DeviceIdType.MESH,
                )
                copy.start()
                copies.append(copy)
            started[number, phase] = copies

    def finish():
        for copies in started.values():
            for copy in copies:
                copy.wait_send()

    return advance, finish


def gather_kernel(dims, own_ref, out_ref, local_sem, send_sem, recv_sem):
    me = place(dims)
    greet(dims, me)
    advance, finish = gather_steps(dims, me, own_ref, out_ref, local_sem, send_sem, recv_sem)
    for phase in range(5):
        for layer in range(own_ref.shape[0]):
            advance(layer, phase)
    finish()


def gather_shards(dims, own, collective_id):
    layers, rows, lanes = own.shape
    zs, ys, xs = dims
    most = max(zs, ys, xs, 2) - 1
    slots = layers * PIECES * 4 * most
    return pl.pallas_call(
        functools.partial(gather_kernel, dims),
        out_shape=jax.ShapeDtypeStruct((layers, zs, ys, 2, xs, rows, lanes), own.dtype),
        in_specs=[pl.BlockSpec(memory_space=pltpu.VMEM)],
        out_specs=pl.BlockSpec(memory_space=pltpu.VMEM),
        scratch_shapes=[
            pltpu.SemaphoreType.DMA,
            pltpu.SemaphoreType.DMA((slots,)),
            pltpu.SemaphoreType.DMA((slots,)),
        ],
        compiler_params=pltpu.CompilerParams(
            collective_id=collective_id, has_side_effects=True, vmem_limit_bytes=48 << 20
        ),
        name="gather_shards",
    )(own)


def reduce_buffers(dims, pairs, part):
    zs = dims[0]
    buffers = []
    for first, second, count in pairs:
        n1, n2 = size_of(dims, first), size_of(dims, second)
        buffers += [
            pltpu.VMEM((count, zs, n2, part, LANES), jnp.float32),
            pltpu.VMEM((count, n1 - 1, zs, n2, part, LANES), LINK),
            pltpu.VMEM((count, n1 - 1, zs, n2, part, LANES), LINK),
            pltpu.VMEM((count, zs, part, LANES), jnp.float32),
            pltpu.VMEM((count, n2 - 1, zs, part, LANES), LINK),
            pltpu.VMEM((count, n2 - 1, zs, part, LANES), LINK),
            pltpu.VMEM((count, part, LANES), jnp.float32),
            pltpu.VMEM((count, zs - 1, part, LANES), LINK),
            pltpu.VMEM((count, zs - 1, part, LANES), LINK),
        ]
    return buffers


def reduce_items(layers):
    items = []
    for layer in reversed(range(layers)):
        for piece in range(PIECES):
            number = len(items)
            items.append((layer, piece, number % 2, number // 2))
    return items


def reduce_steps(dims, me, grad_ref, out_ref, pair_buf, scratch):
    zs = dims[0]
    buffers = (scratch[:9], scratch[9:18])
    send_sem, recv_sem = scratch[18:20]
    layers, rows = out_ref.shape[0], out_ref.shape[1]
    part = rows // PIECES
    items = reduce_items(layers)
    most = max(size_of(dims, a) for a in "zyxc") - 1
    pending = []

    def send(number, phase, step, axis, src, dst):
        slot = (number * 4 + phase) * most + step - 1
        copy = pltpu.make_async_remote_copy(
            src_ref=src,
            dst_ref=dst,
            send_sem=send_sem.at[slot],
            recv_sem=recv_sem.at[slot],
            device_id=device(dims, peer_of(dims, me, axis, step)),
            device_id_type=pl.DeviceIdType.MESH,
        )
        copy.start()
        pending.append(copy)
        return copy

    def f32(value):
        return value.astype(jnp.float32)

    waits = {}

    def advance(wanted, now):
        phase = now - 1
        for number, (layer, piece, kind, place_in) in enumerate(items):
            if layer != wanted:
                continue
            if now == 0:
                waits[number] = [
                    send(
                        number, 0, 1, "c",
                        grad_ref.at[layer, :, :, 1 - me["c"], :, pl.ds(piece * part, part)],
                        pair_buf.at[number],
                    )
                ]
                continue
            span = pl.ds(piece * part, part)
            acc1, send1, recv1, acc2, send2, recv2, acc3, send3, recv3 = (
                buf.at[place_in] for buf in buffers[kind]
            )
            first, second = ("x", "y") if kind == 0 else ("y", "x")
            n1, n2 = size_of(dims, first), size_of(dims, second)
            for copy in waits[number]:
                copy.wait_recv()
            copies = []
            if phase == 0:
                for step in list(range(1, n1)) + [0]:
                    k1 = lax.rem(me[first] + step, n1)

                    def one(i, carry, step=step, k1=k1):
                        z, k2 = i // n2, lax.rem(i, n2)
                        y, x = (k2, k1) if kind == 0 else (k1, k2)
                        total = f32(grad_ref[layer, z, y, me["c"], x, span]) + f32(
                            pair_buf[number, z, y, x]
                        )
                        if step:
                            send1[step - 1, z, k2] = total.astype(LINK)
                        else:
                            acc1[z, k2] = total
                        return carry

                    lax.fori_loop(0, zs * n2, one, 0)
                    if step:
                        copies.append(
                            send(number, 1, step, first, send1.at[step - 1], recv1.at[step - 1])
                        )
            elif phase == 1:
                for step in list(range(1, n2)) + [0]:
                    k2 = lax.rem(me[second] + step, n2)

                    def one(z, carry, step=step, k2=k2):
                        total = acc1[z, k2]
                        for e in range(n1 - 1):
                            total = total + f32(recv1[e, z, k2])
                        if step:
                            send2[step - 1, z] = total.astype(LINK)
                        else:
                            acc2[z] = total
                        return carry

                    lax.fori_loop(0, zs, one, 0)
                    if step:
                        copies.append(
                            send(number, 2, step, second, send2.at[step - 1], recv2.at[step - 1])
                        )
            elif phase == 2:
                for step in list(range(1, zs)) + [0]:
                    z = lax.rem(me["z"] + step, zs)
                    total = acc2[z]
                    for e in range(n2 - 1):
                        total = total + f32(recv2[e, z])
                    if step:
                        send3[step - 1] = total.astype(LINK)
                        copies.append(
                            send(number, 3, step, "z", send3.at[step - 1], recv3.at[step - 1])
                        )
                    else:
                        acc3[...] = total
            else:
                total = acc3[...]
                for e in range(zs - 1):
                    total = total + f32(recv3[e])
                out_ref[layer, span] = total
            waits[number] = copies

    def finish():
        for copy in pending:
            copy.wait_send()

    return advance, finish


def reduce_kernel(dims, grad_ref, out_ref, pair_buf, *scratch):
    me = place(dims)
    greet(dims, me)
    advance, finish = reduce_steps(dims, me, grad_ref, out_ref, pair_buf, scratch)
    for phase in range(5):
        for layer in reversed(range(out_ref.shape[0])):
            advance(layer, phase)
    finish()


def reduce_shards(dims, grad, collective_id):
    layers, _, _, _, _, rows, lanes = grad.shape
    return pl.pallas_call(
        functools.partial(reduce_kernel, dims),
        out_shape=jax.ShapeDtypeStruct((layers, rows, lanes), jnp.float32),
        in_specs=[pl.BlockSpec(memory_space=pltpu.VMEM)],
        out_specs=pl.BlockSpec(memory_space=pltpu.VMEM),
        scratch_shapes=reduce_scratch(dims, layers, rows),
        compiler_params=pltpu.CompilerParams(
            collective_id=collective_id, has_side_effects=True, vmem_limit_bytes=48 << 20
        ),
        name="reduce_shards",
    )(grad)


def dot(a, b, over=(1, 0)):
    return lax.dot_general(
        a, b, (((over[0],), (over[1],)), ((), ())), preferred_element_type=jnp.float32
    )


def compute_kernel(
    shape, count_ref, x_ref, cot_ref, wig_ref, rad_ref, src_ref, dst_ref, flat_ref, grad_ref,
    *scratch,
):
    rows_f = scratch[0]

    def unpack(layer):
        rows_f[...] = flat_ref[layer].astype(jnp.float32)

    def packed(layer, block):
        if block == 2:
            grad_ref[layer] = rows_f[...].astype(jnp.bfloat16)

    refs = (count_ref, x_ref, cot_ref, wig_ref, rad_ref, src_ref, dst_ref)
    skip = lambda *step: None
    compute(shape, refs, scratch, unpack, packed, skip, skip, skip)


def node_rows(nat, coef):
    return -(-nat * coef // 32) * 32


def compute(shape, refs, scratch, unpack, packed, gather, reduce, ready):
    count_ref, x_ref, cot_ref, wig_ref, rad_ref, src_ref, dst_ref = refs
    (
        rows_f, wzero, wreal, wimag, pick, put, scale, rotated, flat_a, mixed, node_t,
        outs, nodes, back, dnode, dmix,
    ) = scratch
    nat, coef, chan, rows, edges = shape
    lone = (rows + 2) // 3
    kzero, kone = lone * chan, (lone - 1) * chan
    used, tall = nat * coef, node_rows(nat, coef)
    bf16, f32 = jnp.bfloat16, jnp.float32
    eye = (
        lax.broadcasted_iota(jnp.int32, (chan, chan), 0)
        == lax.broadcasted_iota(jnp.int32, (chan, chan), 1)
    ).astype(f32).astype(bf16)

    def span(k, size):
        return slice(k * size, (k + 1) * size)

    def filled(value):
        value = value.reshape(used, chan)
        return jnp.concatenate([value, jnp.zeros((tall - used, chan), f32)], axis=0)

    def spread_wigner(hooks):
        atoms = lax.broadcasted_iota(jnp.int32, (nat, edges), 0)
        slots = lax.broadcasted_iota(jnp.int32, (nat, edges), 1)
        taken = (src_ref[...] == atoms).astype(f32)
        live = ((dst_ref[...] == atoms) & (slots < count_ref[0])).astype(f32)

        def write(first, coefs, at, size):
            values = [wig_ref[first + n].astype(f32) for n in range(coefs)]
            for k in range(rows):
                for ref, mask in ((pick, taken), (put, live)):
                    parts = [value[k : k + 1] * mask for value in values]
                    if size > coefs * nat:
                        parts.append(jnp.zeros((size - coefs * nat, edges), f32))
                    ref[pl.ds(at, size), span(k, edges)] = jnp.concatenate(
                        parts, axis=0
                    ).astype(bf16)

        pairs = coef // 2

        def one(p, carry):
            write(2 * p, 2, pl.multiple_of(p * 2 * nat, 2 * nat), 2 * nat)
            return carry

        parts = len(hooks) + 1
        for n in range(parts):
            lax.fori_loop(n * pairs // parts, (n + 1) * pairs // parts, one, 0)
            if n < len(hooks):
                hooks[n]()
        at = pairs * 2 * nat
        write(2 * pairs, coef - 2 * pairs, at, tall - at)

    def blocks():
        cut = kzero * kzero // LANES
        step = kone * kone // LANES
        return ((wzero, 0, kzero), (wreal, cut, kone), (wimag, cut + step, kone))

    def load_weights(layer):
        unpack(layer)
        for ref, start, size in blocks():
            per = size // LANES
            for c in range(per):
                ref[:, c * LANES : (c + 1) * LANES] = rows_f[
                    pl.ds(start + c, size, stride=per), :
                ].astype(bf16)

    def store_grads(layer, grads):
        for block, ((_, start, size), grad) in enumerate(zip(blocks(), grads)):
            per = size // LANES
            wide = 2 * LANES
            for n in range(0, size, wide):
                value = grad(n, min(n + wide, size))
                for c in range(value.shape[1] // LANES):
                    rows_f[pl.ds(start + n // LANES + c, size, stride=per), :] = value[
                        :, span(c, LANES)
                    ]
            packed(layer, block)

    def to_nodes(matrix, source):
        half = tall // 2
        return jnp.concatenate(
            [dot(matrix[span(n, half), :], source[...]) for n in range(2)], axis=0
        )[:used]

    def rotate(layer, hooks):
        node_t[...] = dot(eye, nodes[...], (1, 1)).astype(bf16)
        for k in range(rows):
            for n, hook in enumerate(hooks):
                if k == (n + 1) * rows // (len(hooks) + 1):
                    hook()
            value = dot(node_t[...], pick[:, span(k, edges)]) * scale[layer]
            value = value.astype(bf16)
            rotated[layer, span(k, chan)] = value
            flat_a[:, span(k, chan)] = value.T

    def forward(layer, last, hooks):
        gather(layer, 5)
        load_weights(layer)
        for hook in hooks[:1]:
            hook()
        azero = flat_a[:, :kzero]
        aplus = flat_a[:, kzero : kzero + kone]
        aminus = flat_a[:, kzero + kone :]

        def keep(first, value):
            for c in range(value.shape[1] // chan):
                mixed[span(first + c, edges)] = value[:, span(c, chan)].astype(bf16)

        wide = 2 * LANES
        for n in range(0, kzero, wide):
            keep(n // chan, dot(azero, wzero[:, n : min(n + wide, kzero)]))
        for n in range(0, kone, wide):
            real, imag = (w[:, n : min(n + wide, kone)] for w in (wreal, wimag))
            keep(lone + n // chan, dot(aplus, real) - dot(aminus, imag))
            keep(2 * lone - 1 + n // chan, dot(aplus, imag) + dot(aminus, real))
        for hook in hooks[1:]:
            hook()
        total = to_nodes(put, mixed)
        before = nodes[...].astype(f32)[:used]
        outs[layer] = before + total / AVG
        if last:
            return
        value = outs[layer].reshape(coef, nat, chan)
        gate = jax.nn.sigmoid(value[0])
        nodes[...] = filled(value * gate[None]).astype(bf16)

    def backward(layer, cot, last, hooks):
        value = outs[layer].reshape(coef, nat, chan)
        scalar = value[0]
        gate = jax.nn.sigmoid(scalar)
        slope = gate * (1.0 - gate)
        total = jnp.sum(cot[1:] * value[1:], axis=0)
        lead = cot[0] * (gate + scalar * slope) + total * slope
        dout = jnp.concatenate([lead[None], cot[1:] * gate[None]], axis=0)
        dnode[...] = dout.reshape(used, chan)
        share = filled(dout / AVG)
        high = share.astype(bf16)
        node_t[...] = dot(eye, high, (1, 1)).astype(bf16)
        for k in range(rows):
            dmix[span(k, chan)] = dot(node_t[...], put[:, span(k, edges)]).astype(bf16)
        dzero = dmix.at[:kzero]
        dplus = dmix.at[kzero : kzero + kone]
        dminus = dmix.at[kzero + kone :]
        azero = rotated[layer, :kzero]
        aplus = rotated[layer, kzero : kzero + kone]
        aminus = rotated[layer, kzero + kone :]
        for hook in hooks[:1]:
            hook()
        nt = (1, 1)
        store_grads(
            layer,
            (
                lambda a, b: dot(azero, dzero[a:b], nt),
                lambda a, b: dot(aplus, dplus[a:b], nt) + dot(aminus, dminus[a:b], nt),
                lambda a, b: dot(aplus, dminus[a:b], nt) - dot(aminus, dplus[a:b], nt),
            ),
        )
        if last:
            return

        def keep(first, value):
            for c in range(value.shape[0] // chan):
                part = value[span(c, chan)].astype(bf16).astype(f32) * scale[layer]
                mixed[span(first + c, edges)] = part.astype(bf16).T

        keep(0, dot(wzero[...], dzero[...]))
        keep(lone, dot(wreal[...], dplus[...]) + dot(wimag[...], dminus[...]))
        for hook in hooks[1:2]:
            hook()
        keep(2 * lone - 1, dot(wreal[...], dminus[...]) - dot(wimag[...], dplus[...]))
        total = to_nodes(pick, mixed)
        for hook in hooks[2:]:
            hook()
        back[...] = filled(dnode[...] + total).astype(bf16)

    def step(move, layer, phase):
        return lambda: move(layer, phase)

    def none():
        return None

    gather(0, 0)
    gather(0, 6)
    ready("next")
    ready("x")
    nodes[...] = filled(x_ref[...].astype(f32)).astype(bf16)
    ready("rad")
    for layer in range(rad_ref.shape[0]):
        scale[layer] = rad_ref[layer].astype(f32).T
    ready("wig")
    spread_wigner((none, step(gather, 0, 1)))
    gather(1, 0)
    gather(1, 6)
    rotate(0, (step(gather, 0, 2), ))
    gather(0, 3)
    gather(1, 1)
    gather(0, 4)
    forward(0, False, (step(gather, 1, 2), ))
    rotate(1, (step(gather, 1, 3), step(gather, 1, 4), ))
    forward(1, True, ())
    ready("cot")
    backward(1, cot_ref[...].astype(f32), False, (none, step(reduce, 1, 1)))
    last = back[...].astype(f32)[:used].reshape(coef, nat, chan)
    backward(0, last, True, ())
    for layer, phase in ((1, 2), (0, 1), (1, 3), (0, 2), (0, 3), (1, 4), (0, 4)):
        reduce(layer, phase)


def side(me):
    core = me["c"]
    return me["y"] * (1 - core) + me["x"] * core, me["x"] * (1 - core) + me["y"] * core


def spot(me, z, a, b):
    core = me["c"]
    return {"z": z, "y": a * (1 - core) + b * core, "c": core, "x": b * (1 - core) + a * core}


def flip(z, step):
    bit = 1
    while bit <= step:
        if step & bit:
            z = z + bit - 2 * bit * lax.rem(z // bit, 2)
        bit *= 2
    return z


def order_of(zs):
    return sorted(range(1, zs), key=lambda step: (step >= zs // 2, -step))


def remote(src, dst, send_sem, recv_sem, target):
    return pltpu.make_async_remote_copy(
        src_ref=src,
        dst_ref=dst,
        send_sem=send_sem,
        recv_sem=recv_sem,
        device_id=target,
        device_id_type=pl.DeviceIdType.MESH,
    )


def gather_slots(dims):
    return 4 * dims[0] + 3


def stream_gather(dims, me, full_ref, send_sem, recv_sem):
    zs = dims[0]
    a, b = side(me)
    near = order_of(zs)
    across = {layer: near[len(near) - count :] for layer, count in enumerate(ACROSS)}
    copies = {}

    def send(layer, slot, at, target):
        where = full_ref.at[(layer, at["z"], at["y"], at["c"], at["x"])]
        sems = (send_sem.at[layer, slot], recv_sem.at[layer, slot])
        copies[layer, slot] = remote(where, where, *sems, device(dims, target))
        copies[layer, slot].start()

    def by_z(layer, step):
        target = dict(me, z=flip(me["z"], step))
        send(layer, step - 1, me, target)

    def by_a(layer, step):
        z = flip(me["z"], step)
        send(layer, zs - 1 + step, spot(me, z, a, b), spot(me, me["z"], 1 - a, b))

    def by_b(layer, step, far):
        z = flip(me["z"], step)
        at = spot(me, z, 1 - a if far else a, b)
        send(layer, (3 if far else 2) * zs - 1 + step, at, spot(me, me["z"], a, 1 - b))

    def by_corner(layer, step):
        z = flip(me["z"], step)
        send(layer, 3 * zs - 1 + step, spot(me, z, a, b), spot(me, me["z"], 1 - a, 1 - b))

    def by_c(layer, number):
        at = spot(me, slice(None), 1 - a if number % 2 else a, 1 - b if number // 2 else b)
        send(layer, 4 * zs - 1 + number, at, dict(me, c=1 - me["c"]))

    def wait(layer, slot):
        copies[layer, slot].wait_recv()

    def advance(layer, phase):
        if phase == 0:
            for step in near:
                by_z(layer, step)
        elif phase == 6:
            by_a(layer, 0)
            by_b(layer, 0, False)
        elif phase == 1:
            for step in near:
                wait(layer, step - 1)
                by_a(layer, step)
                by_b(layer, step, False)
                if step in across[layer]:
                    by_corner(layer, step)
            wait(layer, zs - 1)
            by_b(layer, 0, True)
            by_c(layer, 0)
        elif phase == 2:
            for step in near:
                wait(layer, zs - 1 + step)
                if step not in across[layer]:
                    by_b(layer, step, True)
            by_c(layer, 1)
        elif phase == 3:
            for step in [0] + near:
                wait(layer, 2 * zs - 1 + step)
            by_c(layer, 2)
        elif phase == 4:
            for step in [0] + near:
                wait(layer, 3 * zs - 1 + step)
            by_c(layer, 3)
        else:
            for number in range(4):
                wait(layer, 4 * zs - 1 + number)

    def finish():
        for copy in copies.values():
            copy.wait_send()

    return advance, finish


def reduce_slots(dims):
    return 5 * dims[0] - 1


def stream_reduce(dims, me, grad_ref, store, buffers, send_sem, recv_sem):
    zs = dims[0]
    a, b = side(me)
    pair, send_b, recv_b, send_a, recv_a, send_z, recv_z, total = buffers
    steps = sorted(order_of(zs), reverse=True) + [0]
    copies = {}

    def send(key, layer, slot, src, dst, target):
        sems = (send_sem.at[layer, slot], recv_sem.at[layer, slot])
        copies[key] = remote(src, dst, *sems, device(dims, target))
        copies[key].start()

    def f32(value):
        return value.astype(jnp.float32)

    def depth(step):
        return flip(me["z"], step)

    def own(layer, z, a, b):
        at = spot(me, z, a, b)
        return f32(grad_ref[layer, z, at["y"], at["c"], at["x"]]) + f32(
            pair[layer, z, at["y"], at["x"]]
        )

    def exchange(layer, z):
        send(
            ("c", layer, z), layer, z, grad_ref.at[layer, z, :, 1 - me["c"]], pair.at[layer, z],
            dict(me, c=1 - me["c"]),
        )

    def advance(layer, phase):
        if phase == 1:
            for z in range(zs):
                copies["c", layer, z].wait_recv()
            for near in range(2):
                for step in steps:
                    value = own(layer, depth(step), a if near else 1 - a, 1 - b)
                    send_b[layer, step, near] = value.astype(LINK)
                    send(
                        ("b", layer, step, near), layer, zs + 2 * step + near,
                        send_b.at[layer, step, near], recv_b.at[layer, step, near],
                        spot(me, me["z"], a, 1 - b),
                    )
        elif phase == 2:
            for step in steps:
                copies["b", layer, step, 0].wait_recv()
                value = own(layer, depth(step), 1 - a, b) + f32(recv_b[layer, step, 0])
                send_a[layer, step] = value.astype(LINK)
                send(
                    ("a", layer, step), layer, 3 * zs + step, send_a.at[layer, step],
                    recv_a.at[layer, step], spot(me, me["z"], 1 - a, b),
                )
        elif phase == 3:
            for step in steps:
                copies["b", layer, step, 1].wait_recv()
                copies["a", layer, step].wait_recv()
                value = (
                    own(layer, depth(step), a, b)
                    + f32(recv_b[layer, step, 1])
                    + f32(recv_a[layer, step])
                )
                if step == 0:
                    total[layer] = value
                    continue
                send_z[layer, step - 1] = value.astype(LINK)
                send(
                    ("z", layer, step), layer, 4 * zs + step - 1, send_z.at[layer, step - 1],
                    recv_z.at[layer, step - 1], dict(me, z=depth(step)),
                )
        else:
            value = total[layer]
            for step in order_of(zs):
                copies["z", layer, step].wait_recv()
                value = value + f32(recv_z[layer, step - 1])
            store(layer, value)

    def finish():
        for copy in copies.values():
            copy.wait_send()

    return exchange, advance, finish


def fused_kernel(
    dims, shape, length, own_ref, count_ref, x_ref, cot_ref, wig_ref, rad_ref, src_ref, dst_ref,
    out_ref, par, x, cot, wig, rad, load_sem, full_ref, grad_ref, gather_send, gather_recv,
    reduce_send, reduce_recv, *scratch,
):
    zs, ys, xs = dims
    me = place(dims)
    loads = {}
    for number, (name, source, ref) in enumerate(
        (
            ("own", own_ref, par), ("x", x_ref, x), ("rad", rad_ref, rad), ("wig", wig_ref, wig),
            ("cot", cot_ref, cot),
        )
    ):
        loads[name] = pltpu.make_async_copy(source, ref, load_sem.at[number])

    def ready(name):
        if name == "next":
            for layer in range(1, layers):
                place_own(layer)
            return
        loads[name].wait()

    work, rest = scratch[:WORK], scratch[WORK:]
    rows_f = work[0]
    used, rows = length // LANES, full_ref.shape[-2]
    layers, tail = full_ref.shape[0], used % 8
    odd = me["x"] == 1
    wide = used + tail

    def store(layer, value):
        value = jnp.where(odd, value[tail:wide], value[:used])
        out_ref[pl.ds(layer, used, stride=layers), :] = value

    loads["own"].start()

    def meanwhile():
        for name, load in loads.items():
            if name != "own":
                load.start()
        ready("own")
        place_own(0)

    def place_own(layer):
        value = par[pl.ds(layer, used, stride=layers), :]
        low = jnp.zeros((tail, LANES), jnp.float32)
        high = jnp.zeros((rows - wide, LANES), jnp.float32)
        value = jnp.where(
            odd,
            jnp.concatenate([low, value, high], axis=0),
            jnp.concatenate([value, low, high], axis=0),
        )
        full_ref[layer, me["z"], me["y"], me["c"], me["x"]] = value.astype(jnp.bfloat16)

    greet(dims, me, meanwhile, True)
    gather, gathered = stream_gather(dims, me, full_ref, gather_send, gather_recv)
    exchange, reduce, reduced = stream_reduce(
        dims, me, grad_ref, store, rest, reduce_send, reduce_recv
    )

    def pairs():
        for number in range(zs * ys * 2):
            yield number, (number // (2 * ys), number // 2 % ys, number % 2)

    def unpack(layer):
        for number, at in pairs():
            even, uneven = (full_ref[(layer,) + at + (x,)].astype(jnp.float32) for x in range(2))
            first, cut = number * 2 * used, used - tail
            if tail:
                rows_f[first : first + cut, :] = even[:cut]
                rows_f[first + cut : first + cut + 8, :] = even[cut : cut + 8] + uneven[:8]
                rows_f[first + cut + 8 : first + 2 * used, :] = uneven[8:wide]
            else:
                rows_f[first : first + used, :] = even[:used]
                rows_f[first + used : first + 2 * used, :] = uneven[:used]

    ends = [0]
    for size, count in (((shape[3] + 2) // 3, 1), ((shape[3] + 2) // 3 - 1, 2)):
        for _ in range(count):
            ends.append(ends[-1] + (size * shape[2]) ** 2 // LANES)

    def packed(layer, block):
        for number, at in pairs():
            last = (number // (2 * ys) + 1) * (2 * ys) * 2 * used
            if not ends[block] < last <= ends[block + 1]:
                continue
            first = number * 2 * used
            for x, start in enumerate((first, first + used - tail)):
                grad_ref[(layer,) + at + (x,)] = rows_f[start : start + rows, :].astype(
                    jnp.bfloat16
                )
            if number % (2 * ys) == 2 * ys - 1:
                exchange(layer, at[0])

    refs = (count_ref, x, cot, wig, rad, src_ref, dst_ref)
    compute(shape, refs, work, unpack, packed, gather, reduce, ready)
    gathered()
    reduced()


def work_buffers(shape, flat_rows):
    nat, coef, chan, rows, edges = shape
    lone = (rows + 2) // 3
    kzero, kone = lone * chan, (lone - 1) * chan
    used, tall = nat * coef, node_rows(nat, coef)
    return [
        pltpu.VMEM((flat_rows, LANES), jnp.float32),
        pltpu.VMEM((kzero, kzero), jnp.bfloat16),
        pltpu.VMEM((kone, kone), jnp.bfloat16),
        pltpu.VMEM((kone, kone), jnp.bfloat16),
        pltpu.VMEM((tall, rows * edges), jnp.bfloat16),
        pltpu.VMEM((tall, rows * edges), jnp.bfloat16),
        pltpu.VMEM((2, chan, edges), jnp.float32),
        pltpu.VMEM((2, rows * chan, edges), jnp.bfloat16),
        pltpu.VMEM((edges, rows * chan), jnp.bfloat16),
        pltpu.VMEM((rows * edges, chan), jnp.bfloat16),
        pltpu.VMEM((chan, tall), jnp.bfloat16),
        pltpu.VMEM((2, used, chan), jnp.float32),
        pltpu.VMEM((tall, chan), jnp.bfloat16),
        pltpu.VMEM((tall, chan), jnp.bfloat16),
        pltpu.VMEM((used, chan), jnp.float32),
        pltpu.VMEM((rows * chan, edges), jnp.bfloat16),
    ]


def reduce_scratch(dims, layers, rows):
    zs, ys, xs = dims
    part = rows // PIECES
    most = max(zs, ys, xs, 2) - 1
    count = layers * PIECES
    slots = count * 4 * most
    even, odd = (count + 1) // 2, count // 2
    return (
        [pltpu.VMEM((count, zs, ys, xs, part, LANES), jnp.bfloat16)]
        + reduce_buffers(dims, (("x", "y", even), ("y", "x", odd)), part)
        + [pltpu.SemaphoreType.DMA((slots,)), pltpu.SemaphoreType.DMA((slots,))]
    )


def owned_grads(dims, own, length, inputs, shape, collective_id):
    zs, ys, xs = dims
    used = length // LANES
    layers = own.shape[0] // used
    rows = -(-(used + used % 8) // 16) * 16
    spread = (layers, zs, ys, 2, xs, rows, LANES)
    flat_rows = zs * ys * 2 * xs * used
    flat_rows = -(-(flat_rows + rows) // 8) * 8
    vmem = pl.BlockSpec(memory_space=pltpu.VMEM)
    hbm = pl.BlockSpec(memory_space=pl.ANY)
    item, link = (rows, LANES), jnp.bfloat16
    return pl.pallas_call(
        functools.partial(fused_kernel, dims, shape, length),
        out_shape=jax.ShapeDtypeStruct(own.shape, jnp.float32),
        in_specs=[hbm, pl.BlockSpec(memory_space=pltpu.SMEM)] + [hbm] * 4 + [vmem] * 2,
        out_specs=vmem,
        scratch_shapes=[
            pltpu.VMEM(own.shape, own.dtype),
            pltpu.VMEM(inputs[1].shape, inputs[1].dtype),
            pltpu.VMEM(inputs[2].shape, inputs[2].dtype),
            pltpu.VMEM(inputs[3].shape, inputs[3].dtype),
            pltpu.VMEM(inputs[4].shape, inputs[4].dtype),
            pltpu.SemaphoreType.DMA((5,)),
            pltpu.VMEM(spread, jnp.bfloat16),
            pltpu.VMEM(spread, jnp.bfloat16),
            pltpu.SemaphoreType.DMA((layers, gather_slots(dims))),
            pltpu.SemaphoreType.DMA((layers, gather_slots(dims))),
            pltpu.SemaphoreType.DMA((layers, reduce_slots(dims))),
            pltpu.SemaphoreType.DMA((layers, reduce_slots(dims))),
        ]
        + work_buffers(shape, flat_rows)
        + [
            pltpu.VMEM((layers, zs, ys, xs) + item, link),
            pltpu.VMEM((layers, zs, 2) + item, link),
            pltpu.VMEM((layers, zs, 2) + item, link),
            pltpu.VMEM((layers, zs) + item, link),
            pltpu.VMEM((layers, zs) + item, link),
            pltpu.VMEM((layers, zs - 1) + item, link),
            pltpu.VMEM((layers, zs - 1) + item, link),
            pltpu.VMEM((layers,) + item, jnp.float32),
        ],
        compiler_params=pltpu.CompilerParams(
            collective_id=collective_id, has_side_effects=True, vmem_limit_bytes=60 << 20
        ),
        name="owned_grads",
    )(own, *inputs)


def device_grads(inputs, flat, shape):
    vmem = pl.BlockSpec(memory_space=pltpu.VMEM)
    return pl.pallas_call(
        functools.partial(compute_kernel, shape),
        out_shape=jax.ShapeDtypeStruct(flat.shape, jnp.bfloat16),
        in_specs=[pl.BlockSpec(memory_space=pltpu.SMEM)] + [vmem] * 7,
        out_specs=vmem,
        scratch_shapes=work_buffers(shape, flat.shape[1]),
        compiler_params=pltpu.CompilerParams(vmem_limit_bytes=56 << 20),
        name="device_grads",
    )(*inputs, flat)


def woven(rows):
    return with_layout_constraint(rows, Layout(major_to_minor=(1, 0, 2)))


def local(
    dims, node_feats, cotangent, wigner, radial, edge_src, edge_dst, edge_count, params, moment1,
    moment2,
):
    nat, coef, chan = node_feats.shape
    layers, length = params.shape
    zs, ys, xs = dims
    shards = zs * ys * 2 * xs
    edges = edge_src.shape[0]
    shape = (nat, coef, chan, wigner.shape[0], edges)

    inputs = (
        edge_count,
        jnp.transpose(node_feats, (1, 0, 2)),
        jnp.transpose(cotangent, (1, 0, 2)),
        jnp.transpose(wigner, (1, 0, 2)),
        radial,
        edge_src[None, :],
        edge_dst[None, :],
    )
    if length % (4 * LANES) == 0 and ys == 2 and xs == 2 and zs > 1 and zs & (zs - 1) == 0:
        used = length // LANES
        own = woven(params.reshape(layers, used, LANES))
        own = jnp.transpose(own, (1, 0, 2)).reshape(used * layers, LANES)
        owned = owned_grads(dims, own, length, inputs, shape, 0)
        grad = woven(jnp.transpose(owned.reshape(used, layers, LANES), (1, 0, 2)))
        grad = grad.reshape(layers, length)
    else:
        block = LANES * 16 * PIECES
        padded = -(-length // block) * block
        rows = padded // LANES
        own = jnp.pad(params.astype(jnp.bfloat16), ((0, 0), (0, padded - length)))
        full = gather_shards(dims, own.reshape(layers, rows, LANES), 0)
        full = full.reshape(layers, shards, padded)[:, :, :length]
        full = full.reshape(layers, shards * length // LANES, LANES)
        grad = device_grads(inputs, full, shape).reshape(layers, shards, length)
        grad = jnp.pad(grad, ((0, 0), (0, 0), (0, padded - length)))
        owned = reduce_shards(dims, grad.reshape(layers, zs, ys, 2, xs, rows, LANES), 1)
        grad = owned.reshape(layers, padded)[:, :length]
    new_moment1 = 0.9 * moment1 + 0.1 * grad
    new_moment2 = 0.95 * moment2 + 0.05 * grad * grad
    m_hat = new_moment1 / (1.0 - 0.9**60)
    v_hat = new_moment2 / (1.0 - 0.95**60)
    new_params = params - 0.01 * (m_hat / (jnp.sqrt(v_hat) + 1e-08) + 0.1 * params)
    return (new_params, new_moment1, new_moment2)


def solution(mesh):
    both = ("dp", "node")
    return jax.shard_map(
        functools.partial(local, split_axes(mesh)),
        mesh=mesh,
        in_specs=(
            P(both, None, None),
            P(both, None, None),
            P(None, None, both),
            P(None, both, None),
            P(both),
            P(both),
            P(both),
            P(None, both),
            P(None, both),
            P(None, both),
        ),
        out_specs=(P(None, both), P(None, both), P(None, both)),
        check_vma=False,
    )
```

```python
import functools

import jax
import jax.numpy as jnp
from jax import lax
from jax.experimental import pallas as pl
from jax.experimental.layout import Layout, with_layout_constraint
from jax.experimental.pallas import tpu as pltpu
from jax.sharding import PartitionSpec as P

AVG = 10
LANES = 128
PIECES = 3
LINK = jnp.bfloat16
WORK = 16
ACROSS = (1, 1)


def split_axes(mesh):
    rest = mesh.shape["dp"] // 2
    y = 1
    while y * y * 4 <= rest and rest % (y * 2) == 0:
        y *= 2
    return rest // y, y, mesh.shape["node"]


def place(dims):
    zs, ys, xs = dims
    dp = lax.axis_index("dp")
    x = lax.axis_index("node")
    core = lax.rem(dp, 2)
    y = lax.rem(dp // 2, ys)
    z = dp // (2 * ys)
    return {"z": z, "y": y, "c": core, "x": x}


def device(dims, at):
    return {"dp": (at["z"] * dims[1] + at["y"]) * 2 + at["c"], "node": at["x"]}


def peer_of(dims, me, axis, step):
    size = {"z": dims[0], "y": dims[1], "c": 2, "x": dims[2]}[axis]
    other = dict(me)
    other[axis] = lax.rem(me[axis] + step, size)
    return other


def size_of(dims, axis):
    return {"z": dims[0], "y": dims[1], "c": 2, "x": dims[2]}[axis]


def greet(dims, me, meanwhile=lambda: None, corner=False):
    barrier = pltpu.get_barrier_semaphore()
    count = 0
    if corner:
        pl.semaphore_signal(
            barrier,
            inc=1,
            device_id=device(dims, dict(me, x=1 - me["x"], y=1 - me["y"])),
            device_id_type=pl.DeviceIdType.MESH,
        )
        count += 1
    for axis in "zyxc":
        for step in range(1, size_of(dims, axis)):
            pl.semaphore_signal(
                barrier,
                inc=1,
                device_id=device(dims, peer_of(dims, me, axis, step)),
                device_id_type=pl.DeviceIdType.MESH,
            )
            count += 1
    meanwhile()
    pl.semaphore_wait(barrier, count)


def gather_steps(dims, me, own_ref, out_ref, local_sem, send_sem, recv_sem):
    layers, rows = own_ref.shape[0], own_ref.shape[1]
    part = rows // PIECES
    mine = pltpu.make_async_copy(
        own_ref, out_ref.at[:, me["z"], me["y"], me["c"], me["x"]], local_sem
    )
    mine.start()
    most = max(size_of(dims, a) for a in "zyxc") - 1
    started = {}
    state = {"mine": True}

    def view(ref, layer, piece, spans, at):
        index = [layer]
        for axis in "zycx":
            index.append(slice(None) if axis in spans else at[axis])
        index.append(pl.ds(piece * part, part))
        return ref.at[tuple(index)]

    def advance(layer, phase):
        for piece in range(PIECES):
            number = layer * PIECES + piece
            order = "zyxc" if number % 2 == 0 else "zxyc"
            if phase:
                for copy in started[number, phase - 1]:
                    copy.wait_recv()
                if state["mine"]:
                    mine.wait()
                    state["mine"] = False
            if phase == 4:
                continue
            axis, spans = order[phase], order[:phase]
            copies = []
            for step in range(1, size_of(dims, axis)):
                if phase == 0:
                    src = own_ref.at[layer, pl.ds(piece * part, part)]
                else:
                    src = view(out_ref, layer, piece, spans, me)
                slot = (number * 4 + phase) * most + step - 1
                copy = pltpu.make_async_remote_copy(
                    src_ref=src,
                    dst_ref=view(out_ref, layer, piece, spans, me),
                    send_sem=send_sem.at[slot],
                    recv_sem=recv_sem.at[slot],
                    device_id=device(dims, peer_of(dims, me, axis, step)),
                    device_id_type=pl.DeviceIdType.MESH,
                )
                copy.start()
                copies.append(copy)
            started[number, phase] = copies

    def finish():
        for copies in started.values():
            for copy in copies:
                copy.wait_send()

    return advance, finish


def gather_kernel(dims, own_ref, out_ref, local_sem, send_sem, recv_sem):
    me = place(dims)
    greet(dims, me)
    advance, finish = gather_steps(dims, me, own_ref, out_ref, local_sem, send_sem, recv_sem)
    for phase in range(5):
        for layer in range(own_ref.shape[0]):
            advance(layer, phase)
    finish()


def gather_shards(dims, own, collective_id):
    layers, rows, lanes = own.shape
    zs, ys, xs = dims
    most = max(zs, ys, xs, 2) - 1
    slots = layers * PIECES * 4 * most
    return pl.pallas_call(
        functools.partial(gather_kernel, dims),
        out_shape=jax.ShapeDtypeStruct((layers, zs, ys, 2, xs, rows, lanes), own.dtype),
        in_specs=[pl.BlockSpec(memory_space=pltpu.VMEM)],
        out_specs=pl.BlockSpec(memory_space=pltpu.VMEM),
        scratch_shapes=[
            pltpu.SemaphoreType.DMA,
            pltpu.SemaphoreType.DMA((slots,)),
            pltpu.SemaphoreType.DMA((slots,)),
        ],
        compiler_params=pltpu.CompilerParams(
            collective_id=collective_id, has_side_effects=True, vmem_limit_bytes=48 << 20
        ),
        name="gather_shards",
    )(own)


def reduce_buffers(dims, pairs, part):
    zs = dims[0]
    buffers = []
    for first, second, count in pairs:
        n1, n2 = size_of(dims, first), size_of(dims, second)
        buffers += [
            pltpu.VMEM((count, zs, n2, part, LANES), jnp.float32),
            pltpu.VMEM((count, n1 - 1, zs, n2, part, LANES), LINK),
            pltpu.VMEM((count, n1 - 1, zs, n2, part, LANES), LINK),
            pltpu.VMEM((count, zs, part, LANES), jnp.float32),
            pltpu.VMEM((count, n2 - 1, zs, part, LANES), LINK),
            pltpu.VMEM((count, n2 - 1, zs, part, LANES), LINK),
            pltpu.VMEM((count, part, LANES), jnp.float32),
            pltpu.VMEM((count, zs - 1, part, LANES), LINK),
            pltpu.VMEM((count, zs - 1, part, LANES), LINK),
        ]
    return buffers


def reduce_items(layers):
    items = []
    for layer in reversed(range(layers)):
        for piece in range(PIECES):
            number = len(items)
            items.append((layer, piece, number % 2, number // 2))
    return items


def reduce_steps(dims, me, grad_ref, out_ref, pair_buf, scratch):
    zs = dims[0]
    buffers = (scratch[:9], scratch[9:18])
    send_sem, recv_sem = scratch[18:20]
    layers, rows = out_ref.shape[0], out_ref.shape[1]
    part = rows // PIECES
    items = reduce_items(layers)
    most = max(size_of(dims, a) for a in "zyxc") - 1
    pending = []

    def send(number, phase, step, axis, src, dst):
        slot = (number * 4 + phase) * most + step - 1
        copy = pltpu.make_async_remote_copy(
            src_ref=src,
            dst_ref=dst,
            send_sem=send_sem.at[slot],
            recv_sem=recv_sem.at[slot],
            device_id=device(dims, peer_of(dims, me, axis, step)),
            device_id_type=pl.DeviceIdType.MESH,
        )
        copy.start()
        pending.append(copy)
        return copy

    def f32(value):
        return value.astype(jnp.float32)

    waits = {}

    def advance(wanted, now):
        phase = now - 1
        for number, (layer, piece, kind, place_in) in enumerate(items):
            if layer != wanted:
                continue
            if now == 0:
                waits[number] = [
                    send(
                        number, 0, 1, "c",
                        grad_ref.at[layer, :, :, 1 - me["c"], :, pl.ds(piece * part, part)],
                        pair_buf.at[number],
                    )
                ]
                continue
            span = pl.ds(piece * part, part)
            acc1, send1, recv1, acc2, send2, recv2, acc3, send3, recv3 = (
                buf.at[place_in] for buf in buffers[kind]
            )
            first, second = ("x", "y") if kind == 0 else ("y", "x")
            n1, n2 = size_of(dims, first), size_of(dims, second)
            for copy in waits[number]:
                copy.wait_recv()
            copies = []
            if phase == 0:
                for step in list(range(1, n1)) + [0]:
                    k1 = lax.rem(me[first] + step, n1)

                    def one(i, carry, step=step, k1=k1):
                        z, k2 = i // n2, lax.rem(i, n2)
                        y, x = (k2, k1) if kind == 0 else (k1, k2)
                        total = f32(grad_ref[layer, z, y, me["c"], x, span]) + f32(
                            pair_buf[number, z, y, x]
                        )
                        if step:
                            send1[step - 1, z, k2] = total.astype(LINK)
                        else:
                            acc1[z, k2] = total
                        return carry

                    lax.fori_loop(0, zs * n2, one, 0)
                    if step:
                        copies.append(
                            send(number, 1, step, first, send1.at[step - 1], recv1.at[step - 1])
                        )
            elif phase == 1:
                for step in list(range(1, n2)) + [0]:
                    k2 = lax.rem(me[second] + step, n2)

                    def one(z, carry, step=step, k2=k2):
                        total = acc1[z, k2]
                        for e in range(n1 - 1):
                            total = total + f32(recv1[e, z, k2])
                        if step:
                            send2[step - 1, z] = total.astype(LINK)
                        else:
                            acc2[z] = total
                        return carry

                    lax.fori_loop(0, zs, one, 0)
                    if step:
                        copies.append(
                            send(number, 2, step, second, send2.at[step - 1], recv2.at[step - 1])
                        )
            elif phase == 2:
                for step in list(range(1, zs)) + [0]:
                    z = lax.rem(me["z"] + step, zs)
                    total = acc2[z]
                    for e in range(n2 - 1):
                        total = total + f32(recv2[e, z])
                    if step:
                        send3[step - 1] = total.astype(LINK)
                        copies.append(
                            send(number, 3, step, "z", send3.at[step - 1], recv3.at[step - 1])
                        )
                    else:
                        acc3[...] = total
            else:
                total = acc3[...]
                for e in range(zs - 1):
                    total = total + f32(recv3[e])
                out_ref[layer, span] = total
            waits[number] = copies

    def finish():
        for copy in pending:
            copy.wait_send()

    return advance, finish


def reduce_kernel(dims, grad_ref, out_ref, pair_buf, *scratch):
    me = place(dims)
    greet(dims, me)
    advance, finish = reduce_steps(dims, me, grad_ref, out_ref, pair_buf, scratch)
    for phase in range(5):
        for layer in reversed(range(out_ref.shape[0])):
            advance(layer, phase)
    finish()


def reduce_shards(dims, grad, collective_id):
    layers, _, _, _, _, rows, lanes = grad.shape
    return pl.pallas_call(
        functools.partial(reduce_kernel, dims),
        out_shape=jax.ShapeDtypeStruct((layers, rows, lanes), jnp.float32),
        in_specs=[pl.BlockSpec(memory_space=pltpu.VMEM)],
        out_specs=pl.BlockSpec(memory_space=pltpu.VMEM),
        scratch_shapes=reduce_scratch(dims, layers, rows),
        compiler_params=pltpu.CompilerParams(
            collective_id=collective_id, has_side_effects=True, vmem_limit_bytes=48 << 20
        ),
        name="reduce_shards",
    )(grad)


def dot(a, b, over=(1, 0)):
    return lax.dot_general(
        a, b, (((over[0],), (over[1],)), ((), ())), preferred_element_type=jnp.float32
    )


def compute_kernel(
    shape, count_ref, x_ref, cot_ref, wig_ref, rad_ref, src_ref, dst_ref, flat_ref, grad_ref,
    *scratch,
):
    rows_f = scratch[0]

    def unpack(layer):
        rows_f[...] = flat_ref[layer].astype(jnp.float32)

    def packed(layer, block):
        if block == 2:
            grad_ref[layer] = rows_f[...].astype(jnp.bfloat16)

    refs = (count_ref, x_ref, cot_ref, wig_ref, rad_ref, src_ref, dst_ref)
    skip = lambda *step: None
    compute(shape, refs, scratch, unpack, packed, skip, skip, skip)


def node_rows(nat, coef):
    return -(-nat * coef // 32) * 32


def compute(shape, refs, scratch, unpack, packed, gather, reduce, ready):
    count_ref, x_ref, cot_ref, wig_ref, rad_ref, src_ref, dst_ref = refs
    (
        rows_f, wzero, wreal, wimag, pick, put, scale, rotated, flat_a, mixed, node_t,
        outs, nodes, back, dnode, dmix,
    ) = scratch
    nat, coef, chan, rows, edges = shape
    lone = (rows + 2) // 3
    kzero, kone = lone * chan, (lone - 1) * chan
    used, tall = nat * coef, node_rows(nat, coef)
    bf16, f32 = jnp.bfloat16, jnp.float32
    eye = (
        lax.broadcasted_iota(jnp.int32, (chan, chan), 0)
        == lax.broadcasted_iota(jnp.int32, (chan, chan), 1)
    ).astype(f32).astype(bf16)

    def span(k, size):
        return slice(k * size, (k + 1) * size)

    def filled(value):
        value = value.reshape(used, chan)
        return jnp.concatenate([value, jnp.zeros((tall - used, chan), f32)], axis=0)

    def spread_wigner(hooks):
        atoms = lax.broadcasted_iota(jnp.int32, (nat, edges), 0)
        slots = lax.broadcasted_iota(jnp.int32, (nat, edges), 1)
        taken = (src_ref[...] == atoms).astype(f32)
        live = ((dst_ref[...] == atoms) & (slots < count_ref[0])).astype(f32)

        def write(first, coefs, at, size):
            values = [wig_ref[first + n].astype(f32) for n in range(coefs)]
            for k in range(rows):
                for ref, mask in ((pick, taken), (put, live)):
                    parts = [value[k : k + 1] * mask for value in values]
                    if size > coefs * nat:
                        parts.append(jnp.zeros((size - coefs * nat, edges), f32))
                    ref[pl.ds(at, size), span(k, edges)] = jnp.concatenate(
                        parts, axis=0
                    ).astype(bf16)

        pairs = coef // 2

        def one(p, carry):
            write(2 * p, 2, pl.multiple_of(p * 2 * nat, 2 * nat), 2 * nat)
            return carry

        parts = len(hooks) + 1
        for n in range(parts):
            lax.fori_loop(n * pairs // parts, (n + 1) * pairs // parts, one, 0)
            if n < len(hooks):
                hooks[n]()
        at = pairs * 2 * nat
        write(2 * pairs, coef - 2 * pairs, at, tall - at)

    def blocks():
        cut = kzero * kzero // LANES
        step = kone * kone // LANES
        return ((wzero, 0, kzero), (wreal, cut, kone), (wimag, cut + step, kone))

    def load_weights(layer):
        unpack(layer)
        for ref, start, size in blocks():
            per = size // LANES
            for c in range(per):
                ref[:, c * LANES : (c + 1) * LANES] = rows_f[
                    pl.ds(start + c, size, stride=per), :
                ].astype(bf16)

    def store_grads(layer, grads):
        for block, ((_, start, size), grad) in enumerate(zip(blocks(), grads)):
            per = size // LANES
            wide = 2 * LANES
            for n in range(0, size, wide):
                value = grad(n, min(n + wide, size))
                for c in range(value.shape[1] // LANES):
                    rows_f[pl.ds(start + n // LANES + c, size, stride=per), :] = value[
                        :, span(c, LANES)
                    ]
            packed(layer, block)

    def to_nodes(matrix, source):
        half = tall // 2
        return jnp.concatenate(
            [dot(matrix[span(n, half), :], source[...]) for n in range(2)], axis=0
        )[:used]

    def rotate(layer, hooks):
        node_t[...] = dot(eye, nodes[...], (1, 1)).astype(bf16)
        for k in range(rows):
            for n, hook in enumerate(hooks):
                if k == (n + 1) * rows // (len(hooks) + 1):
                    hook()
            value = dot(node_t[...], pick[:, span(k, edges)]) * scale[layer]
            value = value.astype(bf16)
            rotated[layer, span(k, chan)] = value
            flat_a[:, span(k, chan)] = value.T

    def forward(layer, last, hooks):
        load_weights(layer)
        for hook in hooks[:1]:
            hook()
        azero = flat_a[:, :kzero]
        aplus = flat_a[:, kzero : kzero + kone]
        aminus = flat_a[:, kzero + kone :]

        def keep(first, value):
            for c in range(value.shape[1] // chan):
                mixed[span(first + c, edges)] = value[:, span(c, chan)].astype(bf16)

        wide = 2 * LANES
        for n in range(0, kzero, wide):
            keep(n // chan, dot(azero, wzero[:, n : min(n + wide, kzero)]))
        for n in range(0, kone, wide):
            real, imag = (w[:, n : min(n + wide, kone)] for w in (wreal, wimag))
            keep(lone + n // chan, dot(aplus, real) - dot(aminus, imag))
            keep(2 * lone - 1 + n // chan, dot(aplus, imag) + dot(aminus, real))
        for hook in hooks[1:]:
            hook()
        total = to_nodes(put, mixed)
        before = nodes[...].astype(f32)[:used]
        outs[layer] = before + total / AVG
        if last:
            return
        value = outs[layer].reshape(coef, nat, chan)
        gate = jax.nn.sigmoid(value[0])
        nodes[...] = filled(value * gate[None]).astype(bf16)

    def backward(layer, cot, last, hooks):
        value = outs[layer].reshape(coef, nat, chan)
        scalar = value[0]
        gate = jax.nn.sigmoid(scalar)
        slope = gate * (1.0 - gate)
        total = jnp.sum(cot[1:] * value[1:], axis=0)
        lead = cot[0] * (gate + scalar * slope) + total * slope
        dout = jnp.concatenate([lead[None], cot[1:] * gate[None]], axis=0)
        dnode[...] = dout.reshape(used, chan)
        share = filled(dout / AVG)
        high = share.astype(bf16)
        node_t[...] = dot(eye, high, (1, 1)).astype(bf16)
        for k in range(rows):
            dmix[span(k, chan)] = dot(node_t[...], put[:, span(k, edges)]).astype(bf16)
        dzero = dmix.at[:kzero]
        dplus = dmix.at[kzero : kzero + kone]
        dminus = dmix.at[kzero + kone :]
        azero = rotated[layer, :kzero]
        aplus = rotated[layer, kzero : kzero + kone]
        aminus = rotated[layer, kzero + kone :]
        for hook in hooks[:1]:
            hook()
        nt = (1, 1)
        store_grads(
            layer,
            (
                lambda a, b: dot(azero, dzero[a:b], nt),
                lambda a, b: dot(aplus, dplus[a:b], nt) + dot(aminus, dminus[a:b], nt),
                lambda a, b: dot(aplus, dminus[a:b], nt) - dot(aminus, dplus[a:b], nt),
            ),
        )
        if last:
            return

        def keep(first, value):
            for c in range(value.shape[0] // chan):
                part = value[span(c, chan)].astype(bf16).astype(f32) * scale[layer]
                mixed[span(first + c, edges)] = part.astype(bf16).T

        keep(0, dot(wzero[...], dzero[...]))
        keep(lone, dot(wreal[...], dplus[...]) + dot(wimag[...], dminus[...]))
        for hook in hooks[1:2]:
            hook()
        keep(2 * lone - 1, dot(wreal[...], dminus[...]) - dot(wimag[...], dplus[...]))
        total = to_nodes(pick, mixed)
        for hook in hooks[2:]:
            hook()
        back[...] = filled(dnode[...] + total).astype(bf16)

    def step(move, layer, phase):
        return lambda: move(layer, phase)

    def none():
        return None

    gather(0, 0)
    gather(0, 6)
    ready("next")
    ready("x")
    nodes[...] = filled(x_ref[...].astype(f32)).astype(bf16)
    ready("rad")
    for layer in range(rad_ref.shape[0]):
        scale[layer] = rad_ref[layer].astype(f32).T
    ready("wig")
    spread_wigner((none, step(gather, 0, 1)))
    gather(1, 0)
    gather(1, 6)
    rotate(0, (step(gather, 0, 2), ))
    gather(0, 3)
    gather(1, 1)
    gather(0, 4)
    forward(0, False, (step(gather, 1, 2), ))
    rotate(1, (step(gather, 1, 3), step(gather, 1, 4), ))
    forward(1, True, ())
    ready("cot")
    backward(1, cot_ref[...].astype(f32), False, (none, step(reduce, 1, 1)))
    last = back[...].astype(f32)[:used].reshape(coef, nat, chan)
    backward(0, last, True, ())
    for layer, phase in ((1, 2), (0, 1), (1, 3), (0, 2), (0, 3), (1, 4), (0, 4)):
        reduce(layer, phase)


def side(me):
    core = me["c"]
    return me["y"] * (1 - core) + me["x"] * core, me["x"] * (1 - core) + me["y"] * core


def spot(me, z, a, b):
    core = me["c"]
    return {"z": z, "y": a * (1 - core) + b * core, "c": core, "x": b * (1 - core) + a * core}


def flip(z, step):
    bit = 1
    while bit <= step:
        if step & bit:
            z = z + bit - 2 * bit * lax.rem(z // bit, 2)
        bit *= 2
    return z


def order_of(zs):
    return sorted(range(1, zs), key=lambda step: (step >= zs // 2, -step))


def remote(src, dst, send_sem, recv_sem, target):
    return pltpu.make_async_remote_copy(
        src_ref=src,
        dst_ref=dst,
        send_sem=send_sem,
        recv_sem=recv_sem,
        device_id=target,
        device_id_type=pl.DeviceIdType.MESH,
    )


def gather_slots(dims):
    return 4 * dims[0] + 3


def stream_gather(dims, me, full_ref, send_sem, recv_sem):
    zs = dims[0]
    a, b = side(me)
    near = order_of(zs)
    across = {layer: near[len(near) - count :] for layer, count in enumerate(ACROSS)}
    copies = {}

    def send(layer, slot, at, target):
        where = full_ref.at[(layer, at["z"], at["y"], at["c"], at["x"])]
        sems = (send_sem.at[layer, slot], recv_sem.at[layer, slot])
        copies[layer, slot] = remote(where, where, *sems, device(dims, target))
        copies[layer, slot].start()

    def by_z(layer, step):
        target = dict(me, z=flip(me["z"], step))
        send(layer, step - 1, me, target)

    def by_a(layer, step):
        z = flip(me["z"], step)
        send(layer, zs - 1 + step, spot(me, z, a, b), spot(me, me["z"], 1 - a, b))

    def by_b(layer, step, far):
        z = flip(me["z"], step)
        at = spot(me, z, 1 - a if far else a, b)
        send(layer, (3 if far else 2) * zs - 1 + step, at, spot(me, me["z"], a, 1 - b))

    def by_corner(layer, step):
        z = flip(me["z"], step)
        send(layer, 3 * zs - 1 + step, spot(me, z, a, b), spot(me, me["z"], 1 - a, 1 - b))

    def by_c(layer, number):
        at = spot(me, slice(None), 1 - a if number % 2 else a, 1 - b if number // 2 else b)
        send(layer, 4 * zs - 1 + number, at, dict(me, c=1 - me["c"]))

    def wait(layer, slot):
        copies[layer, slot].wait_recv()

    def advance(layer, phase):
        if phase == 0:
            for step in near:
                by_z(layer, step)
        elif phase == 6:
            by_a(layer, 0)
            by_b(layer, 0, False)
        elif phase == 1:
            for step in near:
                wait(layer, step - 1)
                by_a(layer, step)
                by_b(layer, step, False)
                if step in across[layer]:
                    by_corner(layer, step)
            wait(layer, zs - 1)
            by_b(layer, 0, True)
            by_c(layer, 0)
        elif phase == 2:
            for step in near:
                wait(layer, zs - 1 + step)
                if step not in across[layer]:
                    by_b(layer, step, True)
            by_c(layer, 1)
        elif phase == 3:
            for step in [0] + near:
                wait(layer, 2 * zs - 1 + step)
            by_c(layer, 2)
        elif phase == 4:
            for step in [0] + near:
                wait(layer, 3 * zs - 1 + step)
            by_c(layer, 3)
        else:
            for number in range(4):
                wait(layer, 4 * zs - 1 + number)

    def finish():
        for copy in copies.values():
            copy.wait_send()

    return advance, finish


def reduce_slots(dims):
    return 5 * dims[0] - 1


def stream_reduce(dims, me, grad_ref, store, buffers, send_sem, recv_sem):
    zs = dims[0]
    a, b = side(me)
    pair, send_b, recv_b, send_a, recv_a, send_z, recv_z, total = buffers
    steps = sorted(order_of(zs), reverse=True) + [0]
    copies = {}

    def send(key, layer, slot, src, dst, target):
        sems = (send_sem.at[layer, slot], recv_sem.at[layer, slot])
        copies[key] = remote(src, dst, *sems, device(dims, target))
        copies[key].start()

    def f32(value):
        return value.astype(jnp.float32)

    def depth(step):
        return flip(me["z"], step)

    def own(layer, z, a, b):
        at = spot(me, z, a, b)
        return f32(grad_ref[layer, z, at["y"], at["c"], at["x"]]) + f32(
            pair[layer, z, at["y"], at["x"]]
        )

    def exchange(layer, z):
        send(
            ("c", layer, z), layer, z, grad_ref.at[layer, z, :, 1 - me["c"]], pair.at[layer, z],
            dict(me, c=1 - me["c"]),
        )

    def advance(layer, phase):
        if phase == 1:
            for z in range(zs):
                copies["c", layer, z].wait_recv()
            for near in range(2):
                for step in steps:
                    value = own(layer, depth(step), a if near else 1 - a, 1 - b)
                    send_b[layer, step, near] = value.astype(LINK)
                    send(
                        ("b", layer, step, near), layer, zs + 2 * step + near,
                        send_b.at[layer, step, near], recv_b.at[layer, step, near],
                        spot(me, me["z"], a, 1 - b),
                    )
        elif phase == 2:
            for step in steps:
                copies["b", layer, step, 0].wait_recv()
                value = own(layer, depth(step), 1 - a, b) + f32(recv_b[layer, step, 0])
                send_a[layer, step] = value.astype(LINK)
                send(
                    ("a", layer, step), layer, 3 * zs + step, send_a.at[layer, step],
                    recv_a.at[layer, step], spot(me, me["z"], 1 - a, b),
                )
        elif phase == 3:
            for step in steps:
                copies["b", layer, step, 1].wait_recv()
                copies["a", layer, step].wait_recv()
                value = (
                    own(layer, depth(step), a, b)
                    + f32(recv_b[layer, step, 1])
                    + f32(recv_a[layer, step])
                )
                if step == 0:
                    total[layer] = value
                    continue
                send_z[layer, step - 1] = value.astype(LINK)
                send(
                    ("z", layer, step), layer, 4 * zs + step - 1, send_z.at[layer, step - 1],
                    recv_z.at[layer, step - 1], dict(me, z=depth(step)),
                )
        else:
            value = total[layer]
            for step in order_of(zs):
                copies["z", layer, step].wait_recv()
                value = value + f32(recv_z[layer, step - 1])
            store(layer, value)

    def finish():
        for copy in copies.values():
            copy.wait_send()

    return exchange, advance, finish


def fused_kernel(
    dims, shape, length, own_ref, count_ref, x_ref, cot_ref, wig_ref, rad_ref, src_ref, dst_ref,
    out_ref, par, x, cot, wig, rad, load_sem, full_ref, grad_ref, gather_send, gather_recv,
    reduce_send, reduce_recv, *scratch,
):
    zs, ys, xs = dims
    me = place(dims)
    loads = {}
    for number, (name, source, ref) in enumerate(
        (
            ("own", own_ref, par), ("x", x_ref, x), ("rad", rad_ref, rad), ("wig", wig_ref, wig),
            ("cot", cot_ref, cot),
        )
    ):
        loads[name] = pltpu.make_async_copy(source, ref, load_sem.at[number])

    def ready(name):
        if name == "next":
            for layer in range(1, layers):
                place_own(layer)
            return
        loads[name].wait()

    work, rest = scratch[:WORK], scratch[WORK:]
    rows_f = work[0]
    used, rows = length // LANES, full_ref.shape[-2]
    layers, tail = full_ref.shape[0], used % 8
    odd = me["x"] == 1
    wide = used + tail

    def store(layer, value):
        value = jnp.where(odd, value[tail:wide], value[:used])
        out_ref[pl.ds(layer, used, stride=layers), :] = value

    loads["own"].start()

    def meanwhile():
        for name, load in loads.items():
            if name != "own":
                load.start()
        ready("own")
        place_own(0)

    def place_own(layer):
        value = par[pl.ds(layer, used, stride=layers), :]
        low = jnp.zeros((tail, LANES), jnp.float32)
        high = jnp.zeros((rows - wide, LANES), jnp.float32)
        value = jnp.where(
            odd,
            jnp.concatenate([low, value, high], axis=0),
            jnp.concatenate([value, low, high], axis=0),
        )
        full_ref[layer, me["z"], me["y"], me["c"], me["x"]] = value.astype(jnp.bfloat16)

    greet(dims, me, meanwhile, True)
    gather, gathered = stream_gather(dims, me, full_ref, gather_send, gather_recv)
    exchange, reduce, reduced = stream_reduce(
        dims, me, grad_ref, store, rest, reduce_send, reduce_recv
    )

    def pairs():
        for number in range(zs * ys * 2):
            yield number, (number // (2 * ys), number // 2 % ys, number % 2)

    def unpack_plane(layer, core):
        for number in range(zs * ys):
            at = (number // ys, number % ys, core)
            even, uneven = (full_ref[(layer,) + at + (x,)].astype(jnp.float32) for x in range(2))
            start, cut = (2 * number + core) * 2 * used, used - tail

            def part(first, size):
                return pl.ds(pl.multiple_of(start + first, 8), size)

            if tail:
                rows_f[part(0, cut), :] = even[:cut]
                rows_f[part(cut, 8), :] = even[cut : cut + 8] + uneven[:8]
                rows_f[part(cut + 8, used + tail - 8), :] = uneven[8:wide]
            else:
                rows_f[part(0, used), :] = even[:used]
                rows_f[part(used, used), :] = uneven[:used]

    def unpack(layer):
        unpack_plane(layer, me["c"])
        gather(layer, 5)
        unpack_plane(layer, 1 - me["c"])

    ends = [0]
    for size, count in (((shape[3] + 2) // 3, 1), ((shape[3] + 2) // 3 - 1, 2)):
        for _ in range(count):
            ends.append(ends[-1] + (size * shape[2]) ** 2 // LANES)

    def packed(layer, block):
        for number, at in pairs():
            last = (number // (2 * ys) + 1) * (2 * ys) * 2 * used
            if not ends[block] < last <= ends[block + 1]:
                continue
            first = number * 2 * used
            for x, start in enumerate((first, first + used - tail)):
                grad_ref[(layer,) + at + (x,)] = rows_f[start : start + rows, :].astype(
                    jnp.bfloat16
                )
            if number % (2 * ys) == 2 * ys - 1:
                exchange(layer, at[0])

    refs = (count_ref, x, cot, wig, rad, src_ref, dst_ref)
    compute(shape, refs, work, unpack, packed, gather, reduce, ready)
    gathered()
    reduced()


def work_buffers(shape, flat_rows):
    nat, coef, chan, rows, edges = shape
    lone = (rows + 2) // 3
    kzero, kone = lone * chan, (lone - 1) * chan
    used, tall = nat * coef, node_rows(nat, coef)
    return [
        pltpu.VMEM((flat_rows, LANES), jnp.float32),
        pltpu.VMEM((kzero, kzero), jnp.bfloat16),
        pltpu.VMEM((kone, kone), jnp.bfloat16),
        pltpu.VMEM((kone, kone), jnp.bfloat16),
        pltpu.VMEM((tall, rows * edges), jnp.bfloat16),
        pltpu.VMEM((tall, rows * edges), jnp.bfloat16),
        pltpu.VMEM((2, chan, edges), jnp.float32),
        pltpu.VMEM((2, rows * chan, edges), jnp.bfloat16),
        pltpu.VMEM((edges, rows * chan), jnp.bfloat16),
        pltpu.VMEM((rows * edges, chan), jnp.bfloat16),
        pltpu.VMEM((chan, tall), jnp.bfloat16),
        pltpu.VMEM((2, used, chan), jnp.float32),
        pltpu.VMEM((tall, chan), jnp.bfloat16),
        pltpu.VMEM((tall, chan), jnp.bfloat16),
        pltpu.VMEM((used, chan), jnp.float32),
        pltpu.VMEM((rows * chan, edges), jnp.bfloat16),
    ]


def reduce_scratch(dims, layers, rows):
    zs, ys, xs = dims
    part = rows // PIECES
    most = max(zs, ys, xs, 2) - 1
    count = layers * PIECES
    slots = count * 4 * most
    even, odd = (count + 1) // 2, count // 2
    return (
        [pltpu.VMEM((count, zs, ys, xs, part, LANES), jnp.bfloat16)]
        + reduce_buffers(dims, (("x", "y", even), ("y", "x", odd)), part)
        + [pltpu.SemaphoreType.DMA((slots,)), pltpu.SemaphoreType.DMA((slots,))]
    )


def owned_grads(dims, own, length, inputs, shape, collective_id):
    zs, ys, xs = dims
    used = length // LANES
    layers = own.shape[0] // used
    rows = -(-(used + used % 8) // 16) * 16
    spread = (layers, zs, ys, 2, xs, rows, LANES)
    flat_rows = zs * ys * 2 * xs * used
    flat_rows = -(-(flat_rows + rows) // 8) * 8
    vmem = pl.BlockSpec(memory_space=pltpu.VMEM)
    hbm = pl.BlockSpec(memory_space=pl.ANY)
    item, link = (rows, LANES), jnp.bfloat16
    return pl.pallas_call(
        functools.partial(fused_kernel, dims, shape, length),
        out_shape=jax.ShapeDtypeStruct(own.shape, jnp.float32),
        in_specs=[hbm, pl.BlockSpec(memory_space=pltpu.SMEM)] + [hbm] * 4 + [vmem] * 2,
        out_specs=vmem,
        scratch_shapes=[
            pltpu.VMEM(own.shape, own.dtype),
            pltpu.VMEM(inputs[1].shape, inputs[1].dtype),
            pltpu.VMEM(inputs[2].shape, inputs[2].dtype),
            pltpu.VMEM(inputs[3].shape, inputs[3].dtype),
            pltpu.VMEM(inputs[4].shape, inputs[4].dtype),
            pltpu.SemaphoreType.DMA((5,)),
            pltpu.VMEM(spread, jnp.bfloat16),
            pltpu.VMEM(spread, jnp.bfloat16),
            pltpu.SemaphoreType.DMA((layers, gather_slots(dims))),
            pltpu.SemaphoreType.DMA((layers, gather_slots(dims))),
            pltpu.SemaphoreType.DMA((layers, reduce_slots(dims))),
            pltpu.SemaphoreType.DMA((layers, reduce_slots(dims))),
        ]
        + work_buffers(shape, flat_rows)
        + [
            pltpu.VMEM((layers, zs, ys, xs) + item, link),
            pltpu.VMEM((layers, zs, 2) + item, link),
            pltpu.VMEM((layers, zs, 2) + item, link),
            pltpu.VMEM((layers, zs) + item, link),
            pltpu.VMEM((layers, zs) + item, link),
            pltpu.VMEM((layers, zs - 1) + item, link),
            pltpu.VMEM((layers, zs - 1) + item, link),
            pltpu.VMEM((layers,) + item, jnp.float32),
        ],
        compiler_params=pltpu.CompilerParams(
            collective_id=collective_id, has_side_effects=True, vmem_limit_bytes=60 << 20
        ),
        name="owned_grads",
    )(own, *inputs)


def device_grads(inputs, flat, shape):
    vmem = pl.BlockSpec(memory_space=pltpu.VMEM)
    return pl.pallas_call(
        functools.partial(compute_kernel, shape),
        out_shape=jax.ShapeDtypeStruct(flat.shape, jnp.bfloat16),
        in_specs=[pl.BlockSpec(memory_space=pltpu.SMEM)] + [vmem] * 7,
        out_specs=vmem,
        scratch_shapes=work_buffers(shape, flat.shape[1]),
        compiler_params=pltpu.CompilerParams(vmem_limit_bytes=56 << 20),
        name="device_grads",
    )(*inputs, flat)


def woven(rows):
    return with_layout_constraint(rows, Layout(major_to_minor=(1, 0, 2)))


def local(
    dims, node_feats, cotangent, wigner, radial, edge_src, edge_dst, edge_count, params, moment1,
    moment2,
):
    nat, coef, chan = node_feats.shape
    layers, length = params.shape
    zs, ys, xs = dims
    shards = zs * ys * 2 * xs
    edges = edge_src.shape[0]
    shape = (nat, coef, chan, wigner.shape[0], edges)

    inputs = (
        edge_count,
        jnp.transpose(node_feats, (1, 0, 2)),
        jnp.transpose(cotangent, (1, 0, 2)),
        jnp.transpose(wigner, (1, 0, 2)),
        radial,
        edge_src[None, :],
        edge_dst[None, :],
    )
    if length % (4 * LANES) == 0 and ys == 2 and xs == 2 and zs > 1 and zs & (zs - 1) == 0:
        used = length // LANES
        own = woven(params.reshape(layers, used, LANES))
        own = jnp.transpose(own, (1, 0, 2)).reshape(used * layers, LANES)
        owned = owned_grads(dims, own, length, inputs, shape, 0)
        grad = woven(jnp.transpose(owned.reshape(used, layers, LANES), (1, 0, 2)))
        grad = grad.reshape(layers, length)
    else:
        block = LANES * 16 * PIECES
        padded = -(-length // block) * block
        rows = padded // LANES
        own = jnp.pad(params.astype(jnp.bfloat16), ((0, 0), (0, padded - length)))
        full = gather_shards(dims, own.reshape(layers, rows, LANES), 0)
        full = full.reshape(layers, shards, padded)[:, :, :length]
        full = full.reshape(layers, shards * length // LANES, LANES)
        grad = device_grads(inputs, full, shape).reshape(layers, shards, length)
        grad = jnp.pad(grad, ((0, 0), (0, 0), (0, padded - length)))
        owned = reduce_shards(dims, grad.reshape(layers, zs, ys, 2, xs, rows, LANES), 1)
        grad = owned.reshape(layers, padded)[:, :length]
    new_moment1 = 0.9 * moment1 + 0.1 * grad
    new_moment2 = 0.95 * moment2 + 0.05 * grad * grad
    m_hat = new_moment1 / (1.0 - 0.9**60)
    v_hat = new_moment2 / (1.0 - 0.95**60)
    new_params = params - 0.01 * (m_hat / (jnp.sqrt(v_hat) + 1e-08) + 0.1 * params)
    return (new_params, new_moment1, new_moment2)


def solution(mesh):
    both = ("dp", "node")
    return jax.shard_map(
        functools.partial(local, split_axes(mesh)),
        mesh=mesh,
        in_specs=(
            P(both, None, None),
            P(both, None, None),
            P(None, None, both),
            P(None, both, None),
            P(both),
            P(both),
            P(both),
            P(None, both),
            P(None, both),
            P(None, both),
        ),
        out_specs=(P(None, both), P(None, both), P(None, both)),
        check_vma=False,
    )
```

```python
import functools

import jax
import jax.numpy as jnp
from jax import lax
from jax.experimental import pallas as pl
from jax.experimental.layout import Layout, with_layout_constraint
from jax.experimental.pallas import tpu as pltpu
from jax.sharding import PartitionSpec as P

AVG = 10
LANES = 128
PIECES = 3
LINK = jnp.bfloat16
WORK = 16
ACROSS = (0, 1)


def split_axes(mesh):
    rest = mesh.shape["dp"] // 2
    y = 1
    while y * y * 4 <= rest and rest % (y * 2) == 0:
        y *= 2
    return rest // y, y, mesh.shape["node"]


def place(dims):
    zs, ys, xs = dims
    dp = lax.axis_index("dp")
    x = lax.axis_index("node")
    core = lax.rem(dp, 2)
    y = lax.rem(dp // 2, ys)
    z = dp // (2 * ys)
    return {"z": z, "y": y, "c": core, "x": x}


def device(dims, at):
    return {"dp": (at["z"] * dims[1] + at["y"]) * 2 + at["c"], "node": at["x"]}


def peer_of(dims, me, axis, step):
    size = {"z": dims[0], "y": dims[1], "c": 2, "x": dims[2]}[axis]
    other = dict(me)
    other[axis] = lax.rem(me[axis] + step, size)
    return other


def size_of(dims, axis):
    return {"z": dims[0], "y": dims[1], "c": 2, "x": dims[2]}[axis]


def greet(dims, me, meanwhile=lambda: None, corner=False):
    barrier = pltpu.get_barrier_semaphore()
    count = 0
    if corner:
        pl.semaphore_signal(
            barrier,
            inc=1,
            device_id=device(dims, dict(me, x=1 - me["x"], y=1 - me["y"])),
            device_id_type=pl.DeviceIdType.MESH,
        )
        count += 1
    for axis in "zyxc":
        for step in range(1, size_of(dims, axis)):
            pl.semaphore_signal(
                barrier,
                inc=1,
                device_id=device(dims, peer_of(dims, me, axis, step)),
                device_id_type=pl.DeviceIdType.MESH,
            )
            count += 1
    meanwhile()
    pl.semaphore_wait(barrier, count)


def gather_steps(dims, me, own_ref, out_ref, local_sem, send_sem, recv_sem):
    layers, rows = own_ref.shape[0], own_ref.shape[1]
    part = rows // PIECES
    mine = pltpu.make_async_copy(
        own_ref, out_ref.at[:, me["z"], me["y"], me["c"], me["x"]], local_sem
    )
    mine.start()
    most = max(size_of(dims, a) for a in "zyxc") - 1
    started = {}
    state = {"mine": True}

    def view(ref, layer, piece, spans, at):
        index = [layer]
        for axis in "zycx":
            index.append(slice(None) if axis in spans else at[axis])
        index.append(pl.ds(piece * part, part))
        return ref.at[tuple(index)]

    def advance(layer, phase):
        for piece in range(PIECES):
            number = layer * PIECES + piece
            order = "zyxc" if number % 2 == 0 else "zxyc"
            if phase:
                for copy in started[number, phase - 1]:
                    copy.wait_recv()
                if state["mine"]:
                    mine.wait()
                    state["mine"] = False
            if phase == 4:
                continue
            axis, spans = order[phase], order[:phase]
            copies = []
            for step in range(1, size_of(dims, axis)):
                if phase == 0:
                    src = own_ref.at[layer, pl.ds(piece * part, part)]
                else:
                    src = view(out_ref, layer, piece, spans, me)
                slot = (number * 4 + phase) * most + step - 1
                copy = pltpu.make_async_remote_copy(
                    src_ref=src,
                    dst_ref=view(out_ref, layer, piece, spans, me),
                    send_sem=send_sem.at[slot],
                    recv_sem=recv_sem.at[slot],
                    device_id=device(dims, peer_of(dims, me, axis, step)),
                    device_id_type=pl.DeviceIdType.MESH,
                )
                copy.start()
                copies.append(copy)
            started[number, phase] = copies

    def finish():
        for copies in started.values():
            for copy in copies:
                copy.wait_send()

    return advance, finish


def gather_kernel(dims, own_ref, out_ref, local_sem, send_sem, recv_sem):
    me = place(dims)
    greet(dims, me)
    advance, finish = gather_steps(dims, me, own_ref, out_ref, local_sem, send_sem, recv_sem)
    for phase in range(5):
        for layer in range(own_ref.shape[0]):
            advance(layer, phase)
    finish()


def gather_shards(dims, own, collective_id):
    layers, rows, lanes = own.shape
    zs, ys, xs = dims
    most = max(zs, ys, xs, 2) - 1
    slots = layers * PIECES * 4 * most
    return pl.pallas_call(
        functools.partial(gather_kernel, dims),
        out_shape=jax.ShapeDtypeStruct((layers, zs, ys, 2, xs, rows, lanes), own.dtype),
        in_specs=[pl.BlockSpec(memory_space=pltpu.VMEM)],
        out_specs=pl.BlockSpec(memory_space=pltpu.VMEM),
        scratch_shapes=[
            pltpu.SemaphoreType.DMA,
            pltpu.SemaphoreType.DMA((slots,)),
            pltpu.SemaphoreType.DMA((slots,)),
        ],
        compiler_params=pltpu.CompilerParams(
            collective_id=collective_id, has_side_effects=True, vmem_limit_bytes=48 << 20
        ),
        name="gather_shards",
    )(own)


def reduce_buffers(dims, pairs, part):
    zs = dims[0]
    buffers = []
    for first, second, count in pairs:
        n1, n2 = size_of(dims, first), size_of(dims, second)
        buffers += [
            pltpu.VMEM((count, zs, n2, part, LANES), jnp.float32),
            pltpu.VMEM((count, n1 - 1, zs, n2, part, LANES), LINK),
            pltpu.VMEM((count, n1 - 1, zs, n2, part, LANES), LINK),
            pltpu.VMEM((count, zs, part, LANES), jnp.float32),
            pltpu.VMEM((count, n2 - 1, zs, part, LANES), LINK),
            pltpu.VMEM((count, n2 - 1, zs, part, LANES), LINK),
            pltpu.VMEM((count, part, LANES), jnp.float32),
            pltpu.VMEM((count, zs - 1, part, LANES), LINK),
            pltpu.VMEM((count, zs - 1, part, LANES), LINK),
        ]
    return buffers


def reduce_items(layers):
    items = []
    for layer in reversed(range(layers)):
        for piece in range(PIECES):
            number = len(items)
            items.append((layer, piece, number % 2, number // 2))
    return items


def reduce_steps(dims, me, grad_ref, out_ref, pair_buf, scratch):
    zs = dims[0]
    buffers = (scratch[:9], scratch[9:18])
    send_sem, recv_sem = scratch[18:20]
    layers, rows = out_ref.shape[0], out_ref.shape[1]
    part = rows // PIECES
    items = reduce_items(layers)
    most = max(size_of(dims, a) for a in "zyxc") - 1
    pending = []

    def send(number, phase, step, axis, src, dst):
        slot = (number * 4 + phase) * most + step - 1
        copy = pltpu.make_async_remote_copy(
            src_ref=src,
            dst_ref=dst,
            send_sem=send_sem.at[slot],
            recv_sem=recv_sem.at[slot],
            device_id=device(dims, peer_of(dims, me, axis, step)),
            device_id_type=pl.DeviceIdType.MESH,
        )
        copy.start()
        pending.append(copy)
        return copy

    def f32(value):
        return value.astype(jnp.float32)

    waits = {}

    def advance(wanted, now):
        phase = now - 1
        for number, (layer, piece, kind, place_in) in enumerate(items):
            if layer != wanted:
                continue
            if now == 0:
                waits[number] = [
                    send(
                        number, 0, 1, "c",
                        grad_ref.at[layer, :, :, 1 - me["c"], :, pl.ds(piece * part, part)],
                        pair_buf.at[number],
                    )
                ]
                continue
            span = pl.ds(piece * part, part)
            acc1, send1, recv1, acc2, send2, recv2, acc3, send3, recv3 = (
                buf.at[place_in] for buf in buffers[kind]
            )
            first, second = ("x", "y") if kind == 0 else ("y", "x")
            n1, n2 = size_of(dims, first), size_of(dims, second)
            for copy in waits[number]:
                copy.wait_recv()
            copies = []
            if phase == 0:
                for step in list(range(1, n1)) + [0]:
                    k1 = lax.rem(me[first] + step, n1)

                    def one(i, carry, step=step, k1=k1):
                        z, k2 = i // n2, lax.rem(i, n2)
                        y, x = (k2, k1) if kind == 0 else (k1, k2)
                        total = f32(grad_ref[layer, z, y, me["c"], x, span]) + f32(
                            pair_buf[number, z, y, x]
                        )
                        if step:
                            send1[step - 1, z, k2] = total.astype(LINK)
                        else:
                            acc1[z, k2] = total
                        return carry

                    lax.fori_loop(0, zs * n2, one, 0)
                    if step:
                        copies.append(
                            send(number, 1, step, first, send1.at[step - 1], recv1.at[step - 1])
                        )
            elif phase == 1:
                for step in list(range(1, n2)) + [0]:
                    k2 = lax.rem(me[second] + step, n2)

                    def one(z, carry, step=step, k2=k2):
                        total = acc1[z, k2]
                        for e in range(n1 - 1):
                            total = total + f32(recv1[e, z, k2])
                        if step:
                            send2[step - 1, z] = total.astype(LINK)
                        else:
                            acc2[z] = total
                        return carry

                    lax.fori_loop(0, zs, one, 0)
                    if step:
                        copies.append(
                            send(number, 2, step, second, send2.at[step - 1], recv2.at[step - 1])
                        )
            elif phase == 2:
                for step in list(range(1, zs)) + [0]:
                    z = lax.rem(me["z"] + step, zs)
                    total = acc2[z]
                    for e in range(n2 - 1):
                        total = total + f32(recv2[e, z])
                    if step:
                        send3[step - 1] = total.astype(LINK)
                        copies.append(
                            send(number, 3, step, "z", send3.at[step - 1], recv3.at[step - 1])
                        )
                    else:
                        acc3[...] = total
            else:
                total = acc3[...]
                for e in range(zs - 1):
                    total = total + f32(recv3[e])
                out_ref[layer, span] = total
            waits[number] = copies

    def finish():
        for copy in pending:
            copy.wait_send()

    return advance, finish


def reduce_kernel(dims, grad_ref, out_ref, pair_buf, *scratch):
    me = place(dims)
    greet(dims, me)
    advance, finish = reduce_steps(dims, me, grad_ref, out_ref, pair_buf, scratch)
    for phase in range(5):
        for layer in reversed(range(out_ref.shape[0])):
            advance(layer, phase)
    finish()


def reduce_shards(dims, grad, collective_id):
    layers, _, _, _, _, rows, lanes = grad.shape
    return pl.pallas_call(
        functools.partial(reduce_kernel, dims),
        out_shape=jax.ShapeDtypeStruct((layers, rows, lanes), jnp.float32),
        in_specs=[pl.BlockSpec(memory_space=pltpu.VMEM)],
        out_specs=pl.BlockSpec(memory_space=pltpu.VMEM),
        scratch_shapes=reduce_scratch(dims, layers, rows),
        compiler_params=pltpu.CompilerParams(
            collective_id=collective_id, has_side_effects=True, vmem_limit_bytes=48 << 20
        ),
        name="reduce_shards",
    )(grad)


def dot(a, b, over=(1, 0)):
    return lax.dot_general(
        a, b, (((over[0],), (over[1],)), ((), ())), preferred_element_type=jnp.float32
    )


def compute_kernel(
    shape, count_ref, x_ref, cot_ref, wig_ref, rad_ref, src_ref, dst_ref, flat_ref, grad_ref,
    *scratch,
):
    rows_f = scratch[0]

    def unpack(layer):
        rows_f[...] = flat_ref[layer].astype(jnp.float32)

    def packed(layer, block):
        if block == 2:
            grad_ref[layer] = rows_f[...].astype(jnp.bfloat16)

    refs = (count_ref, x_ref, cot_ref, wig_ref, rad_ref, src_ref, dst_ref)
    skip = lambda *step: None
    compute(shape, refs, scratch, unpack, packed, skip, skip, skip)


def node_rows(nat, coef):
    return -(-nat * coef // 32) * 32


def compute(shape, refs, scratch, unpack, packed, gather, reduce, ready):
    count_ref, x_ref, cot_ref, wig_ref, rad_ref, src_ref, dst_ref = refs
    (
        rows_f, wzero, wreal, wimag, pick, put, scale, rotated, flat_a, mixed, node_t,
        outs, nodes, back, dnode, dmix,
    ) = scratch
    nat, coef, chan, rows, edges = shape
    lone = (rows + 2) // 3
    kzero, kone = lone * chan, (lone - 1) * chan
    used, tall = nat * coef, node_rows(nat, coef)
    bf16, f32 = jnp.bfloat16, jnp.float32
    eye = (
        lax.broadcasted_iota(jnp.int32, (chan, chan), 0)
        == lax.broadcasted_iota(jnp.int32, (chan, chan), 1)
    ).astype(f32).astype(bf16)

    def span(k, size):
        return slice(k * size, (k + 1) * size)

    def filled(value):
        value = value.reshape(used, chan)
        return jnp.concatenate([value, jnp.zeros((tall - used, chan), f32)], axis=0)

    def spread_wigner(hooks):
        atoms = lax.broadcasted_iota(jnp.int32, (nat, edges), 0)
        slots = lax.broadcasted_iota(jnp.int32, (nat, edges), 1)
        taken = (src_ref[...] == atoms).astype(f32)
        live = ((dst_ref[...] == atoms) & (slots < count_ref[0])).astype(f32)

        def write(first, coefs, at, size):
            values = [wig_ref[first + n].astype(f32) for n in range(coefs)]
            for k in range(rows):
                for ref, mask in ((pick, taken), (put, live)):
                    parts = [value[k : k + 1] * mask for value in values]
                    if size > coefs * nat:
                        parts.append(jnp.zeros((size - coefs * nat, edges), f32))
                    ref[pl.ds(at, size), span(k, edges)] = jnp.concatenate(
                        parts, axis=0
                    ).astype(bf16)

        pairs = coef // 2

        def one(p, carry):
            write(2 * p, 2, pl.multiple_of(p * 2 * nat, 2 * nat), 2 * nat)
            return carry

        parts = len(hooks) + 1
        for n in range(parts):
            lax.fori_loop(n * pairs // parts, (n + 1) * pairs // parts, one, 0)
            if n < len(hooks):
                hooks[n]()
        at = pairs * 2 * nat
        write(2 * pairs, coef - 2 * pairs, at, tall - at)

    def blocks():
        cut = kzero * kzero // LANES
        step = kone * kone // LANES
        return ((wzero, 0, kzero), (wreal, cut, kone), (wimag, cut + step, kone))

    def load_weights(layer):
        unpack(layer)
        for ref, start, size in blocks():
            per = size // LANES
            for c in range(per):
                ref[:, c * LANES : (c + 1) * LANES] = rows_f[
                    pl.ds(start + c, size, stride=per), :
                ].astype(bf16)

    def store_grads(layer, grads):
        for block, ((_, start, size), grad) in enumerate(zip(blocks(), grads)):
            per = size // LANES
            wide = 2 * LANES
            for n in range(0, size, wide):
                value = grad(n, min(n + wide, size))
                for c in range(value.shape[1] // LANES):
                    rows_f[pl.ds(start + n // LANES + c, size, stride=per), :] = value[
                        :, span(c, LANES)
                    ]
            packed(layer, block)

    def to_nodes(matrix, source):
        half = tall // 2
        return jnp.concatenate(
            [dot(matrix[span(n, half), :], source[...]) for n in range(2)], axis=0
        )[:used]

    def rotate(layer, hooks):
        node_t[...] = dot(eye, nodes[...], (1, 1)).astype(bf16)
        for k in range(rows):
            for n, hook in enumerate(hooks):
                if k == (n + 1) * rows // (len(hooks) + 1):
                    hook()
            value = dot(node_t[...], pick[:, span(k, edges)]) * scale[layer]
            value = value.astype(bf16)
            rotated[layer, span(k, chan)] = value
            flat_a[:, span(k, chan)] = value.T

    def forward(layer, last, hooks):
        load_weights(layer)
        for hook in hooks[:1]:
            hook()
        azero = flat_a[:, :kzero]
        aplus = flat_a[:, kzero : kzero + kone]
        aminus = flat_a[:, kzero + kone :]

        def keep(first, value):
            for c in range(value.shape[1] // chan):
                mixed[span(first + c, edges)] = value[:, span(c, chan)].astype(bf16)

        wide = 2 * LANES
        for n in range(0, kzero, wide):
            keep(n // chan, dot(azero, wzero[:, n : min(n + wide, kzero)]))
        for n in range(0, kone, wide):
            real, imag = (w[:, n : min(n + wide, kone)] for w in (wreal, wimag))
            keep(lone + n // chan, dot(aplus, real) - dot(aminus, imag))
            keep(2 * lone - 1 + n // chan, dot(aplus, imag) + dot(aminus, real))
        for hook in hooks[1:]:
            hook()
        total = to_nodes(put, mixed)
        before = nodes[...].astype(f32)[:used]
        outs[layer] = before + total / AVG
        if last:
            return
        value = outs[layer].reshape(coef, nat, chan)
        gate = jax.nn.sigmoid(value[0])
        nodes[...] = filled(value * gate[None]).astype(bf16)

    def backward(layer, cot, last, hooks):
        value = outs[layer].reshape(coef, nat, chan)
        scalar = value[0]
        gate = jax.nn.sigmoid(scalar)
        slope = gate * (1.0 - gate)
        total = jnp.sum(cot[1:] * value[1:], axis=0)
        lead = cot[0] * (gate + scalar * slope) + total * slope
        dout = jnp.concatenate([lead[None], cot[1:] * gate[None]], axis=0)
        dnode[...] = dout.reshape(used, chan)
        share = filled(dout / AVG)
        high = share.astype(bf16)
        node_t[...] = dot(eye, high, (1, 1)).astype(bf16)
        for k in range(rows):
            dmix[span(k, chan)] = dot(node_t[...], put[:, span(k, edges)]).astype(bf16)
        dzero = dmix.at[:kzero]
        dplus = dmix.at[kzero : kzero + kone]
        dminus = dmix.at[kzero + kone :]
        azero = rotated[layer, :kzero]
        aplus = rotated[layer, kzero : kzero + kone]
        aminus = rotated[layer, kzero + kone :]
        for hook in hooks[:1]:
            hook()
        nt = (1, 1)
        store_grads(
            layer,
            (
                lambda a, b: dot(azero, dzero[a:b], nt),
                lambda a, b: dot(aplus, dplus[a:b], nt) + dot(aminus, dminus[a:b], nt),
                lambda a, b: dot(aplus, dminus[a:b], nt) - dot(aminus, dplus[a:b], nt),
            ),
        )
        if last:
            return

        def keep(first, value):
            for c in range(value.shape[0] // chan):
                part = value[span(c, chan)].astype(bf16).astype(f32) * scale[layer]
                mixed[span(first + c, edges)] = part.astype(bf16).T

        keep(0, dot(wzero[...], dzero[...]))
        keep(lone, dot(wreal[...], dplus[...]) + dot(wimag[...], dminus[...]))
        for hook in hooks[1:2]:
            hook()
        keep(2 * lone - 1, dot(wreal[...], dminus[...]) - dot(wimag[...], dplus[...]))
        total = to_nodes(pick, mixed)
        for hook in hooks[2:]:
            hook()
        back[...] = filled(dnode[...] + total).astype(bf16)

    def step(move, layer, phase):
        return lambda: move(layer, phase)

    def none():
        return None

    gather(0, 0)
    gather(0, 6)
    ready("next")
    ready("x")
    nodes[...] = filled(x_ref[...].astype(f32)).astype(bf16)
    ready("rad")
    for layer in range(rad_ref.shape[0]):
        scale[layer] = rad_ref[layer].astype(f32).T
    ready("wig")
    spread_wigner((none, step(gather, 0, 1)))
    gather(1, 0)
    gather(1, 6)
    rotate(0, (step(gather, 0, 2), ))
    gather(0, 3)
    gather(1, 1)
    gather(0, 4)
    forward(0, False, (step(gather, 1, 2), ))
    rotate(1, (step(gather, 1, 3), step(gather, 1, 4), ))
    forward(1, True, ())
    ready("cot")
    backward(1, cot_ref[...].astype(f32), False, (none, step(reduce, 1, 1)))
    last = back[...].astype(f32)[:used].reshape(coef, nat, chan)
    backward(0, last, True, ())
    for layer, phase in ((1, 2), (0, 1), (1, 3), (0, 2), (0, 3), (1, 4), (0, 4)):
        reduce(layer, phase)


def side(me):
    core = me["c"]
    return me["y"] * (1 - core) + me["x"] * core, me["x"] * (1 - core) + me["y"] * core


def spot(me, z, a, b):
    core = me["c"]
    return {"z": z, "y": a * (1 - core) + b * core, "c": core, "x": b * (1 - core) + a * core}


def flip(z, step):
    bit = 1
    while bit <= step:
        if step & bit:
            z = z + bit - 2 * bit * lax.rem(z // bit, 2)
        bit *= 2
    return z


def order_of(zs):
    return sorted(range(1, zs), key=lambda step: (step >= zs // 2, -step))


def remote(src, dst, send_sem, recv_sem, target):
    return pltpu.make_async_remote_copy(
        src_ref=src,
        dst_ref=dst,
        send_sem=send_sem,
        recv_sem=recv_sem,
        device_id=target,
        device_id_type=pl.DeviceIdType.MESH,
    )


def gather_slots(dims):
    return 4 * dims[0] + 3


def stream_gather(dims, me, full_ref, send_sem, recv_sem):
    zs = dims[0]
    a, b = side(me)
    near = order_of(zs)
    across = {layer: near[len(near) - count :] for layer, count in enumerate(ACROSS)}
    copies = {}

    def send(layer, slot, at, target):
        where = full_ref.at[(layer, at["z"], at["y"], at["c"], at["x"])]
        sems = (send_sem.at[layer, slot], recv_sem.at[layer, slot])
        copies[layer, slot] = remote(where, where, *sems, device(dims, target))
        copies[layer, slot].start()

    def by_z(layer, step):
        target = dict(me, z=flip(me["z"], step))
        send(layer, step - 1, me, target)

    def by_a(layer, step):
        z = flip(me["z"], step)
        send(layer, zs - 1 + step, spot(me, z, a, b), spot(me, me["z"], 1 - a, b))

    def by_b(layer, step, far):
        z = flip(me["z"], step)
        at = spot(me, z, 1 - a if far else a, b)
        send(layer, (3 if far else 2) * zs - 1 + step, at, spot(me, me["z"], a, 1 - b))

    def by_corner(layer, step):
        z = flip(me["z"], step)
        send(layer, 3 * zs - 1 + step, spot(me, z, a, b), spot(me, me["z"], 1 - a, 1 - b))

    def by_c(layer, number):
        at = spot(me, slice(None), 1 - a if number % 2 else a, 1 - b if number // 2 else b)
        send(layer, 4 * zs - 1 + number, at, dict(me, c=1 - me["c"]))

    def wait(layer, slot):
        copies[layer, slot].wait_recv()

    def advance(layer, phase):
        if phase == 0:
            for step in near:
                by_z(layer, step)
        elif phase == 6:
            by_a(layer, 0)
            by_b(layer, 0, False)
        elif phase == 1:
            for step in near:
                wait(layer, step - 1)
                by_a(layer, step)
                by_b(layer, step, False)
                if step in across[layer]:
                    by_corner(layer, step)
            wait(layer, zs - 1)
            by_b(layer, 0, True)
            by_c(layer, 0)
        elif phase == 2:
            for step in near:
                wait(layer, zs - 1 + step)
                if step not in across[layer]:
                    by_b(layer, step, True)
            by_c(layer, 1)
        elif phase == 3:
            for step in [0] + near:
                wait(layer, 2 * zs - 1 + step)
            by_c(layer, 2)
        elif phase == 4:
            for step in [0] + near:
                wait(layer, 3 * zs - 1 + step)
            by_c(layer, 3)
        else:
            for number in range(4):
                wait(layer, 4 * zs - 1 + number)

    def finish():
        for copy in copies.values():
            copy.wait_send()

    return advance, finish


def reduce_slots(dims):
    return 5 * dims[0] - 1


def stream_reduce(dims, me, grad_ref, store, buffers, send_sem, recv_sem):
    zs = dims[0]
    a, b = side(me)
    pair, send_b, recv_b, send_a, recv_a, send_z, recv_z, total = buffers
    steps = sorted(order_of(zs), reverse=True) + [0]
    copies = {}

    def send(key, layer, slot, src, dst, target):
        sems = (send_sem.at[layer, slot], recv_sem.at[layer, slot])
        copies[key] = remote(src, dst, *sems, device(dims, target))
        copies[key].start()

    def f32(value):
        return value.astype(jnp.float32)

    def depth(step):
        return flip(me["z"], step)

    def own(layer, z, a, b):
        at = spot(me, z, a, b)
        return f32(grad_ref[layer, z, at["y"], at["c"], at["x"]]) + f32(
            pair[layer, z, at["y"], at["x"]]
        )

    def exchange(layer, z):
        send(
            ("c", layer, z), layer, z, grad_ref.at[layer, z, :, 1 - me["c"]], pair.at[layer, z],
            dict(me, c=1 - me["c"]),
        )

    def advance(layer, phase):
        if phase == 1:
            for z in range(zs):
                copies["c", layer, z].wait_recv()
            for near in range(2):
                for step in steps:
                    value = own(layer, depth(step), a if near else 1 - a, 1 - b)
                    send_b[layer, step, near] = value.astype(LINK)
                    send(
                        ("b", layer, step, near), layer, zs + 2 * step + near,
                        send_b.at[layer, step, near], recv_b.at[layer, step, near],
                        spot(me, me["z"], a, 1 - b),
                    )
        elif phase == 2:
            for step in steps:
                copies["b", layer, step, 0].wait_recv()
                value = own(layer, depth(step), 1 - a, b) + f32(recv_b[layer, step, 0])
                send_a[layer, step] = value.astype(LINK)
                send(
                    ("a", layer, step), layer, 3 * zs + step, send_a.at[layer, step],
                    recv_a.at[layer, step], spot(me, me["z"], 1 - a, b),
                )
        elif phase == 3:
            for step in steps:
                copies["b", layer, step, 1].wait_recv()
                copies["a", layer, step].wait_recv()
                value = (
                    own(layer, depth(step), a, b)
                    + f32(recv_b[layer, step, 1])
                    + f32(recv_a[layer, step])
                )
                if step == 0:
                    total[layer] = value
                    continue
                send_z[layer, step - 1] = value.astype(LINK)
                send(
                    ("z", layer, step), layer, 4 * zs + step - 1, send_z.at[layer, step - 1],
                    recv_z.at[layer, step - 1], dict(me, z=depth(step)),
                )
        else:
            value = total[layer]
            for step in order_of(zs):
                copies["z", layer, step].wait_recv()
                value = value + f32(recv_z[layer, step - 1])
            store(layer, value)

    def finish():
        for copy in copies.values():
            copy.wait_send()

    return exchange, advance, finish


def fused_kernel(
    dims, shape, length, own_ref, count_ref, x_ref, cot_ref, wig_ref, rad_ref, src_ref, dst_ref,
    out_ref, par, x, cot, wig, rad, load_sem, full_ref, grad_ref, gather_send, gather_recv,
    reduce_send, reduce_recv, *scratch,
):
    zs, ys, xs = dims
    me = place(dims)
    loads = {}
    for number, (name, source, ref) in enumerate(
        (
            ("own", own_ref, par), ("x", x_ref, x), ("rad", rad_ref, rad), ("wig", wig_ref, wig),
            ("cot", cot_ref, cot),
        )
    ):
        loads[name] = pltpu.make_async_copy(source, ref, load_sem.at[number])

    def ready(name):
        if name == "next":
            for layer in range(1, layers):
                place_own(layer)
            return
        loads[name].wait()

    work, rest = scratch[:WORK], scratch[WORK:]
    rows_f = work[0]
    used, rows = length // LANES, full_ref.shape[-2]
    layers, tail = full_ref.shape[0], used % 8
    odd = me["x"] == 1
    wide = used + tail

    def store(layer, value):
        value = jnp.where(odd, value[tail:wide], value[:used])
        out_ref[pl.ds(layer, used, stride=layers), :] = value

    loads["own"].start()

    def meanwhile():
        for name, load in loads.items():
            if name != "own":
                load.start()
        ready("own")
        place_own(0)

    def place_own(layer):
        value = par[pl.ds(layer, used, stride=layers), :]
        low = jnp.zeros((tail, LANES), jnp.float32)
        high = jnp.zeros((rows - wide, LANES), jnp.float32)
        value = jnp.where(
            odd,
            jnp.concatenate([low, value, high], axis=0),
            jnp.concatenate([value, low, high], axis=0),
        )
        full_ref[layer, me["z"], me["y"], me["c"], me["x"]] = value.astype(jnp.bfloat16)

    greet(dims, me, meanwhile, True)
    gather, gathered = stream_gather(dims, me, full_ref, gather_send, gather_recv)
    exchange, reduce, reduced = stream_reduce(
        dims, me, grad_ref, store, rest, reduce_send, reduce_recv
    )

    def pairs():
        for number in range(zs * ys * 2):
            yield number, (number // (2 * ys), number // 2 % ys, number % 2)

    def unpack_plane(layer, core):
        for number in range(zs * ys):
            at = (number // ys, number % ys, core)
            even, uneven = (full_ref[(layer,) + at + (x,)].astype(jnp.float32) for x in range(2))
            start, cut = (2 * number + core) * 2 * used, used - tail

            def part(first, size):
                return pl.ds(pl.multiple_of(start + first, 8), size)

            if tail:
                rows_f[part(0, cut), :] = even[:cut]
                rows_f[part(cut, 8), :] = even[cut : cut + 8] + uneven[:8]
                rows_f[part(cut + 8, used + tail - 8), :] = uneven[8:wide]
            else:
                rows_f[part(0, used), :] = even[:used]
                rows_f[part(used, used), :] = uneven[:used]

    def unpack(layer):
        unpack_plane(layer, me["c"])
        gather(layer, 5)
        unpack_plane(layer, 1 - me["c"])

    ends = [0]
    for size, count in (((shape[3] + 2) // 3, 1), ((shape[3] + 2) // 3 - 1, 2)):
        for _ in range(count):
            ends.append(ends[-1] + (size * shape[2]) ** 2 // LANES)

    def packed(layer, block):
        for number, at in pairs():
            last = (number // (2 * ys) + 1) * (2 * ys) * 2 * used
            if not ends[block] < last <= ends[block + 1]:
                continue
            first = number * 2 * used
            for x, start in enumerate((first, first + used - tail)):
                grad_ref[(layer,) + at + (x,)] = rows_f[start : start + rows, :].astype(
                    jnp.bfloat16
                )
            if number % (2 * ys) == 2 * ys - 1:
                exchange(layer, at[0])

    refs = (count_ref, x, cot, wig, rad, src_ref, dst_ref)
    compute(shape, refs, work, unpack, packed, gather, reduce, ready)
    gathered()
    reduced()


def work_buffers(shape, flat_rows):
    nat, coef, chan, rows, edges = shape
    lone = (rows + 2) // 3
    kzero, kone = lone * chan, (lone - 1) * chan
    used, tall = nat * coef, node_rows(nat, coef)
    return [
        pltpu.VMEM((flat_rows, LANES), jnp.float32),
        pltpu.VMEM((kzero, kzero), jnp.bfloat16),
        pltpu.VMEM((kone, kone), jnp.bfloat16),
        pltpu.VMEM((kone, kone), jnp.bfloat16),
        pltpu.VMEM((tall, rows * edges), jnp.bfloat16),
        pltpu.VMEM((tall, rows * edges), jnp.bfloat16),
        pltpu.VMEM((2, chan, edges), jnp.float32),
        pltpu.VMEM((2, rows * chan, edges), jnp.bfloat16),
        pltpu.VMEM((edges, rows * chan), jnp.bfloat16),
        pltpu.VMEM((rows * edges, chan), jnp.bfloat16),
        pltpu.VMEM((chan, tall), jnp.bfloat16),
        pltpu.VMEM((2, used, chan), jnp.float32),
        pltpu.VMEM((tall, chan), jnp.bfloat16),
        pltpu.VMEM((tall, chan), jnp.bfloat16),
        pltpu.VMEM((used, chan), jnp.float32),
        pltpu.VMEM((rows * chan, edges), jnp.bfloat16),
    ]


def reduce_scratch(dims, layers, rows):
    zs, ys, xs = dims
    part = rows // PIECES
    most = max(zs, ys, xs, 2) - 1
    count = layers * PIECES
    slots = count * 4 * most
    even, odd = (count + 1) // 2, count // 2
    return (
        [pltpu.VMEM((count, zs, ys, xs, part, LANES), jnp.bfloat16)]
        + reduce_buffers(dims, (("x", "y", even), ("y", "x", odd)), part)
        + [pltpu.SemaphoreType.DMA((slots,)), pltpu.SemaphoreType.DMA((slots,))]
    )


def owned_grads(dims, own, length, inputs, shape, collective_id):
    zs, ys, xs = dims
    used = length // LANES
    layers = own.shape[0] // used
    rows = -(-(used + used % 8) // 16) * 16
    spread = (layers, zs, ys, 2, xs, rows, LANES)
    flat_rows = zs * ys * 2 * xs * used
    flat_rows = -(-(flat_rows + rows) // 8) * 8
    vmem = pl.BlockSpec(memory_space=pltpu.VMEM)
    hbm = pl.BlockSpec(memory_space=pl.ANY)
    item, link = (rows, LANES), jnp.bfloat16
    return pl.pallas_call(
        functools.partial(fused_kernel, dims, shape, length),
        out_shape=jax.ShapeDtypeStruct(own.shape, jnp.float32),
        in_specs=[hbm, pl.BlockSpec(memory_space=pltpu.SMEM)] + [hbm] * 4 + [vmem] * 2,
        out_specs=vmem,
        scratch_shapes=[
            pltpu.VMEM(own.shape, own.dtype),
            pltpu.VMEM(inputs[1].shape, inputs[1].dtype),
            pltpu.VMEM(inputs[2].shape, inputs[2].dtype),
            pltpu.VMEM(inputs[3].shape, inputs[3].dtype),
            pltpu.VMEM(inputs[4].shape, inputs[4].dtype),
            pltpu.SemaphoreType.DMA((5,)),
            pltpu.VMEM(spread, jnp.bfloat16),
            pltpu.VMEM(spread, jnp.bfloat16),
            pltpu.SemaphoreType.DMA((layers, gather_slots(dims))),
            pltpu.SemaphoreType.DMA((layers, gather_slots(dims))),
            pltpu.SemaphoreType.DMA((layers, reduce_slots(dims))),
            pltpu.SemaphoreType.DMA((layers, reduce_slots(dims))),
        ]
        + work_buffers(shape, flat_rows)
        + [
            pltpu.VMEM((layers, zs, ys, xs) + item, link),
            pltpu.VMEM((layers, zs, 2) + item, link),
            pltpu.VMEM((layers, zs, 2) + item, link),
            pltpu.VMEM((layers, zs) + item, link),
            pltpu.VMEM((layers, zs) + item, link),
            pltpu.VMEM((layers, zs - 1) + item, link),
            pltpu.VMEM((layers, zs - 1) + item, link),
            pltpu.VMEM((layers,) + item, jnp.float32),
        ],
        compiler_params=pltpu.CompilerParams(
            collective_id=collective_id, has_side_effects=True, vmem_limit_bytes=60 << 20
        ),
        name="owned_grads",
    )(own, *inputs)


def device_grads(inputs, flat, shape):
    vmem = pl.BlockSpec(memory_space=pltpu.VMEM)
    return pl.pallas_call(
        functools.partial(compute_kernel, shape),
        out_shape=jax.ShapeDtypeStruct(flat.shape, jnp.bfloat16),
        in_specs=[pl.BlockSpec(memory_space=pltpu.SMEM)] + [vmem] * 7,
        out_specs=vmem,
        scratch_shapes=work_buffers(shape, flat.shape[1]),
        compiler_params=pltpu.CompilerParams(vmem_limit_bytes=56 << 20),
        name="device_grads",
    )(*inputs, flat)


def woven(rows):
    return with_layout_constraint(rows, Layout(major_to_minor=(1, 0, 2)))


def local(
    dims, node_feats, cotangent, wigner, radial, edge_src, edge_dst, edge_count, params, moment1,
    moment2,
):
    nat, coef, chan = node_feats.shape
    layers, length = params.shape
    zs, ys, xs = dims
    shards = zs * ys * 2 * xs
    edges = edge_src.shape[0]
    shape = (nat, coef, chan, wigner.shape[0], edges)

    inputs = (
        edge_count,
        jnp.transpose(node_feats, (1, 0, 2)),
        jnp.transpose(cotangent, (1, 0, 2)),
        jnp.transpose(wigner, (1, 0, 2)),
        radial,
        edge_src[None, :],
        edge_dst[None, :],
    )
    if length % (4 * LANES) == 0 and ys == 2 and xs == 2 and zs > 1 and zs & (zs - 1) == 0:
        used = length // LANES
        own = woven(params.reshape(layers, used, LANES))
        own = jnp.transpose(own, (1, 0, 2)).reshape(used * layers, LANES)
        owned = owned_grads(dims, own, length, inputs, shape, 0)
        grad = woven(jnp.transpose(owned.reshape(used, layers, LANES), (1, 0, 2)))
        grad = grad.reshape(layers, length)
    else:
        block = LANES * 16 * PIECES
        padded = -(-length // block) * block
        rows = padded // LANES
        own = jnp.pad(params.astype(jnp.bfloat16), ((0, 0), (0, padded - length)))
        full = gather_shards(dims, own.reshape(layers, rows, LANES), 0)
        full = full.reshape(layers, shards, padded)[:, :, :length]
        full = full.reshape(layers, shards * length // LANES, LANES)
        grad = device_grads(inputs, full, shape).reshape(layers, shards, length)
        grad = jnp.pad(grad, ((0, 0), (0, 0), (0, padded - length)))
        owned = reduce_shards(dims, grad.reshape(layers, zs, ys, 2, xs, rows, LANES), 1)
        grad = owned.reshape(layers, padded)[:, :length]
    new_moment1 = 0.9 * moment1 + 0.1 * grad
    new_moment2 = 0.95 * moment2 + 0.05 * grad * grad
    m_hat = new_moment1 / (1.0 - 0.9**60)
    v_hat = new_moment2 / (1.0 - 0.95**60)
    new_params = params - 0.01 * (m_hat / (jnp.sqrt(v_hat) + 1e-08) + 0.1 * params)
    return (new_params, new_moment1, new_moment2)


def solution(mesh):
    both = ("dp", "node")
    return jax.shard_map(
        functools.partial(local, split_axes(mesh)),
        mesh=mesh,
        in_specs=(
            P(both, None, None),
            P(both, None, None),
            P(None, None, both),
            P(None, both, None),
            P(both),
            P(both),
            P(both),
            P(None, both),
            P(None, both),
            P(None, both),
        ),
        out_specs=(P(None, both), P(None, both), P(None, both)),
        check_vma=False,
    )
```
